128 devices in a mesh: gy: 8 (over x_hi, y), gx: 16 (over z, x_lo, core).
Axes of the slice: x: 4 (x_hi: 2, x_lo: 2; x = x_hi * 2 + x_lo), y: 4, z: 4, core: 2. Of those that a mesh axis runs over, the one named last changes fastest.
Arguments:
- features: bfloat16 [256, 2048, 256], P('gy', 'gx'), may hold values from -8 to 8
- tissue: int32 [16, 128], P('gy', 'gx'), may hold values 0 or 1
- owner_map: int32 [8, 16, 16, 1], P('gy', 'gx'), may hold values from 0 to 15; in each aligned block of 16 rows (0 to 15, 16 to 31, ..., all dimensions but the last counted through in order) at most 2 rows name the same one
- w_conv: bfloat16 [9, 256, 256], replicated, may hold values from -0.125 to 0.125
- w_stride: bfloat16 [4, 256, 256], replicated, may hold values from -0.1875 to 0.1875
- w_query: float32 [256, 256], replicated, may hold values from -0.375 to 0.375
- w_key: float32 [256, 256], replicated, may hold values from -0.375 to 0.375
- w_value: float32 [256, 256], replicated, may hold values from -0.375 to 0.375
- cotangent: float32 [256], replicated, may hold values from -6 to 6
Outputs:
- embedding: float32 [256], replicated
- input_grad: bfloat16 [256, 2048, 256], P('gy', 'gx')
- conv_grad: float32 [9, 256, 256], replicated
The draws below stay inside these ranges and needn't reach their ends.
Inputs may be any that keep to these rules, and one draw needn't show every extreme that they name: `owner_map`: among the tiles of one device, no owner index is named more than 2 times.
All inputs are finite; a program needn't handle non-finite values. No bound on the sum of `tissue` on one device may be relied on, other than what follows from the above.
Results may differ from the reference program's by a relative error of at most 0.017.
Values may be sent and summed in bfloat16 or wider, within the bound.
A program may use at most 128 MiB of HBM per device.

```python
import math
from functools import partial
import jax
import jax.numpy as jnp
import numpy as np
from jax import lax

C = 256
HEADS = 4
TILE = 8
TYD = 2
TXD = 8
CAP = 2
TILES_DEV = 16
NH = 256
NW = 2048
NTY = 16
NTX = 128
ALL_TILES = 2048
N_GY = 8
N_GX = 16


def draw_features(key, part):
    first = jax.random.fold_in(jax.random.fold_in(key, 11), 0)
    values = jax.random.normal(first, (NH, NW, C), jnp.float32)
    return jnp.clip(values, -8.0, 8.0).astype(jnp.bfloat16)


def set_ends(array, key, low, top_value):
    shape = array.shape
    spot = [jax.random.randint(jax.random.fold_in(key, axis), (), 0, shape[axis]) for axis in range(len(shape))]
    array = array.at[tuple(spot)].set(low)
    longest = shape.index(max(shape))
    spot[longest] = (spot[longest] + 1) % shape[longest]
    return array.at[tuple(spot)].set(top_value)


def shared_out(own_key, own, number, rows, count, top, reach, lean):
    ranking = jax.random.permutation(own_key, count)
    heavy_load, usual = shares(count, rows * top, reach, lean, True), shares(count, rows * top, reach, lean, False)
    places = jnp.arange(count)

    def named(sizes, rotation):
        used = int((sizes > 0).sum())
        fixed = max(1, used // 4)
        moved = fixed + (places - fixed + rotation * (used - fixed)) % max(1, count - fixed)
        return jnp.zeros((count,), jnp.int32).at[ranking[jnp.where(places < fixed, places, moved)]].set(jnp.asarray(sizes, jnp.int32))

    sizes = jnp.where(number % 4 == 0, named(heavy_load, number // 4), named(usual, number - number // 4 - 1))
    mixed = jax.random.permutation(jax.random.fold_in(own, 3), count)
    source_of, sink = mixed[0:count // 2 * 2:2], mixed[1:count // 2 * 2:2]
    margin = jnp.minimum(sizes[source_of] - 1, reach - sizes[sink]) // 2
    margin = jnp.where((source_of == ranking[0]) | (sink == ranking[0]) | (sizes[sink] == 0), 0, jnp.maximum(margin, 0))
    moved = jax.random.randint(jax.random.fold_in(own, 4), (count // 2,), 0, 1 << 20) % (margin + 1)
    sizes = sizes.at[source_of].add(-moved).at[sink].add(moved)
    items = jnp.searchsorted(jnp.cumsum(sizes), jnp.arange(rows * top), side="right").astype(jnp.int32)
    table = items.reshape(top, rows).T
    table = table[jax.random.permutation(jax.random.fold_in(own, 1), rows)]
    rotation = jax.random.randint(jax.random.fold_in(own, 2), (rows, 1), 0, top)
    return jnp.take_along_axis(table, (jnp.arange(top)[None, :] + rotation) % top, axis=1)


def shares(number_of, total, bound, skew, full):
    weights = [(1 << 20) // math.isqrt(standing ** skew) + 1 for standing in range(1, number_of + 1)]
    largest = bound if full else min(bound, max(-(-total // number_of), total * weights[0] // sum(weights)))
    least = 1 if total - largest >= number_of - 1 else 0
    given, surplus = [largest] + [least] * (number_of - 1), total - largest - least * (number_of - 1)
    while surplus > 0:
        movable = [i for i in range(1, number_of) if given[i] < largest] or [i for i in range(1, number_of) if given[i] < bound]
        pool, remaining = sum([weights[i] for i in movable]), surplus
        for i in movable:
            extra = min(bound - given[i], max(1, remaining * weights[i] // pool), surplus)
            given[i] = given[i] + extra
            surplus = surplus - extra
    return np.array(given)


def gaussian(stream_key, shape, scale, most, held_as=jnp.bfloat16):
    return jnp.clip(scale * jax.random.normal(stream_key, shape, jnp.float32), -most, most).astype(held_as)


def setup_inputs(seed: int = 0) -> dict:
    key_of = jax.random.split(jax.random.key(seed), 10)
    features = draw_features(jax.random.fold_in(key_of[9], 71), 0)
    tissue = set_ends((jax.random.randint(key_of[1], (NTY, NTX), 0, 3) < 2).astype(jnp.int32), jax.random.fold_in(key_of[1], 1), 0, 1)
    owner_map_keys = jax.random.split(jax.random.fold_in(key_of[2], 1), N_GY * N_GX * TILES_DEV // TILES_DEV)
    owner_map_turns = jax.random.permutation(jax.random.fold_in(key_of[2], 3), N_GY * N_GX * TILES_DEV // TILES_DEV)
    owner_map = jax.vmap(lambda own, number: shared_out(jax.random.fold_in(key_of[2], 2), own, number, TILES_DEV, N_GX, 1, CAP, 2))(owner_map_keys, owner_map_turns).reshape((N_GY, N_GX, TILES_DEV, 1))
    w_conv = gaussian(key_of[3], (9, C, C), (9 * C) ** -0.5, 0.125)
    w_stride = gaussian(key_of[4], (4, C, C), (4 * C) ** -0.5, 0.1875)
    w_query = gaussian(key_of[5], (C, C), C ** -0.5, 0.375, jnp.float32)
    w_key = gaussian(key_of[6], (C, C), C ** -0.5, 0.375, jnp.float32)
    w_value = gaussian(key_of[7], (C, C), C ** -0.5, 0.375, jnp.float32)
    cotangent = gaussian(key_of[8], (C,), 1.0, 6.0, jnp.float32)
    return dict(features=features, tissue=tissue, owner_map=owner_map, w_conv=w_conv, w_stride=w_stride, w_query=w_query, w_key=w_key, w_value=w_value, cotangent=cotangent)


attention_bias = -1.0
loss_scale = 512.0

def forward_taps(padded, weight, pix_rows, pix_cols):
    channels = padded.shape[2]
    running = jnp.zeros((pix_rows * pix_cols, weight.shape[2]), jnp.float32)
    for tap_index in range(9):
        row_off, col_off = (tap_index // 3, tap_index % 3)
        window = padded[row_off:row_off + pix_rows, col_off:col_off + pix_cols].reshape(pix_rows * pix_cols, channels)
        running = running + jnp.dot(window, weight[tap_index], preferred_element_type=jnp.float32)
    return running.reshape(pix_rows, pix_cols, weight.shape[2])

def backward_taps(padded, weight, pix_rows, pix_cols):
    channels = padded.shape[2]
    running = jnp.zeros((pix_rows * pix_cols, weight.shape[1]), jnp.float32)
    for tap_index in range(9):
        row_off, col_off = (tap_index // 3, tap_index % 3)
        window = padded[2 - row_off:2 - row_off + pix_rows, 2 - col_off:2 - col_off + pix_cols].reshape(pix_rows * pix_cols, channels)
        running = running + lax.dot_general(window, weight[tap_index], (((1,), (1,)), ((), ())), preferred_element_type=jnp.float32)
    return running.reshape(pix_rows, pix_cols, weight.shape[1])

def weight_taps(padded, upstream, pix_rows, pix_cols):
    channels = padded.shape[2]
    flat_up = upstream.reshape(pix_rows * pix_cols, upstream.shape[2])
    pieces = []
    for tap_index in range(9):
        row_off, col_off = (tap_index // 3, tap_index % 3)
        window = padded[row_off:row_off + pix_rows, col_off:col_off + pix_cols].reshape(pix_rows * pix_cols, channels)
        pieces.append(lax.dot_general(window, flat_up, (((0,), (0,)), ((), ())), preferred_element_type=jnp.float32))
    return jnp.stack(pieces)

def strided_forward(field, weight):
    pix_rows, pix_cols, channels = field.shape
    running = jnp.zeros((pix_rows // 2 * (pix_cols // 2), weight.shape[2]), jnp.float32)
    for tap_index in range(4):
        row_off, col_off = (tap_index // 2, tap_index % 2)
        window = field[row_off::2, col_off::2].reshape(-1, channels)
        running = running + jnp.dot(window, weight[tap_index], preferred_element_type=jnp.float32)
    return running.reshape(pix_rows // 2, pix_cols // 2, weight.shape[2])

def strided_backward(upstream, weight):
    half_rows, half_cols, channels = upstream.shape
    flat_up = upstream.reshape(half_rows * half_cols, channels)
    tap_parts = []
    for tap_index in range(4):
        tap_parts.append(lax.dot_general(flat_up, weight[tap_index], (((1,), (1,)), ((), ())), preferred_element_type=jnp.float32).reshape(half_rows, half_cols, -1))
    upper_rows = jnp.stack([tap_parts[0], tap_parts[1]], axis=2)
    bottom = jnp.stack([tap_parts[2], tap_parts[3]], axis=2)
    stacked = jnp.stack([upper_rows, bottom], axis=1)
    return stacked.reshape(2 * half_rows, 2 * half_cols, -1)

def rms_normed(tokens_in):
    return tokens_in * lax.rsqrt(lax.optimization_barrier(jnp.mean(tokens_in * tokens_in, axis=-1, keepdims=True)) + 1e-05)

def silu_slope(values):
    gate_sig = jax.nn.sigmoid(values)
    return gate_sig * (1.0 + values * (1.0 - gate_sig))

def attend(query_tokens, query_flags, query_groups, key_tokens, key_flags, key_groups, w_query, w_key, w_value, head_count):
    highest = lax.Precision.HIGHEST
    query_count = query_tokens.shape[0]
    key_count = key_tokens.shape[0]
    query_rows = jnp.dot(query_tokens, w_query, precision=highest).reshape(query_count, head_count, -1)
    key_rows = jnp.dot(key_tokens, w_key, precision=highest).reshape(key_count, head_count, -1)
    value_rows = jnp.dot(key_tokens, w_value, precision=highest).reshape(key_count, head_count, -1)
    scores = jnp.einsum('qhd,khd->hqk', query_rows, key_rows, precision=highest) / math.sqrt(query_rows.shape[2])
    allowed = (query_groups[:, None] == key_groups[None, :]).astype(jnp.float32) * key_flags[None, :]
    weights = jax.nn.sigmoid(scores + attention_bias) * allowed[None]
    mixed_rows = jnp.einsum('hqk,khd->qhd', weights, value_rows, precision=highest).reshape(query_count, -1)
    return jnp.dot(query_flags, mixed_rows, precision=highest)

def self_attend(tokens_in, tile_flags, tile_groups, w_query, w_key, w_value, head_count):
    return attend(tokens_in, tile_flags, tile_groups, tokens_in, tile_flags, tile_groups, w_query, w_key, w_value, head_count)

def reference(features, tissue, owner_map, w_conv, w_stride, w_query, w_key, w_value, cotangent):
    channels = features.shape[2]
    padded = jnp.pad(features, ((1, 1), (1, 1), (0, 0)))
    pre_act = forward_taps(padded, w_conv, NH, NW)
    pixel_mask = jnp.repeat(jnp.repeat(tissue.astype(jnp.float32), 2 * TILE, axis=0), 2 * TILE, axis=1)[:, :, None]
    summed = (features.astype(jnp.float32) + jax.nn.silu(pre_act) * pixel_mask).astype(jnp.bfloat16)
    reduced = strided_forward(summed, w_stride)
    pooled = reduced.reshape(NTY, TILE, NTX, TILE, channels).mean(axis=(1, 3))
    normed = rms_normed(pooled).astype(jnp.bfloat16)
    group_owner = owner_map.reshape(N_GY, N_GX, TYD, TXD).transpose(0, 2, 1, 3).reshape(NTY, NTX)
    tile_flags = tissue.astype(jnp.float32)
    norm_scale = 1.0 / math.sqrt(ALL_TILES)
    seed_grad = cotangent * (loss_scale * norm_scale)
    partial_sums = []
    band_grads = []
    for band_index in range(N_GY):
        first_row = band_index * TYD
        band_tokens = normed[first_row:first_row + TYD].reshape(-1, channels).astype(jnp.float32)
        band_flags = tile_flags[first_row:first_row + TYD].reshape(-1)
        band_groups = group_owner[first_row:first_row + TYD].reshape(-1)
        band_fn = partial(self_attend, tile_flags=band_flags, tile_groups=band_groups, w_query=w_query, w_key=w_key, w_value=w_value, head_count=HEADS)
        band_sum, pull_band = jax.vjp(band_fn, band_tokens)
        partial_sums.append(band_sum)
        band_grads.append(pull_band(seed_grad)[0].reshape(TYD, NTX, channels))
    embedding = lax.optimization_barrier(jnp.sum(jnp.stack(partial_sums), axis=0)) * norm_scale
    token_grad = jnp.concatenate(band_grads, axis=0).astype(jnp.bfloat16)
    token_grad = lax.optimization_barrier(token_grad).astype(jnp.float32)
    pooled_grad = jax.vjp(rms_normed, pooled)[1](token_grad)[0]
    cell_grad = (pooled_grad / (TILE * TILE)).astype(jnp.bfloat16)
    cell_grad = jnp.broadcast_to(cell_grad[:, None, :, None, :], (NTY, TILE, NTX, TILE, channels)).reshape(NH // 2, NW // 2, channels)
    sum_grad = strided_backward(cell_grad, w_stride)
    pre_grad = (sum_grad * pixel_mask * silu_slope(pre_act)).astype(jnp.bfloat16)
    grad_pad = jnp.pad(pre_grad, ((1, 1), (1, 1), (0, 0)))
    input_grad = (sum_grad + backward_taps(grad_pad, w_conv, NH, NW)).astype(jnp.bfloat16)
    conv_grad = weight_taps(padded, pre_grad, NH, NW) / loss_scale
    return (embedding, input_grad, conv_grad)
```

```python
import math

import jax
import jax.numpy as jnp
from jax import lax
from jax.experimental import pallas as pl
from jax.experimental.pallas import tpu as pltpu
from jax.sharding import PartitionSpec as P

MESH = pl.DeviceIdType.MESH
F32, BF16 = jnp.float32, jnp.bfloat16
HEADS = 4
attention_bias = -1.0
loss_scale = 512.0

GY, GX = 8, 16
ROWS, COLS, CH = 32, 128, 256
PAD = ROWS + 2
TILES, SLOTS = 16, 32
CONV_ROWS = 4
AXIS_ORDER = (("x", "y", "z"), ("y", "z", "x"), ("z", "x", "y"))
BARRIER_SIGNALS = 32


def exact_dot(a, b, a_dim=1, b_dim=0):
    return lax.dot_general(
        a, b, (((a_dim,), (b_dim,)), ((), ())),
        precision=lax.Precision.HIGHEST, preferred_element_type=F32,
    )


def half_dot(a, b, a_dim=1, b_dim=0):
    return lax.dot_general(
        a.astype(BF16), b.astype(BF16), (((a_dim,), (b_dim,)), ((), ())),
        preferred_element_type=F32,
    )


def three_parts(value):
    high = value.astype(BF16)
    rest = value - high.astype(F32)
    middle = rest.astype(BF16)
    low = (rest - middle.astype(F32)).astype(BF16)
    return high, middle, low


def iota(shape, dim):
    return lax.broadcasted_iota(jnp.int32, shape, dim)


def kernel(
    feat, tissue, owner, w_conv, w_stride, w_query, w_key, w_value, cot,
    emb_out, grad_out, conv_out,
    field, cols3, trans, slope, grad3, taps, taps_t, stride_w, proj, mask,
    sums, spread, send_l, send_r, halo_l, halo_r, gsend_l, gsend_r, ghalo_l, ghalo_r,
    tok_send, tok_recv, ret_send, ret_recv, own_rows, stride_back,
    local_w, pair_w, half_w, hop1, mid_w, hop2, hop3, full_w, emb_buf, out_buf, conv_buf,
    load_sem, halo_ssem, halo_rsem, ghalo_ssem, ghalo_rsem, tok_ssem, tok_rsem,
    ret_ssem, ret_rsem, red_ssem, red_rsem, pair_ssem, pair_rsem, emb_ssem, emb_rsem,
    out_sem,
):
    g, h = lax.axis_index("gy"), lax.axis_index("gx")
    x_hi, y = g // 4, g % 4
    z, x_lo, core = h // 4, (h // 2) % 2, h % 2
    position = {"x": 2 * x_hi + x_lo, "y": y, "z": z}
    partner = (g, h + 1 - 2 * core)

    def on_axis(axis, pos):
        if axis == "x":
            return ((pos // 2) * 4 + y, z * 4 + (pos % 2) * 2 + core)
        if axis == "y":
            return (x_hi * 4 + pos, h)
        return (g, pos * 4 + x_lo * 2 + core)

    up, down = (g + GY - 1) % GY, (g + 1) % GY
    left, right = (h + GX - 1) % GX, (h + 1) % GX

    def remote(src, dst, ssem, rsem, device):
        return pltpu.make_async_remote_copy(
            src_ref=src, dst_ref=dst, send_sem=ssem, recv_sem=rsem,
            device_id=device, device_id_type=MESH,
        )

    barrier = pltpu.get_barrier_semaphore()
    peers = [
        (up, h), (down, h), (g, left), (g, right),
        (up, left), (up, right), (down, left), (down, right),
    ]
    peers += [(g, (h + j) % GX) for j in range(1, GX)]
    for axis in ("x", "y", "z"):
        peers += [on_axis(axis, (position[axis] + j) % 4) for j in range(1, 4)]
    for device in peers:
        pl.semaphore_signal(barrier, inc=1, device_id=device, device_id_type=MESH)

    loads = [
        pltpu.make_async_copy(feat, field.at[pl.ds(1, ROWS)], load_sem.at[0]),
        pltpu.make_async_copy(w_conv, taps, load_sem.at[1]),
        pltpu.make_async_copy(w_stride, stride_w, load_sem.at[2]),
        pltpu.make_async_copy(w_query, proj.at[:, pl.ds(0, CH)], load_sem.at[3]),
        pltpu.make_async_copy(w_key, proj.at[:, pl.ds(CH, CH)], load_sem.at[4]),
        pltpu.make_async_copy(w_value, proj.at[:, pl.ds(2 * CH, CH)], load_sem.at[5]),
    ]
    for copy in loads:
        copy.start()
    loads[0].wait()

    def edge_columns(row, carry):
        send_l[pl.ds(row, 1), :] = field[row + 1, 0:16, :].astype(F32)[0:1, :]
        send_r[pl.ds(row, 1), :] = field[row + 1, COLS - 16 : COLS, :].astype(F32)[15:16, :]
        return carry

    lax.fori_loop(0, ROWS, edge_columns, 0)
    pl.semaphore_wait(barrier, BARRIER_SIGNALS)

    def halo_copies(first_row, last_row, low_row, high_row, col_l, col_r, got_l, got_r, ss, rs):
        top, bottom = pl.ds(0, 8), pl.ds(ROWS - 8, 8)
        return [
            remote(first_row, high_row, ss.at[0], rs.at[0], (up, h)),
            remote(last_row, low_row, ss.at[1], rs.at[1], (down, h)),
            remote(col_l, got_r.at[pl.ds(8, ROWS)], ss.at[2], rs.at[2], (g, left)),
            remote(col_r, got_l.at[pl.ds(8, ROWS)], ss.at[3], rs.at[3], (g, right)),
            remote(col_r.at[bottom], got_l.at[pl.ds(0, 8)], ss.at[4], rs.at[4], (down, right)),
            remote(col_r.at[top], got_l.at[pl.ds(40, 8)], ss.at[5], rs.at[5], (up, right)),
            remote(col_l.at[bottom], got_r.at[pl.ds(0, 8)], ss.at[6], rs.at[6], (down, left)),
            remote(col_l.at[top], got_r.at[pl.ds(40, 8)], ss.at[7], rs.at[7], (up, left)),
        ]

    halos = halo_copies(
        field.at[1], field.at[ROWS], field.at[0], field.at[PAD - 1],
        send_l, send_r, halo_l, halo_r, halo_ssem, halo_rsem,
    )
    for copy in halos:
        copy.start()

    has_left, has_right = h > 0, h < GX - 1
    has_up, has_down = g > 0, g < GY - 1

    def columns_of(center, before, after):
        spot = iota(center.shape, 0)
        low = jnp.where(spot == 0, before, pltpu.roll(center, 1, 0))
        high = jnp.where(spot == COLS - 1, after, pltpu.roll(center, COLS - 1, 0))
        return low, high

    def shift_row(row, carry):
        center = field[row]
        wide = center.astype(F32)
        cols3[row, :, 0:CH] = pltpu.roll(wide, 1, 0).astype(BF16)
        cols3[row, :, CH : 2 * CH] = center
        cols3[row, :, 2 * CH : 3 * CH] = pltpu.roll(wide, COLS - 1, 0).astype(BF16)
        return carry

    lax.fori_loop(1, ROWS + 1, shift_row, 0)
    for tile in range(TILES):
        tr, tc = tile // 8, tile % 8
        flag = tissue[tr, tc].astype(F32)
        mask[tr, tc * 16 : tc * 16 + 16, :] = jnp.zeros((16, CH), F32) + flag
        own_rows[tile : tile + 1, :] = jnp.zeros((1, 128), F32) + owner[0, 0, tile, 0].astype(F32)
    sums[...] = jnp.zeros_like(sums)
    loads[1].wait()

    for copy in halos:
        copy.wait_recv()

    def patch_row(row, carry):
        near = halo_l[pl.ds(7 + row, 1), :]
        far = halo_r[pl.ds(7 + row, 1), :]
        near = jnp.where(has_left, near, 0.0)
        far = jnp.where(has_right, far, 0.0)
        head = cols3[row, 0:16, 0:CH].astype(F32)
        tail = cols3[row, COLS - 16 : COLS, 2 * CH : 3 * CH].astype(F32)
        spot = iota(head.shape, 0)
        cols3[row, 0:16, 0:CH] = jnp.where(spot == 0, near, head).astype(BF16)
        cols3[row, COLS - 16 : COLS, 2 * CH : 3 * CH] = jnp.where(spot == 15, far, tail).astype(BF16)
        return carry

    lax.fori_loop(1, ROWS + 1, patch_row, 0)
    for row, present in ((0, has_up), (PAD - 1, has_down)):
        wide = jnp.where(present, field[row].astype(F32), 0.0)
        near = jnp.where(has_left & present, halo_l[7 + row : 8 + row, :], 0.0)
        far = jnp.where(has_right & present, halo_r[7 + row : 8 + row, :], 0.0)
        low, high = columns_of(wide, near, far)
        cols3[row, :, 0:CH] = low.astype(BF16)
        cols3[row, :, CH : 2 * CH] = wide.astype(BF16)
        cols3[row, :, 2 * CH : 3 * CH] = high.astype(BF16)

    def conv_block(source, weights, first, flipped):
        total = None
        for a in range(3):
            start = first + (2 - a if flipped else a)
            block = source[pl.ds(start, CONV_ROWS)].reshape(CONV_ROWS * COLS, 3 * CH)
            part = jnp.dot(block, weights[a], preferred_element_type=F32)
            total = part if total is None else total + part
        return total.reshape(CONV_ROWS, COLS, CH)

    def forward_block(step, carry):
        first = step * CONV_ROWS
        tr = step // (16 // CONV_ROWS)
        pre = conv_block(cols3, taps, first, False)
        gate = jax.nn.sigmoid(pre)
        slope[pl.ds(first, CONV_ROWS)] = gate * (1.0 + pre * (1.0 - gate))
        own = cols3[pl.ds(first + 1, CONV_ROWS), :, CH : 2 * CH].astype(F32)
        summed = (own + pre * gate * mask[tr][None]).astype(BF16).astype(F32)
        for a in range(2):
            total = sums[tr, a]
            for k in range(a, CONV_ROWS, 2):
                total = total + summed[k]
            sums[tr, a] = total
        return carry

    lax.fori_loop(0, ROWS // CONV_ROWS, forward_block, 0)

    lane_col, row_id = iota((16, COLS), 1), iota((16, COLS), 0)
    select = ((lane_col // 16 == row_id % 8) & (lane_col % 2 == row_id // 8)).astype(BF16)
    gathered = jnp.concatenate([sums[tr, a] for tr in range(2) for a in range(2)], axis=1)
    parts = three_parts(gathered)
    cell_sums = sum(jnp.dot(select, part, preferred_element_type=F32) for part in parts)
    loads[2].wait()
    pooled = jnp.zeros((TILES, CH), F32)
    for a in range(2):
        for b in range(2):
            tap = 2 * a + b
            lhs = jnp.concatenate(
                [cell_sums[b * 8 : b * 8 + 8, (2 * tr + a) * CH : (2 * tr + a + 1) * CH] for tr in range(2)],
                axis=0,
            )
            rhs = stride_w[tap * CH : (tap + 1) * CH, :]
            pooled = pooled + sum(
                jnp.dot(part, rhs, preferred_element_type=F32) for part in three_parts(lhs)
            )
    pooled = pooled * (1.0 / 64.0)
    inverse = lax.rsqrt(jnp.mean(pooled * pooled, axis=-1, keepdims=True) + 1e-05)
    normed = (pooled * inverse).astype(BF16)

    own = own_rows[...]
    lane0 = (iota((TILES, 128), 1) == 0).astype(F32)
    own_across = half_dot(lane0, own, 1, 1)
    same = (own[:, 0:TILES] == own_across) & (iota((TILES, TILES), 1) < iota((TILES, TILES), 0))
    rank = jnp.sum(same.astype(F32), axis=1, keepdims=True)
    slot = own * 8.0 + rank
    slot_lane = iota((TILES, 128), 1).astype(F32)
    place = (slot == slot_lane).astype(F32)
    place_flag = (slot + 2.0 == slot_lane).astype(F32)
    flag_rows = jnp.concatenate(
        [mask[tr, tc * 16 : tc * 16 + 1, :] for tr in range(2) for tc in range(8)], axis=0
    )
    table = half_dot(place, normed, 0, 0) + half_dot(place_flag, flag_rows, 0, 0)
    tok_send[...] = table.reshape(GX, 8, CH)
    tok_copies = [
        remote(
            tok_send.at[(h + j) % GX], tok_recv.at[h], tok_ssem.at[j], tok_rsem.at[j],
            (g, (h + j) % GX),
        )
        for j in range(1, GX)
    ]
    for copy in tok_copies:
        copy.start()
    tok_recv[h] = tok_send[h]

    def transpose_row(row, carry):
        lanes = pl.ds(pl.multiple_of(row * COLS, COLS), COLS)
        for b in range(3):
            trans[b, :, lanes] = cols3[row, :, b * CH : (b + 1) * CH].T
        return carry

    lax.fori_loop(0, PAD, transpose_row, 0)
    for k in range(3, 6):
        loads[k].wait()
    for copy in tok_copies:
        copy.wait_recv()

    got = tok_recv[...].reshape(GX * 8, CH)
    pick_row, pick_lane = iota((2 * SLOTS, GX * 8), 0), iota((2 * SLOTS, GX * 8), 1)
    index = pick_row % SLOTS
    pick = (pick_lane == (index // 2) * 8 + index % 2 + 2 * (pick_row // SLOTS)).astype(BF16)
    packed = half_dot(pick, got)
    tokens, flags = packed[0:SLOTS, :], packed[SLOTS : 2 * SLOTS, :]
    qkv = exact_dot(tokens, proj[...])
    query, key, value = qkv[:, 0:CH], qkv[:, CH : 2 * CH], qkv[:, 2 * CH : 3 * CH]
    head_of = iota((1, CH), 1) // (CH // HEADS)
    heads = [(head_of == k).astype(F32) for k in range(HEADS)]
    seed = cot[...] * (loss_scale / math.sqrt(GY * GX * TILES))
    query_by_head = jnp.concatenate([query * m for m in heads], axis=0)
    flag_by_head = jnp.concatenate([flags * m for m in heads], axis=0)
    scale = 1.0 / math.sqrt(CH // HEADS)
    scores = exact_dot(query_by_head, key, 1, 1) * scale
    first_lane = (iota((HEADS * SLOTS, CH), 1) == 0).astype(F32)
    key_flags = half_dot(first_lane, flags, 1, 1)
    gates = jax.nn.sigmoid(scores + attention_bias)
    column_sums = exact_dot(gates * key_flags, flag_by_head, 0, 0)
    d_value = column_sums * seed
    partial = jnp.sum(column_sums * value, axis=0, keepdims=True)
    d_weights = exact_dot(flag_by_head * seed, value, 1, 1)
    d_scores = d_weights * key_flags * gates * (1.0 - gates) * scale
    d_query_all = exact_dot(d_scores, key)
    d_query = sum(d_query_all[k * SLOTS : (k + 1) * SLOTS, :] * heads[k] for k in range(HEADS))
    d_key = exact_dot(d_scores, query_by_head, 0, 0)
    d_qkv = jnp.concatenate([d_query, d_key, d_value], axis=1)
    d_tokens = exact_dot(d_qkv, proj[...], 1, 1)
    back_row, back_lane = iota((GX * 8, SLOTS), 0), iota((GX * 8, SLOTS), 1)
    unpick = (back_row == (back_lane // 2) * 8 + back_lane % 2).astype(BF16)
    ret_send[...] = half_dot(unpick, d_tokens).reshape(GX, 8, CH)
    ret_copies = [
        remote(
            ret_send.at[(h + j) % GX], ret_recv.at[h], ret_ssem.at[j], ret_rsem.at[j],
            (g, (h + j) % GX),
        )
        for j in range(1, GX)
    ]
    for copy in ret_copies:
        copy.start()
    ret_recv[h] = ret_send[h]

    emb_steps = [("core", 2, core)] + [(axis, 4, position[axis]) for axis in ("x", "y", "z")]

    def emb_copies(step):
        axis, count, pos = emb_steps[step]
        copies = []
        for j in range(1, count):
            device = partner if axis == "core" else on_axis(axis, (pos + j) % 4)
            spot = emb_buf.at[step, pos]
            copies.append(
                remote(spot, spot, emb_ssem.at[step, j], emb_rsem.at[step, j], device)
            )
        return copies

    def emb_start(step, term):
        emb_buf[step, emb_steps[step][2]] = term
        for copy in emb_copies(step):
            copy.start()

    def emb_finish(step):
        for copy in emb_copies(step):
            copy.wait_recv()
        total = emb_buf[step, 0]
        for k in range(1, emb_steps[step][1]):
            total = total + emb_buf[step, k]
        return total

    emb_start(0, jnp.broadcast_to(partial, (8, CH)))

    for a in range(3):
        for b in range(3):
            taps_t[a, b * CH : (b + 1) * CH, :] = taps[a, b * CH : (b + 1) * CH, :].T

    for copy in ret_copies:
        copy.wait_recv()
    token_grad = half_dot(place, ret_recv[...].reshape(GX * 8, CH)) * flag_rows
    inner = jnp.mean(token_grad * pooled, axis=-1, keepdims=True)
    pooled_grad = token_grad * inverse - pooled * (inverse * inverse * inverse * inner)
    cell_grad = (pooled_grad * (1.0 / 64.0)).astype(BF16)
    stride_back[...] = half_dot(cell_grad, stride_w[...], 1, 1)
    odd = (iota((16, CH), 0) % 2) == 1
    for tile in range(TILES):
        tr, tc = tile // 8, tile % 8
        for a in range(2):
            even_row = stride_back[tile : tile + 1, (2 * a) * CH : (2 * a + 1) * CH]
            odd_row = stride_back[tile : tile + 1, (2 * a + 1) * CH : (2 * a + 2) * CH]
            spread[tr, a, tc * 16 : tc * 16 + 16, :] = jnp.where(odd, odd_row, even_row)

    def pre_grad_row(row, carry):
        tr = row // 16
        value = (spread[tr, row % 2] * mask[tr] * slope[row]).astype(BF16)
        grad3[row + 1, :, CH : 2 * CH] = value
        wide = value.astype(F32)
        gsend_l[pl.ds(row, 1), :] = wide[0:1, :]
        gsend_r[pl.ds(row, 1), :] = wide[COLS - 1 : COLS, :]
        return carry

    lax.fori_loop(0, ROWS, pre_grad_row, 0)
    middle = pl.ds(CH, CH)
    ghalos = halo_copies(
        grad3.at[1, :, middle], grad3.at[ROWS, :, middle],
        grad3.at[0, :, middle], grad3.at[PAD - 1, :, middle],
        gsend_l, gsend_r, ghalo_l, ghalo_r, ghalo_ssem, ghalo_rsem,
    )
    for copy in ghalos:
        copy.start()

    def pair_copy(k):
        rows = pl.ds(k * 768, 768)
        return remote(
            local_w.at[1 - core, rows], pair_w.at[rows], pair_ssem.at[0, k], pair_rsem.at[0, k], partner
        )

    def axis_copies(k, step, axis, source, target):
        pos = position[axis]
        copies = []
        for j in range(1, 4):
            to = (pos + j) % 4
            copies.append(
                remote(
                    source(to), target(j), red_ssem.at[step, k, j], red_rsem.at[step, k, j],
                    on_axis(axis, to),
                )
            )
        return copies

    def aligned(value):
        return pl.multiple_of(value, 16)

    def home_rows(k, count):
        first, second, _ = AXIS_ORDER[k]
        start = k * 768 + position[first] * 192
        if count == 48:
            start = start + position[second] * 48
        return pl.ds(aligned(start), count)

    def hop_copies(k, step):
        first, second, third = AXIS_ORDER[k]
        if step == 1:
            return axis_copies(
                k, 0, first,
                lambda to: half_w.at[pl.ds(aligned(k * 768 + to * 192), 192)],
                lambda j: hop1.at[k, j - 1],
            )
        if step == 2:
            return axis_copies(
                k, 1, second,
                lambda to: mid_w.at[k, pl.ds(aligned(to * 48), 48)],
                lambda j: hop2.at[k, j - 1],
            )
        if step == 3:
            spot = hop3.at[k, position[third]]
            return axis_copies(k, 2, third, lambda to: spot, lambda j: spot)
        if step == 4:
            spot = full_w.at[core, home_rows(k, 48)]
            return axis_copies(k, 3, second, lambda to: spot, lambda j: spot)
        spot = full_w.at[core, home_rows(k, 192)]
        return axis_copies(k, 4, first, lambda to: spot, lambda j: spot)

    def last_copy(k):
        spot = full_w.at[core, pl.ds(k * 768, 768)]
        return remote(spot, spot, pair_ssem.at[1, k], pair_rsem.at[1, k], partner)

    def reduce_step(k, step):
        first, second, third = AXIS_ORDER[k]
        if step == 0:
            pair_copy(k).start()
            return
        if step == 1:
            pair_copy(k).wait_recv()
            rows = pl.ds(k * 768, 768)
            both = local_w[core, rows].astype(F32) + pair_w[rows].astype(F32)
            half_w[rows] = both.astype(BF16)
        elif step == 7:
            last_copy(k).wait_recv()
            rows = pl.ds(k * 768, 768)
            for c in range(2):
                conv_buf[rows, c * 128 : c * 128 + 128] = full_w[c, rows].astype(F32) * (1.0 / loss_scale)
            return
        else:
            for copy in hop_copies(k, step - 1):
                copy.wait_recv()
            if step == 2:
                total = half_w[pl.ds(aligned(k * 768 + position[first] * 192), 192)].astype(F32)
                for j in range(3):
                    total = total + hop1[k, j].astype(F32)
                mid_w[k] = total.astype(BF16)
            elif step == 3:
                total = mid_w[k, pl.ds(aligned(position[second] * 48), 48)].astype(F32)
                for j in range(3):
                    total = total + hop2[k, j].astype(F32)
                hop3[k, position[third]] = total.astype(BF16)
            elif step == 4:
                total = hop3[k, 0].astype(F32)
                for j in range(1, 4):
                    total = total + hop3[k, j].astype(F32)
                full_w[core, home_rows(k, 48)] = total.astype(BF16)
        if step == 6:
            last_copy(k).start()
        else:
            for copy in hop_copies(k, step):
                copy.start()

    for a in range(3):
        def tap_of(b, carry):
            lhs = trans[b, :, a * COLS : a * COLS + ROWS * COLS]
            rhs = grad3[pl.ds(1, ROWS), :, CH : 2 * CH].reshape(ROWS * COLS, CH)
            part = jnp.dot(lhs, rhs, preferred_element_type=F32)
            rows = pl.ds(pl.multiple_of(a * 768 + b * CH, CH), CH)
            for c in range(2):
                local_w[c, rows, :] = part[:, c * 128 : c * 128 + 128].astype(BF16)
            return carry

        lax.fori_loop(0, 3, tap_of, 0)
        for k in range(a, -1, -1):
            reduce_step(k, a - k)
        if a:
            emb_start(a, emb_finish(a - 1))

    for copy in ghalos:
        copy.wait_recv()

    def grad_shift(row, carry):
        wide = grad3[row, :, CH : 2 * CH].astype(F32)
        near = jnp.where(has_left, ghalo_l[pl.ds(7 + row, 1), :], 0.0)
        far = jnp.where(has_right, ghalo_r[pl.ds(7 + row, 1), :], 0.0)
        low, high = columns_of(wide, near, far)
        grad3[row, :, 0:CH] = high.astype(BF16)
        grad3[row, :, 2 * CH : 3 * CH] = low.astype(BF16)
        return carry

    lax.fori_loop(0, PAD, grad_shift, 0)
    for row, present in ((0, has_up), (PAD - 1, has_down)):
        edge = grad3[row].astype(F32)
        grad3[row] = jnp.where(present, edge, 0.0).astype(BF16)

    def out_copy(first):
        rows = pl.ds(first, CONV_ROWS)
        return pltpu.make_async_copy(out_buf.at[rows], grad_out.at[rows], out_sem.at[0])

    def back_block(step, carry):
        first = step * CONV_ROWS
        tr = step // (16 // CONV_ROWS)
        total = conv_block(grad3, taps_t, first, True)
        for k in range(CONV_ROWS):
            out_buf[first + k] = (total[k] + spread[tr, k % 2]).astype(BF16)
        return carry

    blocks = ROWS // CONV_ROWS
    order = [
        [(2, 1), (1, 2), (0, 3)],
        [(0, 4)],
        [(2, 2), (1, 3)],
        [(0, 5)],
        [(2, 3), (1, 4)],
        [(0, 6)],
        [(2, 4), (1, 5)],
        [(0, 7)],
    ]
    for step in range(4):
        for k, phase in order[step]:
            reduce_step(k, phase)
        lax.fori_loop(2 * step, 2 * step + 2, back_block, 0)
    emb_start(3, emb_finish(2))
    whole_out = pltpu.make_async_copy(out_buf, grad_out, out_sem.at[0])
    whole_out.start()
    for step in range(4, 8):
        for k, phase in order[step]:
            reduce_step(k, phase)
    for k, phase in [(2, 5), (1, 6), (2, 6), (1, 7), (2, 7)]:
        reduce_step(k, phase)
    emb_out[...] = emb_finish(3)[0:1, :] * (1.0 / math.sqrt(GY * GX * TILES))
    conv_copy = pltpu.make_async_copy(conv_buf, conv_out, out_sem.at[1])
    conv_copy.start()

    for copy in halos + ghalos + tok_copies + ret_copies:
        copy.wait_send()
    for k in range(3):
        pair_copy(k).wait_send()
        for step in range(1, 6):
            for copy in hop_copies(k, step):
                copy.wait_send()
        last_copy(k).wait_send()
    for step in range(4):
        for copy in emb_copies(step):
            copy.wait_send()
    whole_out.wait()
    conv_copy.wait()


def per_device(features, tissue, owner_map, w_conv, w_stride, w_query, w_key, w_value, cotangent):
    whole = pl.BlockSpec(memory_space=pl.ANY)
    scalars = pl.BlockSpec(memory_space=pltpu.SMEM)
    vector = pl.BlockSpec(memory_space=pltpu.VMEM)
    dma = pltpu.SemaphoreType.DMA
    columns = pltpu.VMEM((ROWS, CH), F32)
    column_halo = pltpu.VMEM((ROWS + 16, CH), F32)
    slot_table = pltpu.VMEM((GX, 8, CH), F32)
    embedding, input_grad, conv_grad = pl.pallas_call(
        kernel,
        out_shape=(
            jax.ShapeDtypeStruct((1, CH), F32),
            jax.ShapeDtypeStruct((ROWS, COLS, CH), BF16),
            jax.ShapeDtypeStruct((9 * CH, CH), F32),
        ),
        in_specs=[whole, scalars, scalars, whole, whole, whole, whole, whole, vector],
        out_specs=(vector, whole, whole),
        scratch_shapes=[
            pltpu.VMEM((PAD, COLS, CH), BF16),
            pltpu.VMEM((PAD, COLS, 3 * CH), BF16),
            pltpu.VMEM((3, CH, PAD * COLS), BF16),
            pltpu.VMEM((ROWS, COLS, CH), F32),
            pltpu.VMEM((PAD, COLS, 3 * CH), BF16),
            pltpu.VMEM((3, 3 * CH, CH), BF16),
            pltpu.VMEM((3, 3 * CH, CH), BF16),
            pltpu.VMEM((4 * CH, CH), BF16),
            pltpu.VMEM((CH, 3 * CH), F32),
            pltpu.VMEM((2, COLS, CH), F32),
            pltpu.VMEM((2, 2, COLS, CH), F32),
            pltpu.VMEM((2, 2, COLS, CH), F32),
            columns, columns, column_halo, column_halo,
            columns, columns, column_halo, column_halo,
            slot_table, slot_table, slot_table, slot_table,
            pltpu.VMEM((TILES, 128), F32),
            pltpu.VMEM((TILES, 4 * CH), F32),
            pltpu.VMEM((2, 9 * CH, 128), BF16),
            pltpu.VMEM((9 * CH, 128), BF16),
            pltpu.VMEM((9 * CH, 128), BF16),
            pltpu.VMEM((3, 3, 192, 128), BF16),
            pltpu.VMEM((3, 192, 128), BF16),
            pltpu.VMEM((3, 3, 48, 128), BF16),
            pltpu.VMEM((3, 4, 48, 128), BF16),
            pltpu.VMEM((2, 9 * CH, 128), BF16),
            pltpu.VMEM((4, 4, 8, CH), F32),
            pltpu.VMEM((ROWS, COLS, CH), BF16),
            pltpu.VMEM((9 * CH, CH), F32),
            dma((6,)), dma((8,)), dma((8,)), dma((8,)), dma((8,)),
            dma((GX,)), dma((GX,)), dma((GX,)), dma((GX,)),
            dma((5, 3, 4)), dma((5, 3, 4)), dma((2, 3)), dma((2, 3)),
            dma((4, 4)), dma((4, 4)), dma((2,)),
        ],
        compiler_params=pltpu.CompilerParams(
            collective_id=0, has_side_effects=True, vmem_limit_bytes=60 * 1024 * 1024
        ),
    )(
        features, tissue, owner_map, w_conv.reshape(3, 3 * CH, CH),
        w_stride.reshape(4 * CH, CH), w_query, w_key, w_value, cotangent.reshape(1, CH),
    )
    return embedding.reshape(CH), input_grad, conv_grad.reshape(9, CH, CH)


def solution(mesh):
    in_specs = (
        P("gy", "gx", None), P("gy", "gx"), P("gy", "gx", None, None),
        P(), P(), P(), P(), P(), P(),
    )
    out_specs = (P(), P("gy", "gx", None), P())
    return jax.shard_map(
        per_device, mesh=mesh, in_specs=in_specs, out_specs=out_specs, check_vma=False
    )
```

```python
import math

import jax
import jax.numpy as jnp
from jax import lax
from jax.experimental import pallas as pl
from jax.experimental.pallas import tpu as pltpu
from jax.sharding import PartitionSpec as P

MESH = pl.DeviceIdType.MESH
F32, BF16 = jnp.float32, jnp.bfloat16
HEADS = 4
attention_bias = -1.0
loss_scale = 512.0

GY, GX = 8, 16
ROWS, COLS, CH = 32, 128, 256
PAD = ROWS + 2
TILES = 16
CONV_ROWS = 4
CHUNKS = ((0, 3, "xyz"), (3, 3, "yzx"), (6, 2, "zxy"), (8, 1, "xyz"))
BARRIER_SIGNALS = 23 + 15 * 3


def exact_dot(a, b, a_dim=1, b_dim=0):
    return lax.dot_general(
        a, b, (((a_dim,), (b_dim,)), ((), ())),
        precision=lax.Precision.HIGHEST, preferred_element_type=F32,
    )


def half_dot(a, b, a_dim=1, b_dim=0):
    return lax.dot_general(
        a.astype(BF16), b.astype(BF16), (((a_dim,), (b_dim,)), ((), ())),
        preferred_element_type=F32,
    )


def three_parts(value):
    high = value.astype(BF16)
    rest = value - high.astype(F32)
    middle = rest.astype(BF16)
    low = (rest - middle.astype(F32)).astype(BF16)
    return high, middle, low


def iota(shape, dim):
    return lax.broadcasted_iota(jnp.int32, shape, dim)


def kernel(
    feat, tissue, owner, w_conv, w_stride, w_query, w_key, w_value, cot,
    emb_out, out_buf, full_w,
    field, cols3, trans, slope, grad3, taps, taps_t, stride_w, proj, parts3, mask,
    sums, spread, send_l, send_r, halo_l, halo_r, gsend_l, gsend_r, ghalo_l, ghalo_r,
    edge_l, edge_r, tok_buf, code_rows, stride_back,
    local_w, pair_w, half_w, plane_w, line_w, emb_buf,
    load_sem, halo_ssem, halo_rsem, ghalo_ssem, ghalo_rsem, tok_ssem, tok_rsem,
    plane_ssem, plane_rsem, line_ssem, line_rsem, pair_ssem, pair_rsem, emb_ssem, emb_rsem,
):
    g, h = lax.axis_index("gy"), lax.axis_index("gx")
    x_hi, y = g // 4, g % 4
    z, x_lo, core = h // 4, (h // 2) % 2, h % 2
    position = {"x": 2 * x_hi + x_lo, "y": y, "z": z}
    partner = (g, h + 1 - 2 * core)

    def device_at(**moved):
        spot = dict(position, **moved)
        return (
            (spot["x"] // 2) * 4 + spot["y"],
            spot["z"] * 4 + (spot["x"] % 2) * 2 + core,
        )

    def on_axis(axis, pos):
        return device_at(**{axis: pos})

    def on_plane(axes, member):
        return device_at(**{axes[0]: member // 4, axes[1]: member % 4})

    def member_of(axes):
        return position[axes[0]] * 4 + position[axes[1]]

    up, down = (g + GY - 1) % GY, (g + 1) % GY
    left, right = (h + GX - 1) % GX, (h + 1) % GX

    def remote(src, dst, ssem, rsem, device):
        return pltpu.make_async_remote_copy(
            src_ref=src, dst_ref=dst, send_sem=ssem, recv_sem=rsem,
            device_id=device, device_id_type=MESH,
        )

    barrier = pltpu.get_barrier_semaphore()
    peers = [
        (up, h), (down, h), (g, left), (g, right),
        (up, left), (up, right), (down, left), (down, right),
    ]
    peers += [(g, (h + j) % GX) for j in range(1, GX)]
    for axes in ("xy", "yz", "zx"):
        peers += [on_plane(axes, (member_of(axes) + j) % 16) for j in range(1, 16)]
    for device in peers:
        pl.semaphore_signal(barrier, inc=1, device_id=device, device_id_type=MESH)

    loads = [
        pltpu.make_async_copy(feat, field.at[pl.ds(1, ROWS)], load_sem.at[0]),
        pltpu.make_async_copy(w_conv, taps, load_sem.at[1]),
        pltpu.make_async_copy(w_stride, stride_w, load_sem.at[2]),
        pltpu.make_async_copy(w_query, proj.at[:, pl.ds(0, CH)], load_sem.at[3]),
        pltpu.make_async_copy(w_key, proj.at[:, pl.ds(CH, CH)], load_sem.at[4]),
        pltpu.make_async_copy(w_value, proj.at[:, pl.ds(2 * CH, CH)], load_sem.at[5]),
    ]
    for copy in loads:
        copy.start()
    for tile in range(TILES):
        tr, tc = tile // 8, tile % 8
        flag = tissue[tr, tc].astype(F32)
        code = flag * (owner[0, tile].astype(F32) + 1.0)
        mask[tr, tc * 16 : tc * 16 + 16, :] = jnp.zeros((16, CH), F32) + flag
        code_rows[tile : tile + 1, :] = jnp.zeros((1, 128), F32) + code
    sums[...] = jnp.zeros_like(sums)
    loads[0].wait()

    def edge_columns(row, carry):
        send_l[pl.ds(row, 1), :] = field[row + 1, 0:16, :].astype(F32)[0:1, :]
        send_r[pl.ds(row, 1), :] = field[row + 1, COLS - 16 : COLS, :].astype(F32)[15:16, :]
        return carry

    lax.fori_loop(0, ROWS, edge_columns, 0)
    def halo_copies(first_row, last_row, low_row, high_row, col_l, col_r, got_l, got_r, ss, rs):
        top, bottom = pl.ds(0, 8), pl.ds(ROWS - 8, 8)
        return [
            remote(first_row, high_row, ss.at[0], rs.at[0], (up, h)),
            remote(last_row, low_row, ss.at[1], rs.at[1], (down, h)),
            remote(col_l, got_r.at[pl.ds(8, ROWS)], ss.at[2], rs.at[2], (g, left)),
            remote(col_r, got_l.at[pl.ds(8, ROWS)], ss.at[3], rs.at[3], (g, right)),
            remote(col_r.at[bottom], got_l.at[pl.ds(0, 8)], ss.at[4], rs.at[4], (down, right)),
            remote(col_r.at[top], got_l.at[pl.ds(40, 8)], ss.at[5], rs.at[5], (up, right)),
            remote(col_l.at[bottom], got_r.at[pl.ds(0, 8)], ss.at[6], rs.at[6], (down, left)),
            remote(col_l.at[top], got_r.at[pl.ds(40, 8)], ss.at[7], rs.at[7], (up, left)),
        ]

    has_left, has_right = h > 0, h < GX - 1
    has_up, has_down = g > 0, g < GY - 1

    def columns_of(center, before, after):
        spot = iota(center.shape, 0)
        low = jnp.where(spot == 0, before, pltpu.roll(center, 1, 0))
        high = jnp.where(spot == COLS - 1, after, pltpu.roll(center, COLS - 1, 0))
        return low, high

    def shift_row(row, carry):
        center = field[row]
        low, high = columns_of(center.astype(F32), 0.0, 0.0)
        cols3[row, :, 0:CH] = low.astype(BF16)
        cols3[row, :, CH : 2 * CH] = center
        cols3[row, :, 2 * CH : 3 * CH] = high.astype(BF16)
        return carry

    lax.fori_loop(1, ROWS + 1, shift_row, 0)
    loads[1].wait()

    def conv_block(source, weights, first, flipped):
        total = None
        for a in range(3):
            start = first + (2 - a if flipped else a)
            block = source[pl.ds(start, CONV_ROWS)].reshape(CONV_ROWS * COLS, 3 * CH)
            part = jnp.dot(block, weights[a], preferred_element_type=F32)
            total = part if total is None else total + part
        return total.reshape(CONV_ROWS, COLS, CH)

    def forward_block(step, carry):
        first = step * CONV_ROWS
        tr = step // (16 // CONV_ROWS)
        pre = conv_block(cols3, taps, first, False)
        for k in range(CONV_ROWS):
            edge_l[pl.ds(first + k, 1), :] = pre[k, 0:1, :]
            edge_r[pl.ds(first + k, 1), :] = pre[k, COLS - 1 : COLS, :]
        gate = jax.nn.sigmoid(pre)
        slope[pl.ds(first, CONV_ROWS)] = gate * (1.0 + pre * (1.0 - gate))
        own = cols3[pl.ds(first + 1, CONV_ROWS), :, CH : 2 * CH].astype(F32)
        summed = (own + pre * gate * mask[tr][None]).astype(BF16).astype(F32)
        for a in range(2):
            total = sums[tr, a]
            for k in range(a, CONV_ROWS, 2):
                total = total + summed[k]
            sums[tr, a] = total
        return carry

    lax.fori_loop(1, 3, forward_block, 0)
    pl.semaphore_wait(barrier, BARRIER_SIGNALS)
    halos = halo_copies(
        field.at[1], field.at[ROWS], field.at[0], field.at[PAD - 1],
        send_l, send_r, halo_l, halo_r, halo_ssem, halo_rsem,
    )
    for copy in halos:
        copy.start()
    lax.fori_loop(3, 7, forward_block, 0)

    def transpose_middle(row, carry):
        lanes = pl.ds(pl.multiple_of(row * COLS, COLS), COLS)
        trans[1, :, lanes] = cols3[row, :, CH : 2 * CH].T
        return carry

    lax.fori_loop(1, ROWS + 1, transpose_middle, 0)
    for a in range(3):
        for b in range(3):
            taps_t[a, b * CH : (b + 1) * CH, :] = taps[a, b * CH : (b + 1) * CH, :].T
    for k in range(3, 6):
        loads[k].wait()
    for k, part in enumerate(three_parts(proj[...])):
        parts3[k] = part
    for copy in halos:
        copy.wait_recv()

    def patch_row(row, carry):
        near = halo_l[pl.ds(7 + row, 1), :]
        far = halo_r[pl.ds(7 + row, 1), :]
        near = jnp.where(has_left, near, 0.0)
        far = jnp.where(has_right, far, 0.0)
        head = cols3[row, 0:16, 0:CH].astype(F32)
        tail = cols3[row, COLS - 16 : COLS, 2 * CH : 3 * CH].astype(F32)
        spot = iota(head.shape, 0)
        cols3[row, 0:16, 0:CH] = jnp.where(spot == 0, near, head).astype(BF16)
        cols3[row, COLS - 16 : COLS, 2 * CH : 3 * CH] = jnp.where(spot == 15, far, tail).astype(BF16)
        return carry

    lax.fori_loop(1, ROWS + 1, patch_row, 0)
    for row, present in ((0, has_up), (PAD - 1, has_down)):
        wide = jnp.where(present, field[row].astype(F32), 0.0)
        near = jnp.where(has_left & present, halo_l[7 + row : 8 + row, :], 0.0)
        far = jnp.where(has_right & present, halo_r[7 + row : 8 + row, :], 0.0)
        low, high = columns_of(wide, near, far)
        cols3[row, :, 0:CH] = low.astype(BF16)
        cols3[row, :, CH : 2 * CH] = wide.astype(BF16)
        cols3[row, :, 2 * CH : 3 * CH] = high.astype(BF16)

    lax.fori_loop(0, 2, lambda i, carry: forward_block(i * 7, carry), 0)
    row_of = iota((ROWS, CH), 0)
    inner_row = (row_of >= CONV_ROWS) & (row_of < ROWS - CONV_ROWS)

    def fix_edge(got, present, edge, own, tap_at, col):
        terms = [jnp.where(present, got[7 + a : 7 + a + ROWS, :], 0.0).astype(BF16) for a in range(3)]
        pre = edge[...]
        flag = jnp.where(row_of < 16, mask[0, col : col + 1, :], mask[1, col : col + 1, :])
        old = (own[...] + pre * jax.nn.sigmoid(pre) * flag).astype(BF16).astype(F32)
        for a in range(3):
            pre = pre + jnp.dot(
                terms[a], taps[a, tap_at * CH : (tap_at + 1) * CH, :], preferred_element_type=F32
            )
        gate = jax.nn.sigmoid(pre)
        new = (own[...] + pre * gate * flag).astype(BF16).astype(F32)
        slant = gate * (1.0 + pre * (1.0 - gate))
        change = jnp.where(inner_row, new - old, 0.0)
        for tr in range(2):
            for a in range(2):
                part = jnp.where((row_of // 16 == tr) & (row_of % 2 == a), change, 0.0)
                sums[tr, a, col : col + 1, :] = sums[tr, a, col : col + 1, :] + jnp.sum(
                    part, axis=0, keepdims=True
                )
        for row in range(CONV_ROWS, ROWS - CONV_ROWS):
            slope[row, col : col + 1, :] = slant[row : row + 1, :]

    fix_edge(halo_l, has_left, edge_l, send_l, 0, 0)
    fix_edge(halo_r, has_right, edge_r, send_r, 2, COLS - 1)


    lane_col, row_id = iota((16, COLS), 1), iota((16, COLS), 0)
    select = ((lane_col // 16 == row_id % 8) & (lane_col % 2 == row_id // 8)).astype(BF16)
    gathered = jnp.concatenate([sums[tr, a] for tr in range(2) for a in range(2)], axis=1)
    parts = three_parts(gathered)
    cell_sums = sum(jnp.dot(select, part, preferred_element_type=F32) for part in parts)
    loads[2].wait()
    pooled = jnp.zeros((TILES, CH), F32)
    for a in range(2):
        for b in range(2):
            tap = 2 * a + b
            lhs = jnp.concatenate(
                [cell_sums[b * 8 : b * 8 + 8, (2 * tr + a) * CH : (2 * tr + a + 1) * CH] for tr in range(2)],
                axis=0,
            )
            rhs = stride_w[tap * CH : (tap + 1) * CH, :]
            pooled = pooled + sum(
                jnp.dot(part, rhs, preferred_element_type=F32) for part in three_parts(lhs)
            )
    pooled = pooled * (1.0 / 64.0)
    inverse = lax.rsqrt(jnp.mean(pooled * pooled, axis=-1, keepdims=True) + 1e-05)
    normed = (pooled * inverse).astype(BF16)

    code = code_rows[...]
    tok_buf[h, :, 0:CH] = normed
    tok_buf[h, :, CH : CH + 128] = code.astype(BF16)
    tok_copies = [
        remote(tok_buf.at[h], tok_buf.at[h], tok_ssem.at[j], tok_rsem.at[j], (g, (h + j) % GX))
        for j in range(1, GX)
    ]
    for copy in tok_copies:
        copy.start()

    head_of = iota((1, CH), 1) // (CH // HEADS)
    heads = [(head_of == k).astype(F32) for k in range(HEADS)]

    def by_head(rows):
        return jnp.concatenate([rows * m for m in heads], axis=0)

    def join_heads(rows):
        return sum(rows[k * TILES : (k + 1) * TILES, :] * heads[k] for k in range(HEADS))

    own_qkv = sum(jnp.dot(normed, parts3[k], preferred_element_type=F32) for k in range(3))
    own_value = own_qkv[:, 2 * CH : 3 * CH]
    query_by_head, key_by_head = by_head(own_qkv[:, 0:CH]), by_head(own_qkv[:, CH : 2 * CH])
    seed = cot[...] * (loss_scale / math.sqrt(GY * GX * TILES))
    seed_by_head = by_head(jnp.broadcast_to(seed, (8, CH)))
    value_seed = exact_dot(seed_by_head, proj[:, 2 * CH : 3 * CH], 1, 1)
    own_value_seed = jnp.sum(by_head(own_value * seed), axis=1, keepdims=True)

    def transpose_row(row, carry):
        lanes = pl.ds(pl.multiple_of(row * COLS, COLS), COLS)
        for b in (0, 2):
            trans[b, :, lanes] = cols3[row, :, b * CH : (b + 1) * CH].T
        return carry

    lax.fori_loop(0, PAD, transpose_row, 0)
    for row in (0, PAD - 1):
        trans[1, :, row * COLS : (row + 1) * COLS] = cols3[row, :, CH : 2 * CH].T
    for copy in tok_copies:
        copy.wait_recv()

    everyone = tok_buf[:, :, 0:CH].reshape(GX * TILES, CH)
    codes = tok_buf[:, :, CH : CH + 128].reshape(GX * TILES, 128)
    all_qk = sum(
        jnp.dot(everyone, parts3[k, :, 0 : 2 * CH], preferred_element_type=F32) for k in range(3)
    )
    all_query, all_key = all_qk[:, 0:CH], all_qk[:, CH : 2 * CH]
    lane0 = (iota((TILES, 128), 1) == 0).astype(F32)
    codes_across = half_dot(lane0, codes, 1, 1)
    allowed = ((codes_across == code[:, 0:1]) & (codes_across > 0.5)).astype(F32)
    allowed = jnp.concatenate([allowed] * HEADS, axis=0)
    scale = 1.0 / math.sqrt(CH // HEADS)
    as_query = jax.nn.sigmoid(exact_dot(query_by_head, all_key, 1, 1) * scale + attention_bias)
    as_key = jax.nn.sigmoid(exact_dot(key_by_head, all_query, 1, 1) * scale + attention_bias)
    weight_sums = jnp.sum(as_key * allowed, axis=1, keepdims=True)
    head_sums = join_heads(jnp.broadcast_to(weight_sums, (HEADS * TILES, CH)))
    partial = jnp.sum(head_sums * own_value, axis=0, keepdims=True)
    d_value = head_sums * seed
    across = sum(half_dot(part, everyone, 1, 1) for part in three_parts(value_seed))
    across = jnp.concatenate([across[8 * k : 8 * k + 8, :] for k in range(HEADS) for _ in range(2)], axis=0)
    d_as_query = across * allowed * as_query * (1.0 - as_query) * scale
    d_as_key = own_value_seed * allowed * as_key * (1.0 - as_key) * scale
    d_query = join_heads(exact_dot(d_as_query, all_key))
    d_key = join_heads(exact_dot(d_as_key, all_query))
    d_qkv = three_parts(jnp.concatenate([d_query, d_key, d_value], axis=1))
    d_tokens = jnp.zeros((TILES, CH), F32)
    for k in range(3):
        lhs = jnp.concatenate(d_qkv[: 3 - k], axis=0)
        product = half_dot(lhs, parts3[k], 1, 1)
        for part in range(3 - k):
            d_tokens = d_tokens + product[part * TILES : (part + 1) * TILES, :]
    token_grad = d_tokens.astype(BF16).astype(F32)

    emb_steps = [("core", 2, core)] + [(axis, 4, position[axis]) for axis in ("x", "y", "z")]

    def emb_copies(step):
        axis, count, pos = emb_steps[step]
        copies = []
        for j in range(1, count):
            device = partner if axis == "core" else on_axis(axis, (pos + j) % 4)
            spot = emb_buf.at[step, pos]
            copies.append(
                remote(spot, spot, emb_ssem.at[step, j], emb_rsem.at[step, j], device)
            )
        return copies

    def emb_start(step, term):
        emb_buf[step, emb_steps[step][2]] = term
        for copy in emb_copies(step):
            copy.start()

    def emb_finish(step):
        for copy in emb_copies(step):
            copy.wait_recv()
        total = emb_buf[step, 0]
        for k in range(1, emb_steps[step][1]):
            total = total + emb_buf[step, k]
        return total

    emb_start(0, jnp.broadcast_to(partial, (8, CH)))

    inner = jnp.mean(token_grad * pooled, axis=-1, keepdims=True)
    pooled_grad = token_grad * inverse - pooled * (inverse * inverse * inverse * inner)
    cell_grad = (pooled_grad * (1.0 / 64.0)).astype(BF16)
    stride_back[...] = half_dot(cell_grad, stride_w[...], 1, 1)
    odd = (iota((16, CH), 0) % 2) == 1
    for tile in range(TILES):
        tr, tc = tile // 8, tile % 8
        for a in range(2):
            even_row = stride_back[tile : tile + 1, (2 * a) * CH : (2 * a + 1) * CH]
            odd_row = stride_back[tile : tile + 1, (2 * a + 1) * CH : (2 * a + 2) * CH]
            spread[tr, a, tc * 16 : tc * 16 + 16, :] = jnp.where(odd, odd_row, even_row)

    def pre_grad_row(row, carry):
        tr = row // 16
        value = (spread[tr, row % 2] * mask[tr] * slope[row]).astype(BF16)
        grad3[row + 1, :, CH : 2 * CH] = value
        wide = value.astype(F32)
        gsend_l[pl.ds(row, 1), :] = wide[0:1, :]
        gsend_r[pl.ds(row, 1), :] = wide[COLS - 1 : COLS, :]
        return carry

    lax.fori_loop(0, ROWS, pre_grad_row, 0)
    middle = pl.ds(CH, CH)
    ghalos = halo_copies(
        grad3.at[1, :, middle], grad3.at[ROWS, :, middle],
        grad3.at[0, :, middle], grad3.at[PAD - 1, :, middle],
        gsend_l, gsend_r, ghalo_l, ghalo_r, ghalo_ssem, ghalo_rsem,
    )
    for copy in ghalos:
        copy.start()

    def chunk_rows(k):
        first, count, _ = CHUNKS[k]
        return pl.ds(first * CH, count * CH)

    def shard_rows(k):
        first, count, _ = CHUNKS[k]
        return pl.ds(first * 16, count * 16)

    def block_rows(k, member):
        first, count, _ = CHUNKS[k]
        return pl.ds(pl.multiple_of(first * CH + member * (count * 16), 16), count * 16)

    def pair_copy(k):
        rows = chunk_rows(k)
        return remote(
            local_w.at[1 - core, rows], pair_w.at[rows], pair_ssem.at[0, k], pair_rsem.at[0, k], partner
        )

    def plane_copies(k, back):
        axes = CHUNKS[k][2]
        me = member_of(axes)
        copies = []
        for j in range(1, 16):
            to = (me + j) % 16
            if back:
                source = target = full_w.at[core, block_rows(k, me)]
            else:
                source, target = half_w.at[block_rows(k, to)], plane_w.at[j - 1, shard_rows(k)]
            copies.append(
                remote(
                    source, target, plane_ssem.at[back, k, j], plane_rsem.at[back, k, j],
                    on_plane(axes, to),
                )
            )
        return copies

    def line_copies(k):
        axis = CHUNKS[k][2][2]
        pos = position[axis]
        spot = line_w.at[pos, shard_rows(k)]
        return [
            remote(
                spot, spot, line_ssem.at[k, j], line_rsem.at[k, j], on_axis(axis, (pos + j) % 4)
            )
            for j in range(1, 4)
        ]

    def last_copy(k):
        spot = full_w.at[core, chunk_rows(k)]
        return remote(spot, spot, pair_ssem.at[1, k], pair_rsem.at[1, k], partner)

    def reduce_step(k, step):
        axes = CHUNKS[k][2]
        rows, shard = chunk_rows(k), shard_rows(k)
        if step == 0:
            pair_copy(k).start()
        elif step == 1:
            pair_copy(k).wait_recv()
            both = local_w[core, rows].astype(F32) + pair_w[rows].astype(F32)
            half_w[rows] = both.astype(BF16)
            for copy in plane_copies(k, 0):
                copy.start()
        elif step == 2:
            for copy in plane_copies(k, 0):
                copy.wait_recv()
            total = half_w[block_rows(k, member_of(axes))].astype(F32)
            for j in range(15):
                total = total + plane_w[j, shard].astype(F32)
            line_w[position[axes[2]], shard] = total.astype(BF16)
            for copy in line_copies(k):
                copy.start()
        elif step == 3:
            for copy in line_copies(k):
                copy.wait_recv()
            total = line_w[0, shard].astype(F32)
            for j in range(1, 4):
                total = total + line_w[j, shard].astype(F32)
            full_w[core, block_rows(k, member_of(axes))] = total.astype(BF16)
            for copy in plane_copies(k, 1):
                copy.start()
        elif step == 4:
            for copy in plane_copies(k, 1):
                copy.wait_recv()
            last_copy(k).start()
        else:
            last_copy(k).wait_recv()

    def tap_of(tap, carry):
        a, b = tap // 3, tap % 3
        lhs = trans[b, :, pl.ds(pl.multiple_of(a * COLS, COLS), ROWS * COLS)]
        rhs = grad3[pl.ds(1, ROWS), :, CH : 2 * CH].reshape(ROWS * COLS, CH)
        part = jnp.dot(lhs, rhs, preferred_element_type=F32)
        rows = pl.ds(pl.multiple_of(tap * CH, CH), CH)
        for c in range(2):
            local_w[c, rows, :] = part[:, c * 128 : c * 128 + 128].astype(BF16)
        return carry

    after_taps = [[(0, 0)], [(1, 0), (0, 1)], [(2, 0), (1, 1)], [(3, 0), (2, 1)]]
    for k, (first, count, _) in enumerate(CHUNKS):
        lax.fori_loop(first, first + count, tap_of, 0)
        for chunk, step in after_taps[k]:
            reduce_step(chunk, step)
        if k < 3:
            emb_start(k + 1, emb_finish(k))

    for copy in ghalos:
        copy.wait_recv()

    def grad_shift(row, carry):
        wide = grad3[row, :, CH : 2 * CH].astype(F32)
        near = jnp.where(has_left, ghalo_l[pl.ds(7 + row, 1), :], 0.0)
        far = jnp.where(has_right, ghalo_r[pl.ds(7 + row, 1), :], 0.0)
        low, high = columns_of(wide, near, far)
        grad3[row, :, 0:CH] = high.astype(BF16)
        grad3[row, :, 2 * CH : 3 * CH] = low.astype(BF16)
        return carry

    lax.fori_loop(0, PAD // 2, grad_shift, 0)
    reduce_step(3, 1)
    lax.fori_loop(PAD // 2, PAD, grad_shift, 0)
    for row, present in ((0, has_up), (PAD - 1, has_down)):
        edge = grad3[row].astype(F32)
        grad3[row] = jnp.where(present, edge, 0.0).astype(BF16)

    def back_block(step, carry):
        first = step * CONV_ROWS
        tr = step // (16 // CONV_ROWS)
        total = conv_block(grad3, taps_t, first, True)
        for k in range(CONV_ROWS):
            out_buf[first + k] = (total[k] + spread[tr, k % 2]).astype(BF16)
        return carry

    order = [[(0, 2)], [(1, 2)], [(2, 2), (0, 3)], [(3, 2), (1, 3)]]
    for part in range(4):
        for chunk, step in order[part]:
            reduce_step(chunk, step)
        lax.fori_loop(2 * part, 2 * part + 2, back_block, 0)
    emb_out[...] = emb_finish(3)[0:1, :] * (1.0 / math.sqrt(GY * GX * TILES))
    for step in (3, 4, 5):
        for chunk in range(4):
            if step > 3 or chunk > 1:
                reduce_step(chunk, step)

    for copy in halos + ghalos + tok_copies:
        copy.wait_send()
    for k in range(len(CHUNKS)):
        for copy in [pair_copy(k), last_copy(k)] + line_copies(k):
            copy.wait_send()
        for back in range(2):
            for copy in plane_copies(k, back):
                copy.wait_send()
    for step in range(4):
        for copy in emb_copies(step):
            copy.wait_send()


def finish(emb, grad, conv, emb_out, grad_out, conv_out, wide, sem):
    copies = [
        pltpu.make_async_copy(emb, emb_out, sem.at[0]),
        pltpu.make_async_copy(grad.at[pl.ds(0, 16)], grad_out.at[pl.ds(0, 16)], sem.at[1]),
        pltpu.make_async_copy(grad.at[pl.ds(16, 16)], grad_out.at[pl.ds(16, 16)], sem.at[2]),
    ]
    for copy in copies:
        copy.start()
    for k in range(3):
        rows = pl.ds(k * 3 * CH, 3 * CH)
        for c in range(2):
            wide[rows, c * 128 : c * 128 + 128] = conv[c, rows].astype(F32) * (1.0 / loss_scale)
        copy = pltpu.make_async_copy(wide.at[rows], conv_out.at[rows], sem.at[3 + k])
        copy.start()
        copies.append(copy)
    for copy in copies:
        copy.wait()


def per_device(features, tissue, owner_map, w_conv, w_stride, w_query, w_key, w_value, cotangent):
    whole = pl.BlockSpec(memory_space=pl.ANY)
    scalars = pl.BlockSpec(memory_space=pltpu.SMEM)
    vector = pl.BlockSpec(memory_space=pltpu.VMEM)
    dma = pltpu.SemaphoreType.DMA
    columns = pltpu.VMEM((ROWS, CH), F32)
    column_halo = pltpu.VMEM((ROWS + 16, CH), F32)
    embedding, input_grad, conv_grad = pl.pallas_call(
        kernel,
        out_shape=(
            pltpu.VMEM((1, CH), F32),
            pltpu.VMEM((ROWS, COLS, CH), BF16),
            pltpu.VMEM((2, 9 * CH, 128), BF16),
        ),
        in_specs=[whole, scalars, scalars, whole, whole, whole, whole, whole, vector],
        out_specs=(vector, vector, vector),
        scratch_shapes=[
            pltpu.VMEM((PAD, COLS, CH), BF16),
            pltpu.VMEM((PAD, COLS, 3 * CH), BF16),
            pltpu.VMEM((3, CH, PAD * COLS), BF16),
            pltpu.VMEM((ROWS, COLS, CH), F32),
            pltpu.VMEM((PAD, COLS, 3 * CH), BF16),
            pltpu.VMEM((3, 3 * CH, CH), BF16),
            pltpu.VMEM((3, 3 * CH, CH), BF16),
            pltpu.VMEM((4 * CH, CH), BF16),
            pltpu.VMEM((CH, 3 * CH), F32),
            pltpu.VMEM((3, CH, 3 * CH), BF16),
            pltpu.VMEM((2, COLS, CH), F32),
            pltpu.VMEM((2, 2, COLS, CH), F32),
            pltpu.VMEM((2, 2, COLS, CH), F32),
            columns, columns, column_halo, column_halo,
            columns, columns, column_halo, column_halo,
            columns, columns,
            pltpu.VMEM((GX, TILES, CH + 128), BF16),
            pltpu.VMEM((TILES, 128), F32),
            pltpu.VMEM((TILES, 4 * CH), F32),
            pltpu.VMEM((2, 9 * CH, 128), BF16),
            pltpu.VMEM((9 * CH, 128), BF16),
            pltpu.VMEM((9 * CH, 128), BF16),
            pltpu.VMEM((15, 144, 128), BF16),
            pltpu.VMEM((4, 144, 128), BF16),
            pltpu.VMEM((4, 4, 8, CH), F32),
            dma((6,)), dma((8,)), dma((8,)), dma((8,)), dma((8,)),
            dma((GX,)), dma((GX,)),
            dma((2, 4, 16)), dma((2, 4, 16)), dma((4, 4)), dma((4, 4)), dma((2, 4)), dma((2, 4)),
            dma((4, 4)), dma((4, 4)),
        ],
        compiler_params=pltpu.CompilerParams(
            collective_id=0, has_side_effects=True, vmem_limit_bytes=56 * 1024 * 1024
        ),
    )(
        features, tissue, owner_map.reshape(1, TILES), w_conv.reshape(3, 3 * CH, CH),
        w_stride.reshape(4 * CH, CH), w_query, w_key, w_value, cotangent.reshape(1, CH),
    )
    embedding, input_grad, conv_grad = pl.pallas_call(
        finish,
        out_shape=(
            jax.ShapeDtypeStruct((1, CH), F32),
            jax.ShapeDtypeStruct((ROWS, COLS, CH), BF16),
            jax.ShapeDtypeStruct((9 * CH, CH), F32),
        ),
        in_specs=[vector, vector, vector],
        out_specs=(whole, whole, whole),
        scratch_shapes=[pltpu.VMEM((9 * CH, CH), F32), dma((6,))],
    )(embedding, input_grad, conv_grad)
    return embedding.reshape(CH), input_grad, conv_grad.reshape(9, CH, CH)


def solution(mesh):
    in_specs = (
        P("gy", "gx", None), P("gy", "gx"), P("gy", "gx", None, None),
        P(), P(), P(), P(), P(), P(),
    )
    out_specs = (P(), P("gy", "gx", None), P())
    return jax.shard_map(
        per_device, mesh=mesh, in_specs=in_specs, out_specs=out_specs, check_vma=False
    )
```

```python
import math

import jax
import jax.numpy as jnp
from jax import lax
from jax.experimental import pallas as pl
from jax.experimental.pallas import tpu as pltpu
from jax.sharding import PartitionSpec as P

MESH = pl.DeviceIdType.MESH
F32, BF16 = jnp.float32, jnp.bfloat16
HEADS = 4
attention_bias = -1.0
loss_scale = 512.0

GY, GX = 8, 16
ROWS, COLS, CH = 32, 128, 256
PAD = ROWS + 2
TILES = 16
CONV_ROWS = 4
CHUNKS = ((0, 3, "xyz"), (3, 3, "yzx"), (6, 2, "zxy"), (8, 1, "xyz"))
BARRIER_SIGNALS = 23 + 15 * 3


def exact_dot(a, b, a_dim=1, b_dim=0):
    return lax.dot_general(
        a, b, (((a_dim,), (b_dim,)), ((), ())),
        precision=lax.Precision.HIGHEST, preferred_element_type=F32,
    )


def half_dot(a, b, a_dim=1, b_dim=0):
    return lax.dot_general(
        a.astype(BF16), b.astype(BF16), (((a_dim,), (b_dim,)), ((), ())),
        preferred_element_type=F32,
    )


def three_parts(value):
    high = value.astype(BF16)
    rest = value - high.astype(F32)
    middle = rest.astype(BF16)
    low = (rest - middle.astype(F32)).astype(BF16)
    return high, middle, low


def iota(shape, dim):
    return lax.broadcasted_iota(jnp.int32, shape, dim)


def kernel(
    feat, tissue, owner, w_conv, w_stride, w_query, w_key, w_value, cot,
    emb_out, out_buf, full_w,
    field, cols3, trans, slope, grad3, taps, taps_t, stride_w, proj, parts3, mask,
    sums, spread, send_l, send_r, halo_l, halo_r, gsend_l, gsend_r, ghalo_l, ghalo_r,
    edge_l, edge_r, tok_buf, code_buf, code_rows, tissue_s, owner_s, cot_v, stride_back,
    local_w, pair_w, half_w, plane_w, line_w, emb_buf,
    load_sem, halo_ssem, halo_rsem, ghalo_ssem, ghalo_rsem, tok_ssem, tok_rsem,
    plane_ssem, plane_rsem, line_ssem, line_rsem, pair_ssem, pair_rsem, emb_ssem, emb_rsem,
):
    g, h = lax.axis_index("gy"), lax.axis_index("gx")
    x_hi, y = lax.div(g, 4), lax.rem(g, 4)
    z, x_lo, core = lax.div(h, 4), lax.rem(lax.div(h, 2), 2), lax.rem(h, 2)
    position = {"x": 2 * x_hi + x_lo, "y": y, "z": z}
    partner = (g, h + 1 - 2 * core)

    around = {axis: [lax.rem(position[axis] + j, 4) for j in range(4)] for axis in "xyz"}
    share_g = {
        "x": [lax.div(pos, 2) * 4 for pos in around["x"]],
        "y": around["y"],
        "z": [0] * 4,
    }
    share_h = {
        "x": [lax.rem(pos, 2) * 2 for pos in around["x"]],
        "y": [0] * 4,
        "z": [pos * 4 for pos in around["z"]],
    }

    def device_at(**steps):
        steps = {axis: steps.get(axis, 0) for axis in "xyz"}
        return (
            sum(share_g[axis][steps[axis]] for axis in "xy"),
            sum(share_h[axis][steps[axis]] for axis in "xz") + core,
        )

    def plane_steps():
        return [(j, k) for j in range(4) for k in range(4) if (j, k) != (0, 0)]

    def on_plane(axes, j, k):
        return device_at(**{axes[0]: j, axes[1]: k})

    def member_of(axes, j=0, k=0):
        return around[axes[0]][j] * 4 + around[axes[1]][k]

    row_peers = [lax.rem(h + j, GX) for j in range(GX)]

    up, down = lax.rem(g + GY - 1, GY), lax.rem(g + 1, GY)
    left, right = row_peers[GX - 1], row_peers[1]

    def remote(src, dst, ssem, rsem, device):
        return pltpu.make_async_remote_copy(
            src_ref=src, dst_ref=dst, send_sem=ssem, recv_sem=rsem,
            device_id=device, device_id_type=MESH,
        )

    loads = [
        pltpu.make_async_copy(feat, field.at[pl.ds(1, ROWS)], load_sem.at[0]),
        pltpu.make_async_copy(w_conv, taps, load_sem.at[1]),
        pltpu.make_async_copy(w_stride, stride_w, load_sem.at[2]),
        pltpu.make_async_copy(w_query, proj.at[:, pl.ds(0, CH)], load_sem.at[3]),
        pltpu.make_async_copy(w_key, proj.at[:, pl.ds(CH, CH)], load_sem.at[4]),
        pltpu.make_async_copy(w_value, proj.at[:, pl.ds(2 * CH, CH)], load_sem.at[5]),
    ]
    small = [
        pltpu.make_async_copy(tissue, tissue_s, load_sem.at[6]),
        pltpu.make_async_copy(owner, owner_s, load_sem.at[7]),
        pltpu.make_async_copy(cot, cot_v, load_sem.at[8]),
    ]
    loads[0].start()
    barrier = pltpu.get_barrier_semaphore()
    peers = [
        (up, h), (down, h), (g, left), (g, right),
        (up, left), (up, right), (down, left), (down, right),
    ]
    peers += [(g, peer) for peer in row_peers[1:]]
    for axes in ("xy", "yz", "zx"):
        peers += [on_plane(axes, j, k) for j, k in plane_steps()]
    for device in peers:
        pl.semaphore_signal(barrier, inc=1, device_id=device, device_id_type=MESH)

    for copy in loads[1:] + small:
        copy.start()
    for copy in small:
        copy.wait()
    for tile in range(TILES):
        tr, tc = tile // 8, tile % 8
        flag = tissue_s[tr, tc].astype(F32)
        code = flag * (owner_s[0, tile].astype(F32) + 1.0)
        mask[tr, tc * 16 : tc * 16 + 16, :] = jnp.zeros((16, CH), F32) + flag
        code_rows[tile : tile + 1, :] = jnp.zeros((1, 128), F32) + code
    code_buf[h] = code_rows[...].astype(BF16)
    sums[...] = jnp.zeros_like(sums)
    loads[0].wait()

    def edge_columns(row, carry):
        send_l[pl.ds(row, 1), :] = field[row + 1, 0:16, :].astype(F32)[0:1, :]
        send_r[pl.ds(row, 1), :] = field[row + 1, COLS - 16 : COLS, :].astype(F32)[15:16, :]
        return carry

    lax.fori_loop(0, ROWS, edge_columns, 0)
    def halo_copies(first_row, last_row, low_row, high_row, col_l, col_r, got_l, got_r, ss, rs):
        top, bottom = pl.ds(0, 8), pl.ds(ROWS - 8, 8)
        return [
            remote(first_row, high_row, ss.at[0], rs.at[0], (up, h)),
            remote(last_row, low_row, ss.at[1], rs.at[1], (down, h)),
            remote(col_l, got_r.at[pl.ds(8, ROWS)], ss.at[2], rs.at[2], (g, left)),
            remote(col_r, got_l.at[pl.ds(8, ROWS)], ss.at[3], rs.at[3], (g, right)),
            remote(col_r.at[bottom], got_l.at[pl.ds(0, 8)], ss.at[4], rs.at[4], (down, right)),
            remote(col_r.at[top], got_l.at[pl.ds(40, 8)], ss.at[5], rs.at[5], (up, right)),
            remote(col_l.at[bottom], got_r.at[pl.ds(0, 8)], ss.at[6], rs.at[6], (down, left)),
            remote(col_l.at[top], got_r.at[pl.ds(40, 8)], ss.at[7], rs.at[7], (up, left)),
        ]

    has_left, has_right = h > 0, h < GX - 1
    has_up, has_down = g > 0, g < GY - 1
    to_send = (
        has_up, has_down, has_left, has_right,
        has_down & has_right, has_up & has_right, has_down & has_left, has_up & has_left,
    )
    to_receive = (
        has_down, has_up, has_right, has_left,
        has_up & has_left, has_down & has_left, has_up & has_right, has_down & has_right,
    )

    def start_halos(copies):
        for copy, there in zip(copies, to_send):
            pl.when(there)(copy.start)

    def receive_halos(copies):
        for copy, there in zip(copies, to_receive):
            pl.when(there)(copy.wait_recv)

    def drain_halos(copies):
        for copy, there in zip(copies, to_send):
            pl.when(there)(copy.wait_send)


    def columns_of(center, before, after):
        spot = iota(center.shape, 0)
        low = jnp.where(spot == 0, before, pltpu.roll(center, 1, 0))
        high = jnp.where(spot == COLS - 1, after, pltpu.roll(center, COLS - 1, 0))
        return low, high

    def shift_row(row, carry):
        center = field[row]
        low, high = columns_of(center.astype(F32), 0.0, 0.0)
        cols3[row, :, 0:CH] = low.astype(BF16)
        cols3[row, :, CH : 2 * CH] = center
        cols3[row, :, 2 * CH : 3 * CH] = high.astype(BF16)
        return carry

    lax.fori_loop(1, ROWS + 1, shift_row, 0)
    loads[1].wait()

    def conv_block(source, weights, first, flipped):
        total = None
        for a in range(3):
            start = first + (2 - a if flipped else a)
            block = source[pl.ds(start, CONV_ROWS)].reshape(CONV_ROWS * COLS, 3 * CH)
            part = jnp.dot(block, weights[a], preferred_element_type=F32)
            total = part if total is None else total + part
        return total.reshape(CONV_ROWS, COLS, CH)

    def forward_block(step, carry):
        first = step * CONV_ROWS
        tr = step // (16 // CONV_ROWS)
        pre = conv_block(cols3, taps, first, False)
        for k in range(CONV_ROWS):
            edge_l[pl.ds(first + k, 1), :] = pre[k, 0:1, :]
            edge_r[pl.ds(first + k, 1), :] = pre[k, COLS - 1 : COLS, :]
        gate = jax.nn.sigmoid(pre)
        slope[pl.ds(first, CONV_ROWS)] = gate * (1.0 + pre * (1.0 - gate))
        own = cols3[pl.ds(first + 1, CONV_ROWS), :, CH : 2 * CH].astype(F32)
        summed = (own + pre * gate * mask[tr][None]).astype(BF16).astype(F32)
        for a in range(2):
            total = sums[tr, a]
            for k in range(a, CONV_ROWS, 2):
                total = total + summed[k]
            sums[tr, a] = total
        return carry

    lax.fori_loop(1, 3, forward_block, 0)
    pl.semaphore_wait(barrier, BARRIER_SIGNALS)
    code_copies = [
        remote(
            code_buf.at[h], code_buf.at[h], tok_ssem.at[0, j], tok_rsem.at[0, j], (g, row_peers[j])
        )
        for j in range(1, GX)
    ]
    halos = halo_copies(
        field.at[1], field.at[ROWS], field.at[0], field.at[PAD - 1],
        send_l, send_r, halo_l, halo_r, halo_ssem, halo_rsem,
    )
    start_halos(halos)
    for copy in code_copies:
        copy.start()
    lax.fori_loop(3, 7, forward_block, 0)

    def transpose_middle(row, carry):
        lanes = pl.ds(pl.multiple_of(row * COLS, COLS), COLS)
        trans[1, :, lanes] = cols3[row, :, CH : 2 * CH].T
        return carry

    lax.fori_loop(1, ROWS + 1, transpose_middle, 0)
    for a in range(3):
        for b in range(3):
            taps_t[a, b * CH : (b + 1) * CH, :] = taps[a, b * CH : (b + 1) * CH, :].T
    for k in range(3, 6):
        loads[k].wait()
    for k, part in enumerate(three_parts(proj[...])):
        parts3[k] = part
    receive_halos(halos)

    def patch_row(row, carry):
        near = halo_l[pl.ds(7 + row, 1), :]
        far = halo_r[pl.ds(7 + row, 1), :]
        near = jnp.where(has_left, near, 0.0)
        far = jnp.where(has_right, far, 0.0)
        head = cols3[row, 0:16, 0:CH].astype(F32)
        tail = cols3[row, COLS - 16 : COLS, 2 * CH : 3 * CH].astype(F32)
        spot = iota(head.shape, 0)
        cols3[row, 0:16, 0:CH] = jnp.where(spot == 0, near, head).astype(BF16)
        cols3[row, COLS - 16 : COLS, 2 * CH : 3 * CH] = jnp.where(spot == 15, far, tail).astype(BF16)
        return carry

    lax.fori_loop(1, ROWS + 1, patch_row, 0)
    for row, present in ((0, has_up), (PAD - 1, has_down)):
        wide = jnp.where(present, field[row].astype(F32), 0.0)
        near = jnp.where(has_left & present, halo_l[7 + row : 8 + row, :], 0.0)
        far = jnp.where(has_right & present, halo_r[7 + row : 8 + row, :], 0.0)
        low, high = columns_of(wide, near, far)
        cols3[row, :, 0:CH] = low.astype(BF16)
        cols3[row, :, CH : 2 * CH] = wide.astype(BF16)
        cols3[row, :, 2 * CH : 3 * CH] = high.astype(BF16)

    lax.fori_loop(0, 2, lambda i, carry: forward_block(i * 7, carry), 0)
    row_of = iota((ROWS, CH), 0)
    inner_row = (row_of >= CONV_ROWS) & (row_of < ROWS - CONV_ROWS)

    def fix_edge(got, present, edge, own, tap_at, col):
        terms = [jnp.where(present, got[7 + a : 7 + a + ROWS, :], 0.0).astype(BF16) for a in range(3)]
        pre = edge[...]
        flag = jnp.where(row_of < 16, mask[0, col : col + 1, :], mask[1, col : col + 1, :])
        old = (own[...] + pre * jax.nn.sigmoid(pre) * flag).astype(BF16).astype(F32)
        for a in range(3):
            pre = pre + jnp.dot(
                terms[a], taps[a, tap_at * CH : (tap_at + 1) * CH, :], preferred_element_type=F32
            )
        gate = jax.nn.sigmoid(pre)
        new = (own[...] + pre * gate * flag).astype(BF16).astype(F32)
        slant = gate * (1.0 + pre * (1.0 - gate))
        change = jnp.where(inner_row, new - old, 0.0)
        for tr in range(2):
            for a in range(2):
                part = jnp.where((row_of // 16 == tr) & (row_of % 2 == a), change, 0.0)
                sums[tr, a, col : col + 1, :] = sums[tr, a, col : col + 1, :] + jnp.sum(
                    part, axis=0, keepdims=True
                )
        for row in range(CONV_ROWS, ROWS - CONV_ROWS):
            slope[row, col : col + 1, :] = slant[row : row + 1, :]

    fix_edge(halo_l, has_left, edge_l, send_l, 0, 0)
    fix_edge(halo_r, has_right, edge_r, send_r, 2, COLS - 1)


    lane_col, row_id = iota((16, COLS), 1), iota((16, COLS), 0)
    select = ((lane_col // 16 == row_id % 8) & (lane_col % 2 == row_id // 8)).astype(BF16)
    gathered = jnp.concatenate([sums[tr, a] for tr in range(2) for a in range(2)], axis=1)
    parts = three_parts(gathered)
    cell_sums = sum(jnp.dot(select, part, preferred_element_type=F32) for part in parts)
    loads[2].wait()
    pooled = jnp.zeros((TILES, CH), F32)
    for a in range(2):
        for b in range(2):
            tap = 2 * a + b
            lhs = jnp.concatenate(
                [cell_sums[b * 8 : b * 8 + 8, (2 * tr + a) * CH : (2 * tr + a + 1) * CH] for tr in range(2)],
                axis=0,
            )
            rhs = stride_w[tap * CH : (tap + 1) * CH, :]
            pooled = pooled + sum(
                jnp.dot(part, rhs, preferred_element_type=F32) for part in three_parts(lhs)
            )
    pooled = pooled * (1.0 / 64.0)
    inverse = lax.rsqrt(jnp.mean(pooled * pooled, axis=-1, keepdims=True) + 1e-05)
    normed = (pooled * inverse).astype(BF16)

    code = code_rows[...]
    tok_buf[h] = normed
    tok_copies = [
        remote(
            tok_buf.at[h], tok_buf.at[h], tok_ssem.at[1, j], tok_rsem.at[1, j], (g, row_peers[j])
        )
        for j in range(1, GX)
    ]
    for copy in tok_copies:
        copy.start()

    head_of = iota((1, CH), 1) // (CH // HEADS)
    heads = [(head_of == k).astype(F32) for k in range(HEADS)]

    def by_head(rows):
        return jnp.concatenate([rows * m for m in heads], axis=0)

    def join_heads(rows):
        return sum(rows[k * TILES : (k + 1) * TILES, :] * heads[k] for k in range(HEADS))

    own_qkv = sum(jnp.dot(normed, parts3[k], preferred_element_type=F32) for k in range(3))
    own_value = own_qkv[:, 2 * CH : 3 * CH]
    query_by_head, key_by_head = by_head(own_qkv[:, 0:CH]), by_head(own_qkv[:, CH : 2 * CH])
    seed = cot_v[...] * (loss_scale / math.sqrt(GY * GX * TILES))
    seed_by_head = by_head(jnp.broadcast_to(seed, (8, CH)))
    value_seed = exact_dot(seed_by_head, proj[:, 2 * CH : 3 * CH], 1, 1)
    own_value_seed = jnp.sum(by_head(own_value * seed), axis=1, keepdims=True)

    def transpose_row(row, carry):
        lanes = pl.ds(pl.multiple_of(row * COLS, COLS), COLS)
        for b in (0, 2):
            trans[b, :, lanes] = cols3[row, :, b * CH : (b + 1) * CH].T
        return carry

    lax.fori_loop(0, PAD, transpose_row, 0)
    for row in (0, PAD - 1):
        trans[1, :, row * COLS : (row + 1) * COLS] = cols3[row, :, CH : 2 * CH].T
    for copy in tok_copies:
        copy.wait_recv()

    everyone = tok_buf[...].reshape(GX * TILES, CH)
    for copy in code_copies:
        copy.wait_recv()
    codes = code_buf[...].reshape(GX * TILES, 128)
    all_qk = sum(
        jnp.dot(everyone, parts3[k, :, 0 : 2 * CH], preferred_element_type=F32) for k in range(3)
    )
    all_query, all_key = all_qk[:, 0:CH], all_qk[:, CH : 2 * CH]
    lane0 = (iota((TILES, 128), 1) == 0).astype(F32)
    codes_across = half_dot(lane0, codes, 1, 1)
    allowed = ((codes_across == code[:, 0:1]) & (codes_across > 0.5)).astype(F32)
    allowed = jnp.concatenate([allowed] * HEADS, axis=0)
    scale = 1.0 / math.sqrt(CH // HEADS)
    as_query = jax.nn.sigmoid(exact_dot(query_by_head, all_key, 1, 1) * scale + attention_bias)
    as_key = jax.nn.sigmoid(exact_dot(key_by_head, all_query, 1, 1) * scale + attention_bias)
    weight_sums = jnp.sum(as_key * allowed, axis=1, keepdims=True)
    head_sums = join_heads(jnp.broadcast_to(weight_sums, (HEADS * TILES, CH)))
    partial = jnp.sum(head_sums * own_value, axis=0, keepdims=True)
    d_value = head_sums * seed
    across = sum(half_dot(part, everyone, 1, 1) for part in three_parts(value_seed))
    across = jnp.concatenate([across[8 * k : 8 * k + 8, :] for k in range(HEADS) for _ in range(2)], axis=0)
    d_as_query = across * allowed * as_query * (1.0 - as_query) * scale
    d_as_key = own_value_seed * allowed * as_key * (1.0 - as_key) * scale
    d_query = join_heads(exact_dot(d_as_query, all_key))
    d_key = join_heads(exact_dot(d_as_key, all_query))
    d_qkv = three_parts(jnp.concatenate([d_query, d_key, d_value], axis=1))
    d_tokens = jnp.zeros((TILES, CH), F32)
    for k in range(3):
        lhs = jnp.concatenate(d_qkv[: 3 - k], axis=0)
        product = half_dot(lhs, parts3[k], 1, 1)
        for part in range(3 - k):
            d_tokens = d_tokens + product[part * TILES : (part + 1) * TILES, :]
    token_grad = d_tokens.astype(BF16).astype(F32)

    emb_steps = [("core", 2, core)] + [(axis, 4, position[axis]) for axis in ("x", "y", "z")]

    def emb_copies(step):
        axis, count, pos = emb_steps[step]
        copies = []
        for j in range(1, count):
            device = partner if axis == "core" else device_at(**{axis: j})
            spot = emb_buf.at[step, pos]
            copies.append(
                remote(spot, spot, emb_ssem.at[step, j], emb_rsem.at[step, j], device)
            )
        return copies

    def emb_start(step, term):
        emb_buf[step, emb_steps[step][2]] = term
        for copy in emb_copies(step):
            copy.start()

    def emb_finish(step):
        for copy in emb_copies(step):
            copy.wait_recv()
        total = emb_buf[step, 0]
        for k in range(1, emb_steps[step][1]):
            total = total + emb_buf[step, k]
        return total

    emb_start(0, jnp.broadcast_to(partial, (8, CH)))

    inner = jnp.mean(token_grad * pooled, axis=-1, keepdims=True)
    pooled_grad = token_grad * inverse - pooled * (inverse * inverse * inverse * inner)
    cell_grad = (pooled_grad * (1.0 / 64.0)).astype(BF16)
    stride_back[...] = half_dot(cell_grad, stride_w[...], 1, 1)
    odd = (iota((16, CH), 0) % 2) == 1
    for tile in range(TILES):
        tr, tc = tile // 8, tile % 8
        for a in range(2):
            even_row = stride_back[tile : tile + 1, (2 * a) * CH : (2 * a + 1) * CH]
            odd_row = stride_back[tile : tile + 1, (2 * a + 1) * CH : (2 * a + 2) * CH]
            spread[tr, a, tc * 16 : tc * 16 + 16, :] = jnp.where(odd, odd_row, even_row)

    def pre_grad_row(row, carry):
        tr = row // 16
        value = (spread[tr, row % 2] * mask[tr] * slope[row]).astype(BF16)
        grad3[row + 1, :, CH : 2 * CH] = value
        wide = value.astype(F32)
        gsend_l[pl.ds(row, 1), :] = wide[0:1, :]
        gsend_r[pl.ds(row, 1), :] = wide[COLS - 1 : COLS, :]
        return carry

    lax.fori_loop(0, ROWS, pre_grad_row, 0)
    middle = pl.ds(CH, CH)
    ghalos = halo_copies(
        grad3.at[1, :, middle], grad3.at[ROWS, :, middle],
        grad3.at[0, :, middle], grad3.at[PAD - 1, :, middle],
        gsend_l, gsend_r, ghalo_l, ghalo_r, ghalo_ssem, ghalo_rsem,
    )
    start_halos(ghalos)

    def chunk_rows(k):
        first, count, _ = CHUNKS[k]
        return pl.ds(first * CH, count * CH)

    def shard_rows(k):
        first, count, _ = CHUNKS[k]
        return pl.ds(first * 16, count * 16)

    def block_rows(k, member):
        first, count, _ = CHUNKS[k]
        return pl.ds(pl.multiple_of(first * CH + member * (count * 16), 16), count * 16)

    def pair_copy(k):
        rows = chunk_rows(k)
        return remote(
            local_w.at[1 - core, rows], pair_w.at[rows], pair_ssem.at[0, k], pair_rsem.at[0, k], partner
        )

    def plane_copies(k, back):
        axes = CHUNKS[k][2]
        copies = []
        for n, (j, i) in enumerate(plane_steps()):
            if back:
                source = target = full_w.at[core, block_rows(k, member_of(axes))]
            else:
                source = half_w.at[block_rows(k, member_of(axes, j, i))]
                target = plane_w.at[n, shard_rows(k)]
            copies.append(
                remote(
                    source, target, plane_ssem.at[back, k, n], plane_rsem.at[back, k, n],
                    on_plane(axes, j, i),
                )
            )
        return copies

    def line_copies(k):
        axis = CHUNKS[k][2][2]
        pos = position[axis]
        spot = line_w.at[pos, shard_rows(k)]
        return [
            remote(
                spot, spot, line_ssem.at[k, j], line_rsem.at[k, j], device_at(**{axis: j})
            )
            for j in range(1, 4)
        ]

    def last_copy(k):
        spot = full_w.at[core, chunk_rows(k)]
        return remote(spot, spot, pair_ssem.at[1, k], pair_rsem.at[1, k], partner)

    def reduce_step(k, step):
        axes = CHUNKS[k][2]
        rows, shard = chunk_rows(k), shard_rows(k)
        if step == 0:
            pair_copy(k).start()
        elif step == 1:
            pair_copy(k).wait_recv()
            both = local_w[core, rows].astype(F32) + pair_w[rows].astype(F32)
            half_w[rows] = both.astype(BF16)
            for copy in plane_copies(k, 0):
                copy.start()
        elif step == 2:
            for copy in plane_copies(k, 0):
                copy.wait_recv()
            total = half_w[block_rows(k, member_of(axes))].astype(F32)
            for j in range(15):
                total = total + plane_w[j, shard].astype(F32)
            line_w[position[axes[2]], shard] = total.astype(BF16)
            for copy in line_copies(k):
                copy.start()
        elif step == 3:
            for copy in line_copies(k):
                copy.wait_recv()
            total = line_w[0, shard].astype(F32)
            for j in range(1, 4):
                total = total + line_w[j, shard].astype(F32)
            full_w[core, block_rows(k, member_of(axes))] = total.astype(BF16)
            for copy in plane_copies(k, 1):
                copy.start()
        elif step == 4:
            for copy in plane_copies(k, 1):
                copy.wait_recv()
            last_copy(k).start()
        else:
            last_copy(k).wait_recv()

    def tap_of(tap, carry):
        a, b = tap // 3, tap % 3
        lhs = trans[b, :, pl.ds(pl.multiple_of(a * COLS, COLS), ROWS * COLS)]
        rhs = grad3[pl.ds(1, ROWS), :, CH : 2 * CH].reshape(ROWS * COLS, CH)
        part = jnp.dot(lhs, rhs, preferred_element_type=F32)
        rows = pl.ds(pl.multiple_of(tap * CH, CH), CH)
        for c in range(2):
            local_w[c, rows, :] = part[:, c * 128 : c * 128 + 128].astype(BF16)
        return carry

    after_taps = [[(0, 0)], [(1, 0), (0, 1)], [(2, 0), (1, 1)], [(3, 0), (2, 1)]]
    for k, (first, count, _) in enumerate(CHUNKS):
        lax.fori_loop(first, first + count, tap_of, 0)
        for chunk, step in after_taps[k]:
            reduce_step(chunk, step)
        if k < 3:
            emb_start(k + 1, emb_finish(k))

    receive_halos(ghalos)

    def grad_shift(row, carry):
        wide = grad3[row, :, CH : 2 * CH].astype(F32)
        near = jnp.where(has_left, ghalo_l[pl.ds(7 + row, 1), :], 0.0)
        far = jnp.where(has_right, ghalo_r[pl.ds(7 + row, 1), :], 0.0)
        low, high = columns_of(wide, near, far)
        grad3[row, :, 0:CH] = high.astype(BF16)
        grad3[row, :, 2 * CH : 3 * CH] = low.astype(BF16)
        return carry

    lax.fori_loop(0, PAD // 2, grad_shift, 0)
    reduce_step(3, 1)
    lax.fori_loop(PAD // 2, PAD, grad_shift, 0)
    for row, present in ((0, has_up), (PAD - 1, has_down)):
        edge = grad3[row].astype(F32)
        grad3[row] = jnp.where(present, edge, 0.0).astype(BF16)

    def back_block(step, carry):
        first = step * CONV_ROWS
        tr = step // (16 // CONV_ROWS)
        total = conv_block(grad3, taps_t, first, True)
        for k in range(CONV_ROWS):
            out_buf[first + k] = (total[k] + spread[tr, k % 2]).astype(BF16)
        return carry

    order = [[(0, 2)], [(1, 2)], [(2, 2), (0, 3)], [(3, 2), (1, 3)]]
    for part in range(4):
        for chunk, step in order[part]:
            reduce_step(chunk, step)
        lax.fori_loop(2 * part, 2 * part + 2, back_block, 0)
    emb_out[...] = emb_finish(3)[0:1, :] * (1.0 / math.sqrt(GY * GX * TILES))
    for step in (3, 4, 5):
        for chunk in range(4):
            if step > 3 or chunk > 1:
                reduce_step(chunk, step)

    drain_halos(halos)
    drain_halos(ghalos)
    for copy in code_copies + tok_copies:
        copy.wait_send()
    for k in range(len(CHUNKS)):
        for copy in [pair_copy(k), last_copy(k)] + line_copies(k):
            copy.wait_send()
        for back in range(2):
            for copy in plane_copies(k, back):
                copy.wait_send()
    for step in range(4):
        for copy in emb_copies(step):
            copy.wait_send()


def finish(emb, grad, conv, emb_out, grad_out, conv_out, wide, sem):
    copies = [
        pltpu.make_async_copy(emb, emb_out, sem.at[0]),
        pltpu.make_async_copy(grad.at[pl.ds(0, 16)], grad_out.at[pl.ds(0, 16)], sem.at[1]),
        pltpu.make_async_copy(grad.at[pl.ds(16, 16)], grad_out.at[pl.ds(16, 16)], sem.at[2]),
    ]
    for copy in copies:
        copy.start()
    for k in range(3):
        rows = pl.ds(k * 3 * CH, 3 * CH)
        for c in range(2):
            wide[rows, c * 128 : c * 128 + 128] = conv[c, rows].astype(F32) * (1.0 / loss_scale)
        copy = pltpu.make_async_copy(wide.at[rows], conv_out.at[rows], sem.at[3 + k])
        copy.start()
        copies.append(copy)
    for copy in copies:
        copy.wait()


def per_device(features, tissue, owner_map, w_conv, w_stride, w_query, w_key, w_value, cotangent):
    whole = pl.BlockSpec(memory_space=pl.ANY)
    vector = pl.BlockSpec(memory_space=pltpu.VMEM)
    dma = pltpu.SemaphoreType.DMA
    columns = pltpu.VMEM((ROWS, CH), F32)
    column_halo = pltpu.VMEM((ROWS + 16, CH), F32)
    embedding, input_grad, conv_grad = pl.pallas_call(
        kernel,
        out_shape=(
            pltpu.VMEM((1, CH), F32),
            pltpu.VMEM((ROWS, COLS, CH), BF16),
            pltpu.VMEM((2, 9 * CH, 128), BF16),
        ),
        in_specs=[whole] * 9,
        out_specs=(vector, vector, vector),
        scratch_shapes=[
            pltpu.VMEM((PAD, COLS, CH), BF16),
            pltpu.VMEM((PAD, COLS, 3 * CH), BF16),
            pltpu.VMEM((3, CH, PAD * COLS), BF16),
            pltpu.VMEM((ROWS, COLS, CH), F32),
            pltpu.VMEM((PAD, COLS, 3 * CH), BF16),
            pltpu.VMEM((3, 3 * CH, CH), BF16),
            pltpu.VMEM((3, 3 * CH, CH), BF16),
            pltpu.VMEM((4 * CH, CH), BF16),
            pltpu.VMEM((CH, 3 * CH), F32),
            pltpu.VMEM((3, CH, 3 * CH), BF16),
            pltpu.VMEM((2, COLS, CH), F32),
            pltpu.VMEM((2, 2, COLS, CH), F32),
            pltpu.VMEM((2, 2, COLS, CH), F32),
            columns, columns, column_halo, column_halo,
            columns, columns, column_halo, column_halo,
            columns, columns,
            pltpu.VMEM((GX, TILES, CH), BF16),
            pltpu.VMEM((GX, TILES, 128), BF16),
            pltpu.VMEM((TILES, 128), F32),
            pltpu.SMEM((2, 8), jnp.int32),
            pltpu.SMEM((1, TILES), jnp.int32),
            pltpu.VMEM((1, CH), F32),
            pltpu.VMEM((TILES, 4 * CH), F32),
            pltpu.VMEM((2, 9 * CH, 128), BF16),
            pltpu.VMEM((9 * CH, 128), BF16),
            pltpu.VMEM((9 * CH, 128), BF16),
            pltpu.VMEM((15, 144, 128), BF16),
            pltpu.VMEM((4, 144, 128), BF16),
            pltpu.VMEM((4, 4, 8, CH), F32),
            dma((9,)), dma((8,)), dma((8,)), dma((8,)), dma((8,)),
            dma((2, GX)), dma((2, GX)),
            dma((2, 4, 16)), dma((2, 4, 16)), dma((4, 4)), dma((4, 4)), dma((2, 4)), dma((2, 4)),
            dma((4, 4)), dma((4, 4)),
        ],
        compiler_params=pltpu.CompilerParams(
            collective_id=0, has_side_effects=True, vmem_limit_bytes=56 * 1024 * 1024
        ),
    )(
        features, tissue, owner_map.reshape(1, TILES), w_conv.reshape(3, 3 * CH, CH),
        w_stride.reshape(4 * CH, CH), w_query, w_key, w_value, cotangent.reshape(1, CH),
    )
    embedding, input_grad, conv_grad = pl.pallas_call(
        finish,
        out_shape=(
            jax.ShapeDtypeStruct((1, CH), F32),
            jax.ShapeDtypeStruct((ROWS, COLS, CH), BF16),
            jax.ShapeDtypeStruct((9 * CH, CH), F32),
        ),
        in_specs=[vector, vector, vector],
        out_specs=(whole, whole, whole),
        scratch_shapes=[pltpu.VMEM((9 * CH, CH), F32), dma((6,))],
    )(*(pltpu.with_memory_space_constraint(x, pltpu.VMEM) for x in (embedding, input_grad, conv_grad)))
    return embedding.reshape(CH), input_grad, conv_grad.reshape(9, CH, CH)


def solution(mesh):
    in_specs = (
        P("gy", "gx", None), P("gy", "gx"), P("gy", "gx", None, None),
        P(), P(), P(), P(), P(), P(),
    )
    out_specs = (P(), P("gy", "gx", None), P())
    return jax.shard_map(
        per_device, mesh=mesh, in_specs=in_specs, out_specs=out_specs, check_vma=False
    )
```

```python
import math

import jax
import jax.numpy as jnp
from jax import lax
from jax.experimental import pallas as pl
from jax.experimental.pallas import tpu as pltpu
from jax.sharding import PartitionSpec as P

MESH = pl.DeviceIdType.MESH
F32, BF16 = jnp.float32, jnp.bfloat16
HEADS = 4
attention_bias = -1.0
loss_scale = 512.0

GY, GX = 8, 16
ROWS, COLS, CH = 32, 128, 256
PAD = ROWS + 2
TILES = 16
CONV_ROWS = 4
CHUNKS = ((0, 3, "xyz"), (3, 3, "yzx"), (6, 3, "zxy"))
BARRIER_SIGNALS = 23 + 15 * 3


def exact_dot(a, b, a_dim=1, b_dim=0):
    return lax.dot_general(
        a, b, (((a_dim,), (b_dim,)), ((), ())),
        precision=lax.Precision.HIGHEST, preferred_element_type=F32,
    )


def close_dot(a, b, a_dim=1, b_dim=0):
    (a_high, a_low, _), (b_high, b_low, _) = three_parts(a), three_parts(b)
    rows = a.shape[0]
    both = half_dot(jnp.concatenate([a_high, a_low], axis=0), b_high, a_dim, b_dim)
    return both[:rows] + both[rows:] + half_dot(a_high, b_low, a_dim, b_dim)


def half_dot(a, b, a_dim=1, b_dim=0):
    return lax.dot_general(
        a.astype(BF16), b.astype(BF16), (((a_dim,), (b_dim,)), ((), ())),
        preferred_element_type=F32,
    )


def three_parts(value):
    high = value.astype(BF16)
    rest = value - high.astype(F32)
    middle = rest.astype(BF16)
    low = (rest - middle.astype(F32)).astype(BF16)
    return high, middle, low


def iota(shape, dim):
    return lax.broadcasted_iota(jnp.int32, shape, dim)


def kernel(
    feat, tissue, owner, w_conv, w_stride, w_query, w_key, w_value, cot,
    emb_out, out_buf, full_w,
    field, cols3, trans, slope, grad3, taps, taps_t, stride_w, proj, parts3, mask,
    sums, spread, send_l, send_r, halo_l, halo_r, gsend_l, gsend_r, ghalo_l, ghalo_r,
    edge_l, edge_r, tok_buf, code_buf, code_rows, tissue_s, owner_s, cot_v, stride_back,
    local_w, pair_w, half_w, plane_w, line_w, emb_buf,
    load_sem, halo_ssem, halo_rsem, ghalo_ssem, ghalo_rsem, tok_ssem, tok_rsem,
    plane_ssem, plane_rsem, line_ssem, line_rsem, pair_ssem, pair_rsem, emb_ssem, emb_rsem,
):
    g, h = lax.axis_index("gy"), lax.axis_index("gx")
    x_hi, y = lax.div(g, 4), lax.rem(g, 4)
    z, x_lo, core = lax.div(h, 4), lax.rem(lax.div(h, 2), 2), lax.rem(h, 2)
    position = {"x": 2 * x_hi + x_lo, "y": y, "z": z}
    partner = (g, h + 1 - 2 * core)

    around = {axis: [lax.rem(position[axis] + j, 4) for j in range(4)] for axis in "xyz"}
    share_g = {
        "x": [lax.div(pos, 2) * 4 for pos in around["x"]],
        "y": around["y"],
        "z": [0] * 4,
    }
    share_h = {
        "x": [lax.rem(pos, 2) * 2 for pos in around["x"]],
        "y": [0] * 4,
        "z": [pos * 4 for pos in around["z"]],
    }

    def device_at(**steps):
        steps = {axis: steps.get(axis, 0) for axis in "xyz"}
        return (
            sum(share_g[axis][steps[axis]] for axis in "xy"),
            sum(share_h[axis][steps[axis]] for axis in "xz") + core,
        )

    def plane_steps():
        return [(j, k) for j in range(4) for k in range(4) if (j, k) != (0, 0)]

    def on_plane(axes, j, k):
        return device_at(**{axes[0]: j, axes[1]: k})

    def member_of(axes, j=0, k=0):
        return around[axes[0]][j] * 4 + around[axes[1]][k]

    row_peers = [lax.rem(h + j, GX) for j in range(GX)]

    up, down = lax.rem(g + GY - 1, GY), lax.rem(g + 1, GY)
    left, right = row_peers[GX - 1], row_peers[1]

    def remote(src, dst, ssem, rsem, device):
        return pltpu.make_async_remote_copy(
            src_ref=src, dst_ref=dst, send_sem=ssem, recv_sem=rsem,
            device_id=device, device_id_type=MESH,
        )

    loads = [
        pltpu.make_async_copy(feat, field.at[pl.ds(1, ROWS)], load_sem.at[0]),
        pltpu.make_async_copy(w_conv, taps, load_sem.at[1]),
        pltpu.make_async_copy(w_stride, stride_w, load_sem.at[2]),
        pltpu.make_async_copy(w_query, proj.at[:, pl.ds(0, CH)], load_sem.at[3]),
        pltpu.make_async_copy(w_key, proj.at[:, pl.ds(CH, CH)], load_sem.at[4]),
        pltpu.make_async_copy(w_value, proj.at[:, pl.ds(2 * CH, CH)], load_sem.at[5]),
    ]
    small = [
        pltpu.make_async_copy(tissue, tissue_s, load_sem.at[6]),
        pltpu.make_async_copy(owner, owner_s, load_sem.at[7]),
        pltpu.make_async_copy(cot, cot_v, load_sem.at[8]),
    ]
    loads[0].start()
    barrier = pltpu.get_barrier_semaphore()
    peers = [
        (up, h), (down, h), (g, left), (g, right),
        (up, left), (up, right), (down, left), (down, right),
    ]
    peers += [(g, peer) for peer in row_peers[1:]]
    for axes in ("xy", "yz", "zx"):
        peers += [on_plane(axes, j, k) for j, k in plane_steps()]
    for device in peers:
        pl.semaphore_signal(barrier, inc=1, device_id=device, device_id_type=MESH)

    for copy in loads[1:] + small:
        copy.start()
    for copy in small:
        copy.wait()
    for tile in range(TILES):
        tr, tc = tile // 8, tile % 8
        flag = tissue_s[tr, tc].astype(F32)
        code = flag * (owner_s[0, tile].astype(F32) + 1.0)
        mask[tr, tc * 16 : tc * 16 + 16, :] = jnp.zeros((16, CH), F32) + flag
        code_rows[tile : tile + 1, :] = jnp.zeros((1, 128), F32) + code
    code_buf[h] = code_rows[...].astype(BF16)
    sums[...] = jnp.zeros_like(sums)
    loads[0].wait()

    def edge_columns(row, carry):
        send_l[pl.ds(row, 1), :] = field[row + 1, 0:16, :].astype(F32)[0:1, :]
        send_r[pl.ds(row, 1), :] = field[row + 1, COLS - 16 : COLS, :].astype(F32)[15:16, :]
        return carry

    lax.fori_loop(0, ROWS, edge_columns, 0)
    def halo_copies(first_row, last_row, low_row, high_row, col_l, col_r, got_l, got_r, ss, rs):
        top, bottom = pl.ds(0, 8), pl.ds(ROWS - 8, 8)
        return [
            remote(first_row, high_row, ss.at[0], rs.at[0], (up, h)),
            remote(last_row, low_row, ss.at[1], rs.at[1], (down, h)),
            remote(col_l, got_r.at[pl.ds(8, ROWS)], ss.at[2], rs.at[2], (g, left)),
            remote(col_r, got_l.at[pl.ds(8, ROWS)], ss.at[3], rs.at[3], (g, right)),
            remote(col_r.at[bottom], got_l.at[pl.ds(0, 8)], ss.at[4], rs.at[4], (down, right)),
            remote(col_r.at[top], got_l.at[pl.ds(40, 8)], ss.at[5], rs.at[5], (up, right)),
            remote(col_l.at[bottom], got_r.at[pl.ds(0, 8)], ss.at[6], rs.at[6], (down, left)),
            remote(col_l.at[top], got_r.at[pl.ds(40, 8)], ss.at[7], rs.at[7], (up, left)),
        ]

    has_left, has_right = h > 0, h < GX - 1
    has_up, has_down = g > 0, g < GY - 1
    to_send = (
        has_up, has_down, has_left, has_right,
        has_down & has_right, has_up & has_right, has_down & has_left, has_up & has_left,
    )
    to_receive = (
        has_down, has_up, has_right, has_left,
        has_up & has_left, has_down & has_left, has_up & has_right, has_down & has_right,
    )

    def start_halos(copies):
        for copy, there in zip(copies, to_send):
            pl.when(there)(copy.start)

    def receive_halos(copies, first=0, last=8):
        for copy, there in list(zip(copies, to_receive))[first:last]:
            pl.when(there)(copy.wait_recv)

    def drain_halos(copies):
        for copy, there in zip(copies, to_send):
            pl.when(there)(copy.wait_send)


    def columns_of(center, before, after):
        spot = iota(center.shape, 0)
        low = jnp.where(spot == 0, before, pltpu.roll(center, 1, 0))
        high = jnp.where(spot == COLS - 1, after, pltpu.roll(center, COLS - 1, 0))
        return low, high

    def shift_row(row, carry):
        center = field[row]
        low, high = columns_of(center.astype(F32), 0.0, 0.0)
        cols3[row, :, 0:CH] = low.astype(BF16)
        cols3[row, :, CH : 2 * CH] = center
        cols3[row, :, 2 * CH : 3 * CH] = high.astype(BF16)
        return carry

    lax.fori_loop(1, ROWS + 1, shift_row, 0)
    loads[1].wait()

    def conv_block(source, weights, first, flipped):
        total = None
        for a in range(3):
            start = first + (2 - a if flipped else a)
            block = source[pl.ds(start, CONV_ROWS)].reshape(CONV_ROWS * COLS, 3 * CH)
            part = jnp.dot(block, weights[a], preferred_element_type=F32)
            total = part if total is None else total + part
        return total.reshape(CONV_ROWS, COLS, CH)

    def forward_block(step, carry):
        first = step * CONV_ROWS
        tr = step // (16 // CONV_ROWS)
        pre = conv_block(cols3, taps, first, False)
        for k in range(CONV_ROWS):
            edge_l[pl.ds(first + k, 1), :] = pre[k, 0:1, :]
            edge_r[pl.ds(first + k, 1), :] = pre[k, COLS - 1 : COLS, :]
        gate = jax.nn.sigmoid(pre)
        slope[pl.ds(first, CONV_ROWS)] = gate * (1.0 + pre * (1.0 - gate))
        own = cols3[pl.ds(first + 1, CONV_ROWS), :, CH : 2 * CH].astype(F32)
        summed = (own + pre * gate * mask[tr][None]).astype(BF16).astype(F32)
        for a in range(2):
            total = sums[tr, a]
            for k in range(a, CONV_ROWS, 2):
                total = total + summed[k]
            sums[tr, a] = total
        return carry

    lax.fori_loop(1, 5, forward_block, 0)
    pl.semaphore_wait(barrier, BARRIER_SIGNALS)
    code_copies = [
        remote(
            code_buf.at[h], code_buf.at[h], tok_ssem.at[0, j], tok_rsem.at[0, j], (g, row_peers[j])
        )
        for j in range(1, GX)
    ]
    halos = halo_copies(
        field.at[1], field.at[ROWS], field.at[0], field.at[PAD - 1],
        send_l, send_r, halo_l, halo_r, halo_ssem, halo_rsem,
    )
    start_halos(halos)
    lax.fori_loop(5, 7, forward_block, 0)

    for k in range(3, 6):
        loads[k].wait()
    for k, part in enumerate(three_parts(proj[...])):
        parts3[k] = part
    receive_halos(halos, 0, 2)
    for row, present in ((0, has_up), (PAD - 1, has_down)):
        wide = jnp.where(present, field[row].astype(F32), 0.0)
        low, high = columns_of(wide, 0.0, 0.0)
        cols3[row, :, 0:CH] = low.astype(BF16)
        cols3[row, :, CH : 2 * CH] = wide.astype(BF16)
        cols3[row, :, 2 * CH : 3 * CH] = high.astype(BF16)

    for copy in code_copies:
        copy.start()

    lax.fori_loop(0, 2, lambda i, carry: forward_block(i * 7, carry), 0)
    receive_halos(halos, 2)
    row_of = iota((ROWS, CH), 0)
    inside = ((row_of > 0) | has_up, None, (row_of < ROWS - 1) | has_down)

    def fix_edge(got, present, edge, own, tap_at, col):
        terms = []
        for a in range(3):
            there = present if inside[a] is None else inside[a] & present
            terms.append(jnp.where(there, got[7 + a : 7 + a + ROWS, :], 0.0).astype(BF16))
        pre = edge[...]
        flag = jnp.where(row_of < 16, mask[0, col : col + 1, :], mask[1, col : col + 1, :])
        old = (own[...] + pre * jax.nn.sigmoid(pre) * flag).astype(BF16).astype(F32)
        for a in range(3):
            pre = pre + jnp.dot(
                terms[a], taps[a, tap_at * CH : (tap_at + 1) * CH, :], preferred_element_type=F32
            )
        gate = jax.nn.sigmoid(pre)
        new = (own[...] + pre * gate * flag).astype(BF16).astype(F32)
        slant = gate * (1.0 + pre * (1.0 - gate))
        change = new - old
        for tr in range(2):
            for a in range(2):
                part = jnp.where((row_of // 16 == tr) & (row_of % 2 == a), change, 0.0)
                sums[tr, a, col : col + 1, :] = sums[tr, a, col : col + 1, :] + jnp.sum(
                    part, axis=0, keepdims=True
                )
        for row in range(ROWS):
            slope[row, col : col + 1, :] = slant[row : row + 1, :]

    fix_edge(halo_l, has_left, edge_l, send_l, 0, 0)
    fix_edge(halo_r, has_right, edge_r, send_r, 2, COLS - 1)


    lane_col, row_id = iota((16, COLS), 1), iota((16, COLS), 0)
    select = ((lane_col // 16 == row_id % 8) & (lane_col % 2 == row_id // 8)).astype(BF16)
    gathered = jnp.concatenate([sums[tr, a] for tr in range(2) for a in range(2)], axis=1)
    parts = three_parts(gathered)
    cell_sums = sum(jnp.dot(select, part, preferred_element_type=F32) for part in parts)
    loads[2].wait()
    pooled = jnp.zeros((TILES, CH), F32)
    for a in range(2):
        for b in range(2):
            tap = 2 * a + b
            lhs = jnp.concatenate(
                [cell_sums[b * 8 : b * 8 + 8, (2 * tr + a) * CH : (2 * tr + a + 1) * CH] for tr in range(2)],
                axis=0,
            )
            rhs = stride_w[tap * CH : (tap + 1) * CH, :]
            pooled = pooled + sum(
                jnp.dot(part, rhs, preferred_element_type=F32) for part in three_parts(lhs)
            )
    pooled = pooled * (1.0 / 64.0)
    inverse = lax.rsqrt(jnp.mean(pooled * pooled, axis=-1, keepdims=True) + 1e-05)
    normed = (pooled * inverse).astype(BF16)

    code = code_rows[...]
    tok_buf[h] = normed
    tok_copies = [
        remote(
            tok_buf.at[h], tok_buf.at[h], tok_ssem.at[1, j], tok_rsem.at[1, j], (g, row_peers[j])
        )
        for j in sorted(range(1, GX), key=lambda j: abs(j - GX // 2))
    ]
    for copy in tok_copies:
        copy.start()

    head_of = iota((1, CH), 1) // (CH // HEADS)
    heads = [(head_of == k).astype(F32) for k in range(HEADS)]

    def by_head(rows):
        return jnp.concatenate([rows * m for m in heads], axis=0)

    def join_heads(rows):
        return sum(rows[k * TILES : (k + 1) * TILES, :] * heads[k] for k in range(HEADS))

    own_qkv = sum(jnp.dot(normed, parts3[k], preferred_element_type=F32) for k in range(3))
    own_value = own_qkv[:, 2 * CH : 3 * CH]
    query_by_head, key_by_head = by_head(own_qkv[:, 0:CH]), by_head(own_qkv[:, CH : 2 * CH])
    seed = cot_v[...] * (loss_scale / math.sqrt(GY * GX * TILES))
    seed_by_head = by_head(jnp.broadcast_to(seed, (8, CH)))
    value_seed = exact_dot(seed_by_head, proj[:, 2 * CH : 3 * CH], 1, 1)
    own_value_seed = jnp.sum(by_head(own_value * seed), axis=1, keepdims=True)

    def patch_row(row, carry):
        near = halo_l[pl.ds(7 + row, 1), :]
        far = halo_r[pl.ds(7 + row, 1), :]
        there = ((row > 0) | has_up) & ((row < PAD - 1) | has_down)
        near = jnp.where(has_left & there, near, 0.0)
        far = jnp.where(has_right & there, far, 0.0)
        head = cols3[row, 0:16, 0:CH].astype(F32)
        tail = cols3[row, COLS - 16 : COLS, 2 * CH : 3 * CH].astype(F32)
        spot = iota(head.shape, 0)
        cols3[row, 0:16, 0:CH] = jnp.where(spot == 0, near, head).astype(BF16)
        cols3[row, COLS - 16 : COLS, 2 * CH : 3 * CH] = jnp.where(spot == 15, far, tail).astype(BF16)
        return carry

    lax.fori_loop(0, PAD, patch_row, 0)

    def transpose_row(row, carry):
        lanes = pl.ds(pl.multiple_of(row * COLS, COLS), COLS)
        for b in range(3):
            trans[b, :, lanes] = cols3[row, :, b * CH : (b + 1) * CH].T
        return carry

    lax.fori_loop(0, PAD, transpose_row, 0)
    for copy in tok_copies:
        copy.wait_recv()

    everyone = tok_buf[...].reshape(GX * TILES, CH)
    for copy in code_copies:
        copy.wait_recv()
    codes = code_buf[...].reshape(GX * TILES, 128)
    all_qk = sum(
        jnp.dot(everyone, parts3[k, :, 0 : 2 * CH], preferred_element_type=F32) for k in range(3)
    )
    all_query, all_key = all_qk[:, 0:CH], all_qk[:, CH : 2 * CH]
    lane0 = (iota((TILES, 128), 1) == 0).astype(F32)
    codes_across = half_dot(lane0, codes, 1, 1)
    allowed = ((codes_across == code[:, 0:1]) & (codes_across > 0.5)).astype(F32)
    allowed = jnp.concatenate([allowed] * HEADS, axis=0)
    scale = 1.0 / math.sqrt(CH // HEADS)
    as_query = jax.nn.sigmoid(close_dot(query_by_head, all_key, 1, 1) * scale + attention_bias)
    as_key = jax.nn.sigmoid(close_dot(key_by_head, all_query, 1, 1) * scale + attention_bias)
    weight_sums = jnp.sum(as_key * allowed, axis=1, keepdims=True)
    head_sums = join_heads(jnp.broadcast_to(weight_sums, (HEADS * TILES, CH)))
    partial = jnp.sum(head_sums * own_value, axis=0, keepdims=True)
    d_value = head_sums * seed
    across = sum(half_dot(part, everyone, 1, 1) for part in three_parts(value_seed))
    across = jnp.concatenate([across[8 * k : 8 * k + 8, :] for k in range(HEADS) for _ in range(2)], axis=0)
    d_as_query = across * allowed * as_query * (1.0 - as_query) * scale
    d_as_key = own_value_seed * allowed * as_key * (1.0 - as_key) * scale
    d_query = join_heads(close_dot(d_as_query, all_key))
    d_key = join_heads(close_dot(d_as_key, all_query))
    d_qkv = three_parts(jnp.concatenate([d_query, d_key, d_value], axis=1))
    d_tokens = jnp.zeros((TILES, CH), F32)
    for k in range(3):
        lhs = jnp.concatenate(d_qkv[: 3 - k], axis=0)
        product = half_dot(lhs, parts3[k], 1, 1)
        for part in range(3 - k):
            d_tokens = d_tokens + product[part * TILES : (part + 1) * TILES, :]
    token_grad = d_tokens.astype(BF16).astype(F32)

    emb_steps = [("core", 2, core)] + [(axis, 4, position[axis]) for axis in ("x", "y", "z")]

    def emb_copies(step):
        axis, count, pos = emb_steps[step]
        copies = []
        for j in range(1, count):
            device = partner if axis == "core" else device_at(**{axis: j})
            spot = emb_buf.at[step, pos]
            copies.append(
                remote(spot, spot, emb_ssem.at[step, j], emb_rsem.at[step, j], device)
            )
        return copies

    def emb_start(step, term):
        emb_buf[step, emb_steps[step][2]] = term
        for copy in emb_copies(step):
            copy.start()

    def emb_finish(step):
        for copy in emb_copies(step):
            copy.wait_recv()
        total = emb_buf[step, 0]
        for k in range(1, emb_steps[step][1]):
            total = total + emb_buf[step, k]
        return total

    emb_start(0, jnp.broadcast_to(partial, (8, CH)))

    inner = jnp.mean(token_grad * pooled, axis=-1, keepdims=True)
    pooled_grad = token_grad * inverse - pooled * (inverse * inverse * inverse * inner)
    cell_grad = (pooled_grad * (1.0 / 64.0)).astype(BF16)
    stride_back[...] = half_dot(cell_grad, stride_w[...], 1, 1)
    odd = (iota((16, CH), 0) % 2) == 1
    for tile in range(TILES):
        tr, tc = tile // 8, tile % 8
        for a in range(2):
            even_row = stride_back[tile : tile + 1, (2 * a) * CH : (2 * a + 1) * CH]
            odd_row = stride_back[tile : tile + 1, (2 * a + 1) * CH : (2 * a + 2) * CH]
            spread[tr, a, tc * 16 : tc * 16 + 16, :] = jnp.where(odd, odd_row, even_row)

    def pre_grad_row(row, carry):
        tr = row // 16
        value = (spread[tr, row % 2] * mask[tr] * slope[row]).astype(BF16)
        grad3[row + 1, :, CH : 2 * CH] = value
        wide = value.astype(F32)
        gsend_l[pl.ds(row, 1), :] = wide[0:1, :]
        gsend_r[pl.ds(row, 1), :] = wide[COLS - 1 : COLS, :]
        return carry

    lax.fori_loop(0, ROWS, pre_grad_row, 0)
    middle = pl.ds(CH, CH)
    ghalos = halo_copies(
        grad3.at[1, :, middle], grad3.at[ROWS, :, middle],
        grad3.at[0, :, middle], grad3.at[PAD - 1, :, middle],
        gsend_l, gsend_r, ghalo_l, ghalo_r, ghalo_ssem, ghalo_rsem,
    )
    start_halos(ghalos)

    def chunk_rows(k):
        first, count, _ = CHUNKS[k]
        return pl.ds(first * CH, count * CH)

    def shard_rows(k):
        first, count, _ = CHUNKS[k]
        return pl.ds(first * 16, count * 16)

    def block_rows(k, member):
        first, count, _ = CHUNKS[k]
        return pl.ds(pl.multiple_of(first * CH + member * (count * 16), 16), count * 16)

    def pair_copy(k):
        rows = chunk_rows(k)
        return remote(
            local_w.at[1 - core, rows], pair_w.at[rows], pair_ssem.at[0, k], pair_rsem.at[0, k], partner
        )

    def plane_copies(k, back):
        axes = CHUNKS[k][2]
        copies = []
        for n, (j, i) in enumerate(plane_steps()):
            if back:
                source = target = full_w.at[core, block_rows(k, member_of(axes))]
            else:
                source = half_w.at[block_rows(k, member_of(axes, j, i))]
                target = plane_w.at[n, shard_rows(k)]
            copies.append(
                remote(
                    source, target, plane_ssem.at[back, k, n], plane_rsem.at[back, k, n],
                    on_plane(axes, j, i),
                )
            )
        return copies

    def line_copies(k):
        axis = CHUNKS[k][2][2]
        pos = position[axis]
        spot = line_w.at[pos, shard_rows(k)]
        return [
            remote(
                spot, spot, line_ssem.at[k, j], line_rsem.at[k, j], device_at(**{axis: j})
            )
            for j in range(1, 4)
        ]

    def last_copy(k):
        spot = full_w.at[core, chunk_rows(k)]
        return remote(spot, spot, pair_ssem.at[1, k], pair_rsem.at[1, k], partner)

    def reduce_step(k, step):
        axes = CHUNKS[k][2]
        rows, shard = chunk_rows(k), shard_rows(k)
        if step == 0:
            pair_copy(k).start()
        elif step == 1:
            pair_copy(k).wait_recv()
            both = local_w[core, rows].astype(F32) + pair_w[rows].astype(F32)
            half_w[rows] = both.astype(BF16)
            for copy in plane_copies(k, 0):
                copy.start()
        elif step == 2:
            for copy in plane_copies(k, 0):
                copy.wait_recv()
            total = half_w[block_rows(k, member_of(axes))].astype(F32)
            for j in range(15):
                total = total + plane_w[j, shard].astype(F32)
            line_w[position[axes[2]], shard] = total.astype(BF16)
            for copy in line_copies(k):
                copy.start()
        elif step == 3:
            for copy in line_copies(k):
                copy.wait_recv()
            total = line_w[0, shard].astype(F32)
            for j in range(1, 4):
                total = total + line_w[j, shard].astype(F32)
            full_w[core, block_rows(k, member_of(axes))] = total.astype(BF16)
            for copy in plane_copies(k, 1):
                copy.start()
        elif step == 4:
            for copy in plane_copies(k, 1):
                copy.wait_recv()
            last_copy(k).start()
        else:
            last_copy(k).wait_recv()

    def tap_of(tap, carry):
        a, b = tap // 3, tap % 3
        lhs = trans[b, :, pl.ds(pl.multiple_of(a * COLS, COLS), ROWS * COLS)]
        rhs = grad3[pl.ds(1, ROWS), :, CH : 2 * CH].reshape(ROWS * COLS, CH)
        part = jnp.dot(lhs, rhs, preferred_element_type=F32)
        rows = pl.ds(pl.multiple_of(tap * CH, CH), CH)
        for c in range(2):
            local_w[c, rows, :] = part[:, c * 128 : c * 128 + 128].astype(BF16)
        return carry

    after_taps = [[(0, 0)], [(1, 0), (0, 1)], [(2, 0), (1, 1)]]
    for k, (first, count, _) in enumerate(CHUNKS):
        lax.fori_loop(first, first + count, tap_of, 0)
        for chunk, step in after_taps[k]:
            reduce_step(chunk, step)
        if k < 2:
            emb_start(k + 1, emb_finish(k))

    receive_halos(ghalos)

    def grad_shift(row, carry):
        wide = grad3[row, :, CH : 2 * CH].astype(F32)
        near = jnp.where(has_left, ghalo_l[pl.ds(7 + row, 1), :], 0.0)
        far = jnp.where(has_right, ghalo_r[pl.ds(7 + row, 1), :], 0.0)
        low, high = columns_of(wide, near, far)
        grad3[row, :, 0:CH] = high.astype(BF16)
        grad3[row, :, 2 * CH : 3 * CH] = low.astype(BF16)
        return carry

    for a in range(3):
        for b in range(3):
            taps_t[a, b * CH : (b + 1) * CH, :] = taps[a, b * CH : (b + 1) * CH, :].T
    lax.fori_loop(0, PAD // 2, grad_shift, 0)
    reduce_step(2, 1)
    lax.fori_loop(PAD // 2, PAD, grad_shift, 0)
    for row, present in ((0, has_up), (PAD - 1, has_down)):
        edge = grad3[row].astype(F32)
        grad3[row] = jnp.where(present, edge, 0.0).astype(BF16)

    def back_block(step, carry):
        first = step * CONV_ROWS
        tr = step // (16 // CONV_ROWS)
        total = conv_block(grad3, taps_t, first, True)
        for k in range(CONV_ROWS):
            out_buf[first + k] = (total[k] + spread[tr, k % 2]).astype(BF16)
        return carry

    order = [[(0, 2)], [(1, 2)], [(0, 3), (2, 2)], [(1, 3)]]
    for part in range(4):
        for chunk, step in order[part]:
            reduce_step(chunk, step)
        lax.fori_loop(2 * part, 2 * part + 2, back_block, 0)
    emb_start(3, emb_finish(2))
    for chunk, step in [(2, 3), (0, 4), (1, 4), (2, 4), (0, 5), (1, 5), (2, 5)]:
        reduce_step(chunk, step)
    emb_out[...] = emb_finish(3)[0:1, :] * (1.0 / math.sqrt(GY * GX * TILES))

    drain_halos(halos)
    drain_halos(ghalos)
    for copy in code_copies + tok_copies:
        copy.wait_send()
    for k in range(len(CHUNKS)):
        for copy in [pair_copy(k), last_copy(k)] + line_copies(k):
            copy.wait_send()
        for back in range(2):
            for copy in plane_copies(k, back):
                copy.wait_send()
    for step in range(4):
        for copy in emb_copies(step):
            copy.wait_send()


def finish(emb, grad, conv, emb_out, grad_out, conv_out, wide, sem):
    copies = [
        pltpu.make_async_copy(emb, emb_out, sem.at[0]),
        pltpu.make_async_copy(grad.at[pl.ds(0, 16)], grad_out.at[pl.ds(0, 16)], sem.at[1]),
        pltpu.make_async_copy(grad.at[pl.ds(16, 16)], grad_out.at[pl.ds(16, 16)], sem.at[2]),
    ]
    for copy in copies:
        copy.start()
    for k in range(3):
        rows = pl.ds(k * 3 * CH, 3 * CH)
        for c in range(2):
            wide[rows, c * 128 : c * 128 + 128] = conv[c, rows].astype(F32) * (1.0 / loss_scale)
        copy = pltpu.make_async_copy(wide.at[rows], conv_out.at[rows], sem.at[3 + k])
        copy.start()
        copies.append(copy)
    for copy in copies:
        copy.wait()


def per_device(features, tissue, owner_map, w_conv, w_stride, w_query, w_key, w_value, cotangent):
    whole = pl.BlockSpec(memory_space=pl.ANY)
    vector = pl.BlockSpec(memory_space=pltpu.VMEM)
    dma = pltpu.SemaphoreType.DMA
    columns = pltpu.VMEM((ROWS, CH), F32)
    column_halo = pltpu.VMEM((ROWS + 16, CH), F32)
    embedding, input_grad, conv_grad = pl.pallas_call(
        kernel,
        out_shape=(
            pltpu.VMEM((1, CH), F32),
            pltpu.VMEM((ROWS, COLS, CH), BF16),
            pltpu.VMEM((2, 9 * CH, 128), BF16),
        ),
        in_specs=[whole] * 9,
        out_specs=(vector, vector, vector),
        scratch_shapes=[
            pltpu.VMEM((PAD, COLS, CH), BF16),
            pltpu.VMEM((PAD, COLS, 3 * CH), BF16),
            pltpu.VMEM((3, CH, PAD * COLS), BF16),
            pltpu.VMEM((ROWS, COLS, CH), F32),
            pltpu.VMEM((PAD, COLS, 3 * CH), BF16),
            pltpu.VMEM((3, 3 * CH, CH), BF16),
            pltpu.VMEM((3, 3 * CH, CH), BF16),
            pltpu.VMEM((4 * CH, CH), BF16),
            pltpu.VMEM((CH, 3 * CH), F32),
            pltpu.VMEM((3, CH, 3 * CH), BF16),
            pltpu.VMEM((2, COLS, CH), F32),
            pltpu.VMEM((2, 2, COLS, CH), F32),
            pltpu.VMEM((2, 2, COLS, CH), F32),
            columns, columns, column_halo, column_halo,
            columns, columns, column_halo, column_halo,
            columns, columns,
            pltpu.VMEM((GX, TILES, CH), BF16),
            pltpu.VMEM((GX, TILES, 128), BF16),
            pltpu.VMEM((TILES, 128), F32),
            pltpu.SMEM((2, 8), jnp.int32),
            pltpu.SMEM((1, TILES), jnp.int32),
            pltpu.VMEM((1, CH), F32),
            pltpu.VMEM((TILES, 4 * CH), F32),
            pltpu.VMEM((2, 9 * CH, 128), BF16),
            pltpu.VMEM((9 * CH, 128), BF16),
            pltpu.VMEM((9 * CH, 128), BF16),
            pltpu.VMEM((15, 144, 128), BF16),
            pltpu.VMEM((4, 144, 128), BF16),
            pltpu.VMEM((4, 4, 8, CH), F32),
            dma((9,)), dma((8,)), dma((8,)), dma((8,)), dma((8,)),
            dma((2, GX)), dma((2, GX)),
            dma((2, 3, 16)), dma((2, 3, 16)), dma((3, 4)), dma((3, 4)), dma((2, 3)), dma((2, 3)),
            dma((4, 4)), dma((4, 4)),
        ],
        compiler_params=pltpu.CompilerParams(
            collective_id=0, has_side_effects=True, vmem_limit_bytes=56 * 1024 * 1024
        ),
    )(
        features, tissue, owner_map.reshape(1, TILES), w_conv.reshape(3, 3 * CH, CH),
        w_stride.reshape(4 * CH, CH), w_query, w_key, w_value, cotangent.reshape(1, CH),
    )
    embedding, input_grad, conv_grad = pl.pallas_call(
        finish,
        out_shape=(
            jax.ShapeDtypeStruct((1, CH), F32),
            jax.ShapeDtypeStruct((ROWS, COLS, CH), BF16),
            jax.ShapeDtypeStruct((9 * CH, CH), F32),
        ),
        in_specs=[vector, vector, vector],
        out_specs=(whole, whole, whole),
        scratch_shapes=[pltpu.VMEM((9 * CH, CH), F32), dma((6,))],
    )(*(pltpu.with_memory_space_constraint(x, pltpu.VMEM) for x in (embedding, input_grad, conv_grad)))
    return embedding.reshape(CH), input_grad, conv_grad.reshape(9, CH, CH)


def solution(mesh):
    in_specs = (
        P("gy", "gx", None), P("gy", "gx"), P("gy", "gx", None, None),
        P(), P(), P(), P(), P(), P(),
    )
    out_specs = (P(), P("gy", "gx", None), P())
    return jax.shard_map(
        per_device, mesh=mesh, in_specs=in_specs, out_specs=out_specs, check_vma=False
    )
```

```python
import math

import jax
import jax.numpy as jnp
from jax import lax
from jax.experimental import pallas as pl
from jax.experimental.pallas import tpu as pltpu
from jax.sharding import PartitionSpec as P

MESH = pl.DeviceIdType.MESH
F32, BF16 = jnp.float32, jnp.bfloat16
HEADS = 4
attention_bias = -1.0
loss_scale = 512.0

GY, GX = 8, 16
ROWS, COLS, CH = 32, 128, 256
PAD = ROWS + 2
TILES = 16
CONV_ROWS = 4
CHUNKS = ((0, 3, "xyz"), (3, 3, "zxy"), (6, 3, "zxy"))
BARRIER_SIGNALS = 23 + 24


def exact_dot(a, b, a_dim=1, b_dim=0):
    return lax.dot_general(
        a, b, (((a_dim,), (b_dim,)), ((), ())),
        precision=lax.Precision.HIGHEST, preferred_element_type=F32,
    )


def close_dot(a, b, a_dim=1, b_dim=0):
    (a_high, a_low, _), (b_high, b_low, _) = three_parts(a), three_parts(b)
    rows = a.shape[0]
    both = half_dot(jnp.concatenate([a_high, a_low], axis=0), b_high, a_dim, b_dim)
    return both[:rows] + both[rows:] + half_dot(a_high, b_low, a_dim, b_dim)


def half_dot(a, b, a_dim=1, b_dim=0):
    return lax.dot_general(
        a.astype(BF16), b.astype(BF16), (((a_dim,), (b_dim,)), ((), ())),
        preferred_element_type=F32,
    )


def three_parts(value):
    high = value.astype(BF16)
    rest = value - high.astype(F32)
    middle = rest.astype(BF16)
    low = (rest - middle.astype(F32)).astype(BF16)
    return high, middle, low


def iota(shape, dim):
    return lax.broadcasted_iota(jnp.int32, shape, dim)


def kernel(
    feat, tissue, owner, w_conv, w_stride, w_query, w_key, w_value, cot,
    emb_out, out_buf, full_w,
    field, cols3, trans, slope, grad3, taps, taps_t, stride_w, proj, parts3, mask,
    sums, spread, send_l, send_r, halo_l, halo_r, gsend_l, gsend_r, ghalo_l, ghalo_r,
    edge_l, edge_r, tok_buf, code_buf, code_rows, tissue_s, owner_s, cot_v, stride_back,
    local_w, pair_w, half_w, plane_w, line_w, emb_buf,
    load_sem, halo_ssem, halo_rsem, ghalo_ssem, ghalo_rsem, tok_ssem, tok_rsem,
    plane_ssem, plane_rsem, line_ssem, line_rsem, pair_ssem, pair_rsem, emb_ssem, emb_rsem,
):
    g, h = lax.axis_index("gy"), lax.axis_index("gx")
    x_hi, y = lax.div(g, 4), lax.rem(g, 4)
    z, x_lo, core = lax.div(h, 4), lax.rem(lax.div(h, 2), 2), lax.rem(h, 2)
    position = {"x": 2 * x_hi + x_lo, "y": y, "z": z}
    partner = (g, h + 1 - 2 * core)

    around = {axis: [lax.rem(position[axis] + j, 4) for j in range(4)] for axis in "xyz"}
    share_g = {
        "x": [lax.div(pos, 2) * 4 for pos in around["x"]],
        "y": around["y"],
        "z": [0] * 4,
    }
    share_h = {
        "x": [lax.rem(pos, 2) * 2 for pos in around["x"]],
        "y": [0] * 4,
        "z": [pos * 4 for pos in around["z"]],
    }

    def device_at(**steps):
        steps = {axis: steps.get(axis, 0) for axis in "xyz"}
        return (
            sum(share_g[axis][steps[axis]] for axis in "xy"),
            sum(share_h[axis][steps[axis]] for axis in "xz") + core,
        )

    def plane_steps():
        return [(j, k) for j in range(4) for k in range(4) if (j, k) != (0, 0)]

    def on_plane(axes, j, k):
        return device_at(**{axes[0]: j, axes[1]: k})

    def member_of(axes, j=0, k=0):
        return around[axes[0]][j] * 4 + around[axes[1]][k]

    row_peers = [lax.rem(h + j, GX) for j in range(GX)]

    up, down = lax.rem(g + GY - 1, GY), lax.rem(g + 1, GY)
    left, right = row_peers[GX - 1], row_peers[1]

    def remote(src, dst, ssem, rsem, device):
        return pltpu.make_async_remote_copy(
            src_ref=src, dst_ref=dst, send_sem=ssem, recv_sem=rsem,
            device_id=device, device_id_type=MESH,
        )

    loads = [
        pltpu.make_async_copy(feat, field.at[pl.ds(1, ROWS)], load_sem.at[0]),
        pltpu.make_async_copy(w_conv, taps, load_sem.at[1]),
        pltpu.make_async_copy(w_stride, stride_w, load_sem.at[2]),
        pltpu.make_async_copy(w_query, proj.at[:, pl.ds(0, CH)], load_sem.at[3]),
        pltpu.make_async_copy(w_key, proj.at[:, pl.ds(CH, CH)], load_sem.at[4]),
        pltpu.make_async_copy(w_value, proj.at[:, pl.ds(2 * CH, CH)], load_sem.at[5]),
    ]
    small = [
        pltpu.make_async_copy(tissue, tissue_s, load_sem.at[6]),
        pltpu.make_async_copy(owner, owner_s, load_sem.at[7]),
        pltpu.make_async_copy(cot, cot_v, load_sem.at[8]),
    ]
    loads[0].start()
    barrier = pltpu.get_barrier_semaphore()
    peers = [
        (up, h), (down, h), (g, left), (g, right),
        (up, left), (up, right), (down, left), (down, right),
    ]
    peers += [(g, peer) for peer in row_peers[1:]]
    peers += [
        device_at(x=i, y=j, z=k)
        for i in range(4) for j in range(4) for k in range(4)
        if 0 in (j, k) and (i, j) != (0, 0)
    ]
    for device in peers:
        pl.semaphore_signal(barrier, inc=1, device_id=device, device_id_type=MESH)

    for copy in loads[1:] + small:
        copy.start()
    for copy in small:
        copy.wait()
    for tile in range(TILES):
        tr, tc = tile // 8, tile % 8
        flag = tissue_s[tr, tc].astype(F32)
        code = flag * (owner_s[0, tile].astype(F32) + 1.0)
        mask[tr, tc * 16 : tc * 16 + 16, :] = jnp.zeros((16, CH), F32) + flag
        code_rows[tile : tile + 1, :] = jnp.zeros((1, 128), F32) + code
    code_buf[h] = code_rows[...].astype(BF16)
    sums[...] = jnp.zeros_like(sums)
    loads[0].wait()

    def edge_columns(row, carry):
        send_l[pl.ds(row, 1), :] = field[row + 1, 0:16, :].astype(F32)[0:1, :]
        send_r[pl.ds(row, 1), :] = field[row + 1, COLS - 16 : COLS, :].astype(F32)[15:16, :]
        return carry

    lax.fori_loop(0, ROWS, edge_columns, 0)
    def halo_copies(first_row, last_row, low_row, high_row, col_l, col_r, got_l, got_r, ss, rs):
        top, bottom = pl.ds(0, 8), pl.ds(ROWS - 8, 8)
        return [
            remote(first_row, high_row, ss.at[0], rs.at[0], (up, h)),
            remote(last_row, low_row, ss.at[1], rs.at[1], (down, h)),
            remote(col_l, got_r.at[pl.ds(8, ROWS)], ss.at[2], rs.at[2], (g, left)),
            remote(col_r, got_l.at[pl.ds(8, ROWS)], ss.at[3], rs.at[3], (g, right)),
            remote(col_r.at[bottom], got_l.at[pl.ds(0, 8)], ss.at[4], rs.at[4], (down, right)),
            remote(col_r.at[top], got_l.at[pl.ds(40, 8)], ss.at[5], rs.at[5], (up, right)),
            remote(col_l.at[bottom], got_r.at[pl.ds(0, 8)], ss.at[6], rs.at[6], (down, left)),
            remote(col_l.at[top], got_r.at[pl.ds(40, 8)], ss.at[7], rs.at[7], (up, left)),
        ]

    has_left, has_right = h > 0, h < GX - 1
    has_up, has_down = g > 0, g < GY - 1
    to_send = (
        has_up, has_down, has_left, has_right,
        has_down & has_right, has_up & has_right, has_down & has_left, has_up & has_left,
    )
    to_receive = (
        has_down, has_up, has_right, has_left,
        has_up & has_left, has_down & has_left, has_up & has_right, has_down & has_right,
    )

    def start_halos(copies):
        for copy, there in zip(copies, to_send):
            pl.when(there)(copy.start)

    def receive_halos(copies, first=0, last=8):
        for copy, there in list(zip(copies, to_receive))[first:last]:
            pl.when(there)(copy.wait_recv)

    def drain_halos(copies):
        for copy, there in zip(copies, to_send):
            pl.when(there)(copy.wait_send)


    def columns_of(center, before, after):
        spot = iota(center.shape, 0)
        low = jnp.where(spot == 0, before, pltpu.roll(center, 1, 0))
        high = jnp.where(spot == COLS - 1, after, pltpu.roll(center, COLS - 1, 0))
        return low, high

    def shift_row(row, carry):
        center = field[row]
        low, high = columns_of(center.astype(F32), 0.0, 0.0)
        cols3[row, :, 0:CH] = low.astype(BF16)
        cols3[row, :, CH : 2 * CH] = center
        cols3[row, :, 2 * CH : 3 * CH] = high.astype(BF16)
        return carry

    lax.fori_loop(1, ROWS + 1, shift_row, 0)
    loads[1].wait()

    def conv_block(source, weights, first, flipped):
        total = None
        for a in range(3):
            start = first + (2 - a if flipped else a)
            block = source[pl.ds(start, CONV_ROWS)].reshape(CONV_ROWS * COLS, 3 * CH)
            part = jnp.dot(block, weights[a], preferred_element_type=F32)
            total = part if total is None else total + part
        return total.reshape(CONV_ROWS, COLS, CH)

    def forward_block(step, carry):
        first = step * CONV_ROWS
        tr = step // (16 // CONV_ROWS)
        pre = conv_block(cols3, taps, first, False)
        for k in range(CONV_ROWS):
            edge_l[pl.ds(first + k, 1), :] = pre[k, 0:1, :]
            edge_r[pl.ds(first + k, 1), :] = pre[k, COLS - 1 : COLS, :]
        gate = jax.nn.sigmoid(pre)
        slope[pl.ds(first, CONV_ROWS)] = gate * (1.0 + pre * (1.0 - gate))
        own = cols3[pl.ds(first + 1, CONV_ROWS), :, CH : 2 * CH].astype(F32)
        summed = (own + pre * gate * mask[tr][None]).astype(BF16).astype(F32)
        for a in range(2):
            total = sums[tr, a]
            for k in range(a, CONV_ROWS, 2):
                total = total + summed[k]
            sums[tr, a] = total
        return carry

    lax.fori_loop(1, 5, forward_block, 0)
    pl.semaphore_wait(barrier, BARRIER_SIGNALS)
    code_copies = [
        remote(
            code_buf.at[h], code_buf.at[h], tok_ssem.at[0, j], tok_rsem.at[0, j], (g, row_peers[j])
        )
        for j in range(1, GX)
    ]
    halos = halo_copies(
        field.at[1], field.at[ROWS], field.at[0], field.at[PAD - 1],
        send_l, send_r, halo_l, halo_r, halo_ssem, halo_rsem,
    )
    start_halos(halos)
    lax.fori_loop(5, 7, forward_block, 0)

    for k in range(3, 6):
        loads[k].wait()
    for k, part in enumerate(three_parts(proj[...])):
        parts3[k] = part
    receive_halos(halos, 0, 2)
    for row, present in ((0, has_up), (PAD - 1, has_down)):
        wide = jnp.where(present, field[row].astype(F32), 0.0)
        low, high = columns_of(wide, 0.0, 0.0)
        cols3[row, :, 0:CH] = low.astype(BF16)
        cols3[row, :, CH : 2 * CH] = wide.astype(BF16)
        cols3[row, :, 2 * CH : 3 * CH] = high.astype(BF16)

    for copy in code_copies:
        copy.start()

    lax.fori_loop(0, 2, lambda i, carry: forward_block(i * 7, carry), 0)
    receive_halos(halos, 2)
    row_of = iota((ROWS, CH), 0)
    inside = ((row_of > 0) | has_up, None, (row_of < ROWS - 1) | has_down)

    def fix_edge(got, present, edge, own, tap_at, col):
        terms = []
        for a in range(3):
            there = present if inside[a] is None else inside[a] & present
            terms.append(jnp.where(there, got[7 + a : 7 + a + ROWS, :], 0.0).astype(BF16))
        pre = edge[...]
        flag = jnp.where(row_of < 16, mask[0, col : col + 1, :], mask[1, col : col + 1, :])
        old = (own[...] + pre * jax.nn.sigmoid(pre) * flag).astype(BF16).astype(F32)
        for a in range(3):
            pre = pre + jnp.dot(
                terms[a], taps[a, tap_at * CH : (tap_at + 1) * CH, :], preferred_element_type=F32
            )
        gate = jax.nn.sigmoid(pre)
        new = (own[...] + pre * gate * flag).astype(BF16).astype(F32)
        slant = gate * (1.0 + pre * (1.0 - gate))
        change = new - old
        for tr in range(2):
            for a in range(2):
                part = jnp.where((row_of // 16 == tr) & (row_of % 2 == a), change, 0.0)
                sums[tr, a, col : col + 1, :] = sums[tr, a, col : col + 1, :] + jnp.sum(
                    part, axis=0, keepdims=True
                )
        for row in range(ROWS):
            slope[row, col : col + 1, :] = slant[row : row + 1, :]

    fix_edge(halo_l, has_left, edge_l, send_l, 0, 0)
    fix_edge(halo_r, has_right, edge_r, send_r, 2, COLS - 1)


    lane_col, row_id = iota((16, COLS), 1), iota((16, COLS), 0)
    select = ((lane_col // 16 == row_id % 8) & (lane_col % 2 == row_id // 8)).astype(BF16)
    gathered = jnp.concatenate([sums[tr, a] for tr in range(2) for a in range(2)], axis=1)
    parts = three_parts(gathered)
    cell_sums = sum(jnp.dot(select, part, preferred_element_type=F32) for part in parts)
    loads[2].wait()
    pooled = jnp.zeros((TILES, CH), F32)
    for a in range(2):
        for b in range(2):
            tap = 2 * a + b
            lhs = jnp.concatenate(
                [cell_sums[b * 8 : b * 8 + 8, (2 * tr + a) * CH : (2 * tr + a + 1) * CH] for tr in range(2)],
                axis=0,
            )
            rhs = stride_w[tap * CH : (tap + 1) * CH, :]
            pooled = pooled + sum(
                jnp.dot(part, rhs, preferred_element_type=F32) for part in three_parts(lhs)
            )
    pooled = pooled * (1.0 / 64.0)
    inverse = lax.rsqrt(jnp.mean(pooled * pooled, axis=-1, keepdims=True) + 1e-05)
    normed = (pooled * inverse).astype(BF16)

    code = code_rows[...]
    tok_buf[h] = normed
    tok_copies = [
        remote(
            tok_buf.at[h], tok_buf.at[h], tok_ssem.at[1, j], tok_rsem.at[1, j], (g, row_peers[j])
        )
        for j in sorted(range(1, GX), key=lambda j: abs(j - GX // 2))
    ]
    for copy in tok_copies:
        copy.start()

    head_of = iota((1, CH), 1) // (CH // HEADS)
    heads = [(head_of == k).astype(F32) for k in range(HEADS)]

    def by_head(rows):
        return jnp.concatenate([rows * m for m in heads], axis=0)

    def join_heads(rows):
        return sum(rows[k * TILES : (k + 1) * TILES, :] * heads[k] for k in range(HEADS))

    own_qkv = sum(jnp.dot(normed, parts3[k], preferred_element_type=F32) for k in range(3))
    own_value = own_qkv[:, 2 * CH : 3 * CH]
    query_by_head, key_by_head = by_head(own_qkv[:, 0:CH]), by_head(own_qkv[:, CH : 2 * CH])
    seed = cot_v[...] * (loss_scale / math.sqrt(GY * GX * TILES))
    seed_by_head = by_head(jnp.broadcast_to(seed, (8, CH)))
    value_seed = exact_dot(seed_by_head, proj[:, 2 * CH : 3 * CH], 1, 1)
    own_value_seed = jnp.sum(by_head(own_value * seed), axis=1, keepdims=True)

    def patch_row(row, carry):
        near = halo_l[pl.ds(7 + row, 1), :]
        far = halo_r[pl.ds(7 + row, 1), :]
        there = ((row > 0) | has_up) & ((row < PAD - 1) | has_down)
        near = jnp.where(has_left & there, near, 0.0)
        far = jnp.where(has_right & there, far, 0.0)
        head = cols3[row, 0:16, 0:CH].astype(F32)
        tail = cols3[row, COLS - 16 : COLS, 2 * CH : 3 * CH].astype(F32)
        spot = iota(head.shape, 0)
        cols3[row, 0:16, 0:CH] = jnp.where(spot == 0, near, head).astype(BF16)
        cols3[row, COLS - 16 : COLS, 2 * CH : 3 * CH] = jnp.where(spot == 15, far, tail).astype(BF16)
        return carry

    lax.fori_loop(0, PAD, patch_row, 0)

    def transpose_row(row, carry):
        lanes = pl.ds(pl.multiple_of(row * COLS, COLS), COLS)
        for b in range(3):
            trans[b, :, lanes] = cols3[row, :, b * CH : (b + 1) * CH].T
        return carry

    lax.fori_loop(0, PAD, transpose_row, 0)
    for copy in tok_copies:
        copy.wait_recv()

    everyone = tok_buf[...].reshape(GX * TILES, CH)
    for copy in code_copies:
        copy.wait_recv()
    codes = code_buf[...].reshape(GX * TILES, 128)
    all_qk = sum(
        jnp.dot(everyone, parts3[k, :, 0 : 2 * CH], preferred_element_type=F32) for k in range(3)
    )
    all_query, all_key = all_qk[:, 0:CH], all_qk[:, CH : 2 * CH]
    lane0 = (iota((TILES, 128), 1) == 0).astype(F32)
    codes_across = half_dot(lane0, codes, 1, 1)
    allowed = ((codes_across == code[:, 0:1]) & (codes_across > 0.5)).astype(F32)
    allowed = jnp.concatenate([allowed] * HEADS, axis=0)
    scale = 1.0 / math.sqrt(CH // HEADS)
    as_query = jax.nn.sigmoid(close_dot(query_by_head, all_key, 1, 1) * scale + attention_bias)
    as_key = jax.nn.sigmoid(close_dot(key_by_head, all_query, 1, 1) * scale + attention_bias)
    weight_sums = jnp.sum(as_key * allowed, axis=1, keepdims=True)
    head_sums = join_heads(jnp.broadcast_to(weight_sums, (HEADS * TILES, CH)))
    partial = jnp.sum(head_sums * own_value, axis=0, keepdims=True)
    d_value = head_sums * seed
    across = sum(half_dot(part, everyone, 1, 1) for part in three_parts(value_seed))
    across = jnp.concatenate([across[8 * k : 8 * k + 8, :] for k in range(HEADS) for _ in range(2)], axis=0)
    d_as_query = across * allowed * as_query * (1.0 - as_query) * scale
    d_as_key = own_value_seed * allowed * as_key * (1.0 - as_key) * scale
    d_query = join_heads(close_dot(d_as_query, all_key))
    d_key = join_heads(close_dot(d_as_key, all_query))
    d_qkv = three_parts(jnp.concatenate([d_query, d_key, d_value], axis=1))
    d_tokens = jnp.zeros((TILES, CH), F32)
    for k in range(3):
        lhs = jnp.concatenate(d_qkv[: 3 - k], axis=0)
        product = half_dot(lhs, parts3[k], 1, 1)
        for part in range(3 - k):
            d_tokens = d_tokens + product[part * TILES : (part + 1) * TILES, :]
    token_grad = d_tokens.astype(BF16).astype(F32)

    emb_steps = [("core", 2, core)] + [(axis, 4, position[axis]) for axis in ("x", "y", "z")]

    def emb_copies(step):
        axis, count, pos = emb_steps[step]
        copies = []
        for j in range(1, count):
            device = partner if axis == "core" else device_at(**{axis: j})
            spot = emb_buf.at[step, pos]
            copies.append(
                remote(spot, spot, emb_ssem.at[step, j], emb_rsem.at[step, j], device)
            )
        return copies

    def emb_start(step, term):
        emb_buf[step, emb_steps[step][2]] = term
        for copy in emb_copies(step):
            copy.start()

    def emb_finish(step):
        for copy in emb_copies(step):
            copy.wait_recv()
        total = emb_buf[step, 0]
        for k in range(1, emb_steps[step][1]):
            total = total + emb_buf[step, k]
        return total

    emb_start(0, jnp.broadcast_to(partial, (8, CH)))

    inner = jnp.mean(token_grad * pooled, axis=-1, keepdims=True)
    pooled_grad = token_grad * inverse - pooled * (inverse * inverse * inverse * inner)
    cell_grad = (pooled_grad * (1.0 / 64.0)).astype(BF16)
    stride_back[...] = half_dot(cell_grad, stride_w[...], 1, 1)
    odd = (iota((16, CH), 0) % 2) == 1
    for tile in range(TILES):
        tr, tc = tile // 8, tile % 8
        for a in range(2):
            even_row = stride_back[tile : tile + 1, (2 * a) * CH : (2 * a + 1) * CH]
            odd_row = stride_back[tile : tile + 1, (2 * a + 1) * CH : (2 * a + 2) * CH]
            spread[tr, a, tc * 16 : tc * 16 + 16, :] = jnp.where(odd, odd_row, even_row)

    def pre_grad_row(row, carry):
        tr = row // 16
        value = (spread[tr, row % 2] * mask[tr] * slope[row]).astype(BF16)
        grad3[row + 1, :, CH : 2 * CH] = value
        wide = value.astype(F32)
        gsend_l[pl.ds(row, 1), :] = wide[0:1, :]
        gsend_r[pl.ds(row, 1), :] = wide[COLS - 1 : COLS, :]
        return carry

    lax.fori_loop(0, ROWS, pre_grad_row, 0)
    middle = pl.ds(CH, CH)
    ghalos = halo_copies(
        grad3.at[1, :, middle], grad3.at[ROWS, :, middle],
        grad3.at[0, :, middle], grad3.at[PAD - 1, :, middle],
        gsend_l, gsend_r, ghalo_l, ghalo_r, ghalo_ssem, ghalo_rsem,
    )
    start_halos(ghalos)

    def chunk_rows(k):
        first, count, _ = CHUNKS[k]
        return pl.ds(first * CH, count * CH)

    def shard_rows(k):
        first, count, _ = CHUNKS[k]
        return pl.ds(first * 16, count * 16)

    def block_rows(k, member):
        first, count, _ = CHUNKS[k]
        return pl.ds(pl.multiple_of(first * CH + member * (count * 16), 16), count * 16)

    def pair_copy(k):
        rows = chunk_rows(k)
        return remote(
            local_w.at[1 - core, rows], pair_w.at[rows], pair_ssem.at[0, k], pair_rsem.at[0, k], partner
        )

    def plane_copies(k, back):
        axes = CHUNKS[k][2]
        copies = []
        for n, (j, i) in enumerate(plane_steps()):
            if back:
                source = target = full_w.at[core, block_rows(k, member_of(axes))]
            else:
                source = half_w.at[block_rows(k, member_of(axes, j, i))]
                target = plane_w.at[n, shard_rows(k)]
            copies.append(
                remote(
                    source, target, plane_ssem.at[back, k, n], plane_rsem.at[back, k, n],
                    on_plane(axes, j, i),
                )
            )
        return copies

    def line_copies(k):
        axis = CHUNKS[k][2][2]
        pos = position[axis]
        spot = line_w.at[pos, shard_rows(k)]
        return [
            remote(
                spot, spot, line_ssem.at[k, j], line_rsem.at[k, j], device_at(**{axis: j})
            )
            for j in range(1, 4)
        ]

    def last_copy(k):
        spot = full_w.at[core, chunk_rows(k)]
        return remote(spot, spot, pair_ssem.at[1, k], pair_rsem.at[1, k], partner)

    def reduce_step(k, step):
        axes = CHUNKS[k][2]
        rows, shard = chunk_rows(k), shard_rows(k)
        if step == 0:
            pair_copy(k).start()
        elif step == 1:
            pair_copy(k).wait_recv()
            both = local_w[core, rows].astype(F32) + pair_w[rows].astype(F32)
            half_w[rows] = both.astype(BF16)
            for copy in plane_copies(k, 0):
                copy.start()
        elif step == 2:
            for copy in plane_copies(k, 0):
                copy.wait_recv()
            total = half_w[block_rows(k, member_of(axes))].astype(F32)
            for j in range(15):
                total = total + plane_w[j, shard].astype(F32)
            line_w[position[axes[2]], shard] = total.astype(BF16)
            for copy in line_copies(k):
                copy.start()
        elif step == 3:
            for copy in line_copies(k):
                copy.wait_recv()
            total = line_w[0, shard].astype(F32)
            for j in range(1, 4):
                total = total + line_w[j, shard].astype(F32)
            full_w[core, block_rows(k, member_of(axes))] = total.astype(BF16)
            for copy in plane_copies(k, 1):
                copy.start()
        elif step == 4:
            for copy in plane_copies(k, 1):
                copy.wait_recv()
            last_copy(k).start()
        else:
            last_copy(k).wait_recv()

    def tap_of(tap, carry):
        a, b = tap // 3, tap % 3
        lhs = trans[b, :, pl.ds(pl.multiple_of(a * COLS, COLS), ROWS * COLS)]
        rhs = grad3[pl.ds(1, ROWS), :, CH : 2 * CH].reshape(ROWS * COLS, CH)
        part = jnp.dot(lhs, rhs, preferred_element_type=F32)
        rows = pl.ds(pl.multiple_of(tap * CH, CH), CH)
        for c in range(2):
            local_w[c, rows, :] = part[:, c * 128 : c * 128 + 128].astype(BF16)
        return carry

    after_taps = [[(0, 0)], [(1, 0), (0, 1)], [(2, 0), (1, 1)]]
    for k, (first, count, _) in enumerate(CHUNKS):
        lax.fori_loop(first, first + count, tap_of, 0)
        for chunk, step in after_taps[k]:
            reduce_step(chunk, step)
        if k < 2:
            emb_start(k + 1, emb_finish(k))

    receive_halos(ghalos)

    def grad_shift(row, carry):
        wide = grad3[row, :, CH : 2 * CH].astype(F32)
        near = jnp.where(has_left, ghalo_l[pl.ds(7 + row, 1), :], 0.0)
        far = jnp.where(has_right, ghalo_r[pl.ds(7 + row, 1), :], 0.0)
        low, high = columns_of(wide, near, far)
        grad3[row, :, 0:CH] = high.astype(BF16)
        grad3[row, :, 2 * CH : 3 * CH] = low.astype(BF16)
        return carry

    for a in range(3):
        for b in range(3):
            taps_t[a, b * CH : (b + 1) * CH, :] = taps[a, b * CH : (b + 1) * CH, :].T
    lax.fori_loop(0, PAD // 2, grad_shift, 0)
    reduce_step(2, 1)
    lax.fori_loop(PAD // 2, PAD, grad_shift, 0)
    for row, present in ((0, has_up), (PAD - 1, has_down)):
        edge = grad3[row].astype(F32)
        grad3[row] = jnp.where(present, edge, 0.0).astype(BF16)

    def back_block(step, carry):
        first = step * CONV_ROWS
        tr = step // (16 // CONV_ROWS)
        total = conv_block(grad3, taps_t, first, True)
        for k in range(CONV_ROWS):
            out_buf[first + k] = (total[k] + spread[tr, k % 2]).astype(BF16)
        return carry

    order = [[(0, 2)], [(1, 2)], [(0, 3), (2, 2)], [(1, 3)]]
    for part in range(4):
        for chunk, step in order[part]:
            reduce_step(chunk, step)
        lax.fori_loop(2 * part, 2 * part + 2, back_block, 0)
    emb_start(3, emb_finish(2))
    for chunk, step in [(2, 3), (0, 4), (1, 4), (2, 4), (0, 5), (1, 5), (2, 5)]:
        reduce_step(chunk, step)
    emb_out[...] = emb_finish(3)[0:1, :] * (1.0 / math.sqrt(GY * GX * TILES))

    drain_halos(halos)
    drain_halos(ghalos)
    for copy in code_copies + tok_copies:
        copy.wait_send()
    for k in range(len(CHUNKS)):
        for copy in [pair_copy(k), last_copy(k)] + line_copies(k):
            copy.wait_send()
        for back in range(2):
            for copy in plane_copies(k, back):
                copy.wait_send()
    for step in range(4):
        for copy in emb_copies(step):
            copy.wait_send()


def finish(emb, grad, conv, emb_out, grad_out, conv_out, wide, sem):
    copies = [
        pltpu.make_async_copy(emb, emb_out, sem.at[0]),
        pltpu.make_async_copy(grad.at[pl.ds(0, 16)], grad_out.at[pl.ds(0, 16)], sem.at[1]),
        pltpu.make_async_copy(grad.at[pl.ds(16, 16)], grad_out.at[pl.ds(16, 16)], sem.at[2]),
    ]
    for copy in copies:
        copy.start()
    for k in range(3):
        rows = pl.ds(k * 3 * CH, 3 * CH)
        for c in range(2):
            wide[rows, c * 128 : c * 128 + 128] = conv[c, rows].astype(F32) * (1.0 / loss_scale)
        copy = pltpu.make_async_copy(wide.at[rows], conv_out.at[rows], sem.at[3 + k])
        copy.start()
        copies.append(copy)
    for copy in copies:
        copy.wait()


def per_device(features, tissue, owner_map, w_conv, w_stride, w_query, w_key, w_value, cotangent):
    whole = pl.BlockSpec(memory_space=pl.ANY)
    vector = pl.BlockSpec(memory_space=pltpu.VMEM)
    dma = pltpu.SemaphoreType.DMA
    columns = pltpu.VMEM((ROWS, CH), F32)
    column_halo = pltpu.VMEM((ROWS + 16, CH), F32)
    embedding, input_grad, conv_grad = pl.pallas_call(
        kernel,
        out_shape=(
            pltpu.VMEM((1, CH), F32),
            pltpu.VMEM((ROWS, COLS, CH), BF16),
            pltpu.VMEM((2, 9 * CH, 128), BF16),
        ),
        in_specs=[whole] * 9,
        out_specs=(vector, vector, vector),
        scratch_shapes=[
            pltpu.VMEM((PAD, COLS, CH), BF16),
            pltpu.VMEM((PAD, COLS, 3 * CH), BF16),
            pltpu.VMEM((3, CH, PAD * COLS), BF16),
            pltpu.VMEM((ROWS, COLS, CH), F32),
            pltpu.VMEM((PAD, COLS, 3 * CH), BF16),
            pltpu.VMEM((3, 3 * CH, CH), BF16),
            pltpu.VMEM((3, 3 * CH, CH), BF16),
            pltpu.VMEM((4 * CH, CH), BF16),
            pltpu.VMEM((CH, 3 * CH), F32),
            pltpu.VMEM((3, CH, 3 * CH), BF16),
            pltpu.VMEM((2, COLS, CH), F32),
            pltpu.VMEM((2, 2, COLS, CH), F32),
            pltpu.VMEM((2, 2, COLS, CH), F32),
            columns, columns, column_halo, column_halo,
            columns, columns, column_halo, column_halo,
            columns, columns,
            pltpu.VMEM((GX, TILES, CH), BF16),
            pltpu.VMEM((GX, TILES, 128), BF16),
            pltpu.VMEM((TILES, 128), F32),
            pltpu.SMEM((2, 8), jnp.int32),
            pltpu.SMEM((1, TILES), jnp.int32),
            pltpu.VMEM((1, CH), F32),
            pltpu.VMEM((TILES, 4 * CH), F32),
            pltpu.VMEM((2, 9 * CH, 128), BF16),
            pltpu.VMEM((9 * CH, 128), BF16),
            pltpu.VMEM((9 * CH, 128), BF16),
            pltpu.VMEM((15, 144, 128), BF16),
            pltpu.VMEM((4, 144, 128), BF16),
            pltpu.VMEM((4, 4, 8, CH), F32),
            dma((9,)), dma((8,)), dma((8,)), dma((8,)), dma((8,)),
            dma((2, GX)), dma((2, GX)),
            dma((2, 3, 16)), dma((2, 3, 16)), dma((3, 4)), dma((3, 4)), dma((2, 3)), dma((2, 3)),
            dma((4, 4)), dma((4, 4)),
        ],
        compiler_params=pltpu.CompilerParams(
            collective_id=0, has_side_effects=True, vmem_limit_bytes=56 * 1024 * 1024
        ),
    )(
        features, tissue, owner_map.reshape(1, TILES), w_conv.reshape(3, 3 * CH, CH),
        w_stride.reshape(4 * CH, CH), w_query, w_key, w_value, cotangent.reshape(1, CH),
    )
    embedding, input_grad, conv_grad = pl.pallas_call(
        finish,
        out_shape=(
            jax.ShapeDtypeStruct((1, CH), F32),
            jax.ShapeDtypeStruct((ROWS, COLS, CH), BF16),
            jax.ShapeDtypeStruct((9 * CH, CH), F32),
        ),
        in_specs=[vector, vector, vector],
        out_specs=(whole, whole, whole),
        scratch_shapes=[pltpu.VMEM((9 * CH, CH), F32), dma((6,))],
    )(*(pltpu.with_memory_space_constraint(x, pltpu.VMEM) for x in (embedding, input_grad, conv_grad)))
    return embedding.reshape(CH), input_grad, conv_grad.reshape(9, CH, CH)


def solution(mesh):
    in_specs = (
        P("gy", "gx", None), P("gy", "gx"), P("gy", "gx", None, None),
        P(), P(), P(), P(), P(), P(),
    )
    out_specs = (P(), P("gy", "gx", None), P())
    return jax.shard_map(
        per_device, mesh=mesh, in_specs=in_specs, out_specs=out_specs, check_vma=False
    )
```

```python
import math

import jax
import jax.numpy as jnp
from jax import lax
from jax.experimental import pallas as pl
from jax.experimental.pallas import tpu as pltpu
from jax.sharding import PartitionSpec as P

MESH = pl.DeviceIdType.MESH
F32, BF16 = jnp.float32, jnp.bfloat16
HEADS = 4
attention_bias = -1.0
loss_scale = 512.0

GY, GX = 8, 16
ROWS, COLS, CH = 32, 128, 256
PAD = ROWS + 2
TILES = 16
CONV_ROWS = 4
CHUNKS = ((0, 3, "zxy"), (3, 3, "zxy"), (6, 3, "zxy"))
BARRIER_SIGNALS = 23 + 24


def exact_dot(a, b, a_dim=1, b_dim=0):
    return lax.dot_general(
        a, b, (((a_dim,), (b_dim,)), ((), ())),
        precision=lax.Precision.HIGHEST, preferred_element_type=F32,
    )


def close_dot(a, b, a_dim=1, b_dim=0):
    (a_high, a_low, _), (b_high, b_low, _) = three_parts(a), three_parts(b)
    rows = a.shape[0]
    both = half_dot(jnp.concatenate([a_high, a_low], axis=0), b_high, a_dim, b_dim)
    return both[:rows] + both[rows:] + half_dot(a_high, b_low, a_dim, b_dim)


def half_dot(a, b, a_dim=1, b_dim=0):
    return lax.dot_general(
        a.astype(BF16), b.astype(BF16), (((a_dim,), (b_dim,)), ((), ())),
        preferred_element_type=F32,
    )


def three_parts(value):
    high = value.astype(BF16)
    rest = value - high.astype(F32)
    middle = rest.astype(BF16)
    low = (rest - middle.astype(F32)).astype(BF16)
    return high, middle, low


def iota(shape, dim):
    return lax.broadcasted_iota(jnp.int32, shape, dim)


def kernel(
    feat, tissue, owner, w_conv, w_stride, w_query, w_key, w_value, cot,
    emb_out, out_buf, full_w,
    field, cols3, trans, slope, grad3, taps, taps_t, stride_w, proj, parts3, mask,
    sums, spread, send_l, send_r, halo_l, halo_r, gsend_l, gsend_r, ghalo_l, ghalo_r,
    edge_l, edge_r, tok_buf, code_buf, code_rows, tissue_s, owner_s, cot_v, stride_back,
    local_w, pair_w, half_w, plane_w, line_w, emb_buf,
    load_sem, halo_ssem, halo_rsem, ghalo_ssem, ghalo_rsem, tok_ssem, tok_rsem,
    plane_ssem, plane_rsem, line_ssem, line_rsem, pair_ssem, pair_rsem, emb_ssem, emb_rsem,
):
    g, h = lax.axis_index("gy"), lax.axis_index("gx")
    x_hi, y = lax.div(g, 4), lax.rem(g, 4)
    z, x_lo, core = lax.div(h, 4), lax.rem(lax.div(h, 2), 2), lax.rem(h, 2)
    position = {"x": 2 * x_hi + x_lo, "y": y, "z": z}
    partner = (g, h + 1 - 2 * core)

    around = {axis: [lax.rem(position[axis] + j, 4) for j in range(4)] for axis in "xyz"}
    share_g = {
        "x": [lax.div(pos, 2) * 4 for pos in around["x"]],
        "y": around["y"],
        "z": [0] * 4,
    }
    share_h = {
        "x": [lax.rem(pos, 2) * 2 for pos in around["x"]],
        "y": [0] * 4,
        "z": [pos * 4 for pos in around["z"]],
    }

    def device_at(**steps):
        steps = {axis: steps.get(axis, 0) for axis in "xyz"}
        return (
            sum(share_g[axis][steps[axis]] for axis in "xy"),
            sum(share_h[axis][steps[axis]] for axis in "xz") + core,
        )

    def plane_steps():
        return [(j, k) for j in range(4) for k in range(4) if (j, k) != (0, 0)]

    def on_plane(axes, j, k):
        return device_at(**{axes[0]: j, axes[1]: k})

    def member_of(axes, j=0, k=0):
        return around[axes[0]][j] * 4 + around[axes[1]][k]

    row_peers = [lax.rem(h + j, GX) for j in range(GX)]

    up, down = lax.rem(g + GY - 1, GY), lax.rem(g + 1, GY)
    left, right = row_peers[GX - 1], row_peers[1]

    def remote(src, dst, ssem, rsem, device):
        return pltpu.make_async_remote_copy(
            src_ref=src, dst_ref=dst, send_sem=ssem, recv_sem=rsem,
            device_id=device, device_id_type=MESH,
        )

    loads = [
        pltpu.make_async_copy(feat, field.at[pl.ds(1, ROWS)], load_sem.at[0]),
        pltpu.make_async_copy(w_conv, taps, load_sem.at[1]),
        pltpu.make_async_copy(w_stride, stride_w, load_sem.at[2]),
        pltpu.make_async_copy(w_query, proj.at[:, pl.ds(0, CH)], load_sem.at[3]),
        pltpu.make_async_copy(w_key, proj.at[:, pl.ds(CH, CH)], load_sem.at[4]),
        pltpu.make_async_copy(w_value, proj.at[:, pl.ds(2 * CH, CH)], load_sem.at[5]),
    ]
    small = [
        pltpu.make_async_copy(tissue, tissue_s, load_sem.at[6]),
        pltpu.make_async_copy(owner, owner_s, load_sem.at[7]),
        pltpu.make_async_copy(cot, cot_v, load_sem.at[8]),
    ]
    loads[0].start()
    barrier = pltpu.get_barrier_semaphore()
    peers = [
        (up, h), (down, h), (g, left), (g, right),
        (up, left), (up, right), (down, left), (down, right),
    ]
    peers += [(g, peer) for peer in row_peers[1:]]
    peers += [
        device_at(x=i, y=j, z=k)
        for i in range(4) for j in range(4) for k in range(4)
        if 0 in (j, k) and (i, j) != (0, 0)
    ]
    for device in peers:
        pl.semaphore_signal(barrier, inc=1, device_id=device, device_id_type=MESH)

    for copy in loads[1:] + small:
        copy.start()
    for copy in small:
        copy.wait()
    for tile in range(TILES):
        tr, tc = tile // 8, tile % 8
        flag = tissue_s[tr, tc].astype(F32)
        code = flag * (owner_s[0, tile].astype(F32) + 1.0)
        mask[tr, tc * 16 : tc * 16 + 16, :] = jnp.zeros((16, CH), F32) + flag
        code_rows[tile : tile + 1, :] = jnp.zeros((1, 128), F32) + code
    code_buf[h] = code_rows[...].astype(BF16)
    sums[...] = jnp.zeros_like(sums)
    loads[0].wait()

    def edge_columns(row, carry):
        send_l[pl.ds(row, 1), :] = field[row + 1, 0:16, :].astype(F32)[0:1, :]
        send_r[pl.ds(row, 1), :] = field[row + 1, COLS - 16 : COLS, :].astype(F32)[15:16, :]
        return carry

    lax.fori_loop(0, ROWS, edge_columns, 0)
    def halo_copies(first_row, last_row, low_row, high_row, col_l, col_r, got_l, got_r, ss, rs):
        top, bottom = pl.ds(0, 8), pl.ds(ROWS - 8, 8)
        return [
            remote(first_row, high_row, ss.at[0], rs.at[0], (up, h)),
            remote(last_row, low_row, ss.at[1], rs.at[1], (down, h)),
            remote(col_l, got_r.at[pl.ds(8, ROWS)], ss.at[2], rs.at[2], (g, left)),
            remote(col_r, got_l.at[pl.ds(8, ROWS)], ss.at[3], rs.at[3], (g, right)),
            remote(col_r.at[bottom], got_l.at[pl.ds(0, 8)], ss.at[4], rs.at[4], (down, right)),
            remote(col_r.at[top], got_l.at[pl.ds(40, 8)], ss.at[5], rs.at[5], (up, right)),
            remote(col_l.at[bottom], got_r.at[pl.ds(0, 8)], ss.at[6], rs.at[6], (down, left)),
            remote(col_l.at[top], got_r.at[pl.ds(40, 8)], ss.at[7], rs.at[7], (up, left)),
        ]

    has_left, has_right = h > 0, h < GX - 1
    has_up, has_down = g > 0, g < GY - 1
    to_send = (
        has_up, has_down, has_left, has_right,
        has_down & has_right, has_up & has_right, has_down & has_left, has_up & has_left,
    )
    to_receive = (
        has_down, has_up, has_right, has_left,
        has_up & has_left, has_down & has_left, has_up & has_right, has_down & has_right,
    )

    def start_halos(copies):
        for copy, there in zip(copies, to_send):
            pl.when(there)(copy.start)

    def receive_halos(copies, first=0, last=8):
        for copy, there in list(zip(copies, to_receive))[first:last]:
            pl.when(there)(copy.wait_recv)

    def drain_halos(copies):
        for copy, there in zip(copies, to_send):
            pl.when(there)(copy.wait_send)


    def columns_of(center, before, after):
        spot = iota(center.shape, 0)
        low = jnp.where(spot == 0, before, pltpu.roll(center, 1, 0))
        high = jnp.where(spot == COLS - 1, after, pltpu.roll(center, COLS - 1, 0))
        return low, high

    def shift_row(row, carry):
        center = field[row]
        low, high = columns_of(center.astype(F32), 0.0, 0.0)
        cols3[row, :, 0:CH] = low.astype(BF16)
        cols3[row, :, CH : 2 * CH] = center
        cols3[row, :, 2 * CH : 3 * CH] = high.astype(BF16)
        return carry

    lax.fori_loop(1, ROWS + 1, shift_row, 0)
    loads[1].wait()

    def conv_block(source, weights, first, flipped):
        total = None
        for a in range(3):
            start = first + (2 - a if flipped else a)
            block = source[pl.ds(start, CONV_ROWS)].reshape(CONV_ROWS * COLS, 3 * CH)
            part = jnp.dot(block, weights[a], preferred_element_type=F32)
            total = part if total is None else total + part
        return total.reshape(CONV_ROWS, COLS, CH)

    def forward_block(step, carry):
        first = step * CONV_ROWS
        tr = step // (16 // CONV_ROWS)
        pre = conv_block(cols3, taps, first, False)
        for k in range(CONV_ROWS):
            edge_l[pl.ds(first + k, 1), :] = pre[k, 0:1, :]
            edge_r[pl.ds(first + k, 1), :] = pre[k, COLS - 1 : COLS, :]
        gate = jax.nn.sigmoid(pre)
        slope[pl.ds(first, CONV_ROWS)] = gate * (1.0 + pre * (1.0 - gate))
        own = cols3[pl.ds(first + 1, CONV_ROWS), :, CH : 2 * CH].astype(F32)
        summed = (own + pre * gate * mask[tr][None]).astype(BF16).astype(F32)
        for a in range(2):
            total = sums[tr, a]
            for k in range(a, CONV_ROWS, 2):
                total = total + summed[k]
            sums[tr, a] = total
        return carry

    lax.fori_loop(1, 5, forward_block, 0)
    pl.semaphore_wait(barrier, BARRIER_SIGNALS)
    code_copies = [
        remote(
            code_buf.at[h], code_buf.at[h], tok_ssem.at[0, j], tok_rsem.at[0, j], (g, row_peers[j])
        )
        for j in range(1, GX)
    ]
    halos = halo_copies(
        field.at[1], field.at[ROWS], field.at[0], field.at[PAD - 1],
        send_l, send_r, halo_l, halo_r, halo_ssem, halo_rsem,
    )
    start_halos(halos)
    lax.fori_loop(5, 7, forward_block, 0)

    for k in range(3, 6):
        loads[k].wait()
    for k, part in enumerate(three_parts(proj[...])):
        parts3[k] = part
    receive_halos(halos, 0, 2)
    for row, present in ((0, has_up), (PAD - 1, has_down)):
        wide = jnp.where(present, field[row].astype(F32), 0.0)
        low, high = columns_of(wide, 0.0, 0.0)
        cols3[row, :, 0:CH] = low.astype(BF16)
        cols3[row, :, CH : 2 * CH] = wide.astype(BF16)
        cols3[row, :, 2 * CH : 3 * CH] = high.astype(BF16)

    for copy in code_copies:
        copy.start()

    lax.fori_loop(0, 2, lambda i, carry: forward_block(i * 7, carry), 0)
    receive_halos(halos, 2)
    row_of = iota((ROWS, CH), 0)
    inside = ((row_of > 0) | has_up, None, (row_of < ROWS - 1) | has_down)

    def fix_edge(got, present, edge, own, tap_at, col):
        terms = []
        for a in range(3):
            there = present if inside[a] is None else inside[a] & present
            terms.append(jnp.where(there, got[7 + a : 7 + a + ROWS, :], 0.0).astype(BF16))
        pre = edge[...]
        flag = jnp.where(row_of < 16, mask[0, col : col + 1, :], mask[1, col : col + 1, :])
        old = (own[...] + pre * jax.nn.sigmoid(pre) * flag).astype(BF16).astype(F32)
        for a in range(3):
            pre = pre + jnp.dot(
                terms[a], taps[a, tap_at * CH : (tap_at + 1) * CH, :], preferred_element_type=F32
            )
        gate = jax.nn.sigmoid(pre)
        new = (own[...] + pre * gate * flag).astype(BF16).astype(F32)
        slant = gate * (1.0 + pre * (1.0 - gate))
        change = new - old
        for tr in range(2):
            for a in range(2):
                part = jnp.where((row_of // 16 == tr) & (row_of % 2 == a), change, 0.0)
                sums[tr, a, col : col + 1, :] = sums[tr, a, col : col + 1, :] + jnp.sum(
                    part, axis=0, keepdims=True
                )
        for row in range(ROWS):
            slope[row, col : col + 1, :] = slant[row : row + 1, :]

    fix_edge(halo_l, has_left, edge_l, send_l, 0, 0)
    fix_edge(halo_r, has_right, edge_r, send_r, 2, COLS - 1)


    lane_col, row_id = iota((16, COLS), 1), iota((16, COLS), 0)
    select = ((lane_col // 16 == row_id % 8) & (lane_col % 2 == row_id // 8)).astype(BF16)
    gathered = jnp.concatenate([sums[tr, a] for tr in range(2) for a in range(2)], axis=1)
    parts = three_parts(gathered)
    cell_sums = sum(jnp.dot(select, part, preferred_element_type=F32) for part in parts)
    loads[2].wait()
    pooled = jnp.zeros((TILES, CH), F32)
    for a in range(2):
        for b in range(2):
            tap = 2 * a + b
            lhs = jnp.concatenate(
                [cell_sums[b * 8 : b * 8 + 8, (2 * tr + a) * CH : (2 * tr + a + 1) * CH] for tr in range(2)],
                axis=0,
            )
            rhs = stride_w[tap * CH : (tap + 1) * CH, :]
            pooled = pooled + sum(
                jnp.dot(part, rhs, preferred_element_type=F32) for part in three_parts(lhs)
            )
    pooled = pooled * (1.0 / 64.0)
    inverse = lax.rsqrt(jnp.mean(pooled * pooled, axis=-1, keepdims=True) + 1e-05)
    normed = (pooled * inverse).astype(BF16)

    code = code_rows[...]
    tok_buf[h] = normed
    tok_copies = [
        remote(
            tok_buf.at[h], tok_buf.at[h], tok_ssem.at[1, j], tok_rsem.at[1, j], (g, row_peers[j])
        )
        for j in sorted(range(1, GX), key=lambda j: abs(j - GX // 2))
    ]
    for copy in tok_copies:
        copy.start()

    head_of = iota((1, CH), 1) // (CH // HEADS)
    heads = [(head_of == k).astype(F32) for k in range(HEADS)]

    def by_head(rows):
        return jnp.concatenate([rows * m for m in heads], axis=0)

    def join_heads(rows):
        return sum(rows[k * TILES : (k + 1) * TILES, :] * heads[k] for k in range(HEADS))

    own_qkv = sum(jnp.dot(normed, parts3[k], preferred_element_type=F32) for k in range(3))
    own_value = own_qkv[:, 2 * CH : 3 * CH]
    query_by_head, key_by_head = by_head(own_qkv[:, 0:CH]), by_head(own_qkv[:, CH : 2 * CH])
    seed = cot_v[...] * (loss_scale / math.sqrt(GY * GX * TILES))
    seed_by_head = by_head(jnp.broadcast_to(seed, (8, CH)))
    value_seed = exact_dot(seed_by_head, proj[:, 2 * CH : 3 * CH], 1, 1)
    own_value_seed = jnp.sum(by_head(own_value * seed), axis=1, keepdims=True)

    def patch_row(row, carry):
        near = halo_l[pl.ds(7 + row, 1), :]
        far = halo_r[pl.ds(7 + row, 1), :]
        there = ((row > 0) | has_up) & ((row < PAD - 1) | has_down)
        near = jnp.where(has_left & there, near, 0.0)
        far = jnp.where(has_right & there, far, 0.0)
        head = cols3[row, 0:16, 0:CH].astype(F32)
        tail = cols3[row, COLS - 16 : COLS, 2 * CH : 3 * CH].astype(F32)
        spot = iota(head.shape, 0)
        cols3[row, 0:16, 0:CH] = jnp.where(spot == 0, near, head).astype(BF16)
        cols3[row, COLS - 16 : COLS, 2 * CH : 3 * CH] = jnp.where(spot == 15, far, tail).astype(BF16)
        return carry

    lax.fori_loop(0, PAD, patch_row, 0)

    def transpose_row(row, carry):
        lanes = pl.ds(pl.multiple_of(row * COLS, COLS), COLS)
        for b in range(3):
            trans[b, :, lanes] = cols3[row, :, b * CH : (b + 1) * CH].T
        return carry

    lax.fori_loop(0, PAD, transpose_row, 0)
    for copy in tok_copies:
        copy.wait_recv()

    everyone = tok_buf[...].reshape(GX * TILES, CH)
    for copy in code_copies:
        copy.wait_recv()
    codes = code_buf[...].reshape(GX * TILES, 128)
    all_qk = sum(
        jnp.dot(everyone, parts3[k, :, 0 : 2 * CH], preferred_element_type=F32) for k in range(3)
    )
    all_query, all_key = all_qk[:, 0:CH], all_qk[:, CH : 2 * CH]
    lane0 = (iota((TILES, 128), 1) == 0).astype(F32)
    codes_across = half_dot(lane0, codes, 1, 1)
    allowed = ((codes_across == code[:, 0:1]) & (codes_across > 0.5)).astype(F32)
    allowed = jnp.concatenate([allowed] * HEADS, axis=0)
    scale = 1.0 / math.sqrt(CH // HEADS)
    as_query = jax.nn.sigmoid(close_dot(query_by_head, all_key, 1, 1) * scale + attention_bias)
    as_key = jax.nn.sigmoid(close_dot(key_by_head, all_query, 1, 1) * scale + attention_bias)
    weight_sums = jnp.sum(as_key * allowed, axis=1, keepdims=True)
    head_sums = join_heads(jnp.broadcast_to(weight_sums, (HEADS * TILES, CH)))
    partial = jnp.sum(head_sums * own_value, axis=0, keepdims=True)
    d_value = head_sums * seed
    across = sum(half_dot(part, everyone, 1, 1) for part in three_parts(value_seed))
    across = jnp.concatenate([across[8 * k : 8 * k + 8, :] for k in range(HEADS) for _ in range(2)], axis=0)
    d_as_query = across * allowed * as_query * (1.0 - as_query) * scale
    d_as_key = own_value_seed * allowed * as_key * (1.0 - as_key) * scale
    d_query = join_heads(close_dot(d_as_query, all_key))
    d_key = join_heads(close_dot(d_as_key, all_query))
    d_qkv = three_parts(jnp.concatenate([d_query, d_key, d_value], axis=1))
    d_tokens = jnp.zeros((TILES, CH), F32)
    for k in range(3):
        lhs = jnp.concatenate(d_qkv[: 3 - k], axis=0)
        product = half_dot(lhs, parts3[k], 1, 1)
        for part in range(3 - k):
            d_tokens = d_tokens + product[part * TILES : (part + 1) * TILES, :]
    token_grad = d_tokens.astype(BF16).astype(F32)

    emb_steps = [("core", 2, core)] + [(axis, 4, position[axis]) for axis in ("x", "y", "z")]

    def emb_copies(step):
        axis, count, pos = emb_steps[step]
        copies = []
        for j in range(1, count):
            device = partner if axis == "core" else device_at(**{axis: j})
            spot = emb_buf.at[step, pos]
            copies.append(
                remote(spot, spot, emb_ssem.at[step, j], emb_rsem.at[step, j], device)
            )
        return copies

    def emb_start(step, term):
        emb_buf[step, emb_steps[step][2]] = term
        for copy in emb_copies(step):
            copy.start()

    def emb_finish(step):
        for copy in emb_copies(step):
            copy.wait_recv()
        total = emb_buf[step, 0]
        for k in range(1, emb_steps[step][1]):
            total = total + emb_buf[step, k]
        return total

    emb_start(0, jnp.broadcast_to(partial, (8, CH)))

    inner = jnp.mean(token_grad * pooled, axis=-1, keepdims=True)
    pooled_grad = token_grad * inverse - pooled * (inverse * inverse * inverse * inner)
    cell_grad = (pooled_grad * (1.0 / 64.0)).astype(BF16)
    stride_back[...] = half_dot(cell_grad, stride_w[...], 1, 1)
    odd = (iota((16, CH), 0) % 2) == 1
    for tile in range(TILES):
        tr, tc = tile // 8, tile % 8
        for a in range(2):
            even_row = stride_back[tile : tile + 1, (2 * a) * CH : (2 * a + 1) * CH]
            odd_row = stride_back[tile : tile + 1, (2 * a + 1) * CH : (2 * a + 2) * CH]
            spread[tr, a, tc * 16 : tc * 16 + 16, :] = jnp.where(odd, odd_row, even_row)

    def pre_grad_row(row, carry):
        tr = row // 16
        value = (spread[tr, row % 2] * mask[tr] * slope[row]).astype(BF16)
        grad3[row + 1, :, CH : 2 * CH] = value
        wide = value.astype(F32)
        gsend_l[pl.ds(row, 1), :] = wide[0:1, :]
        gsend_r[pl.ds(row, 1), :] = wide[COLS - 1 : COLS, :]
        return carry

    lax.fori_loop(0, ROWS, pre_grad_row, 0)
    middle = pl.ds(CH, CH)
    ghalos = halo_copies(
        grad3.at[1, :, middle], grad3.at[ROWS, :, middle],
        grad3.at[0, :, middle], grad3.at[PAD - 1, :, middle],
        gsend_l, gsend_r, ghalo_l, ghalo_r, ghalo_ssem, ghalo_rsem,
    )
    start_halos(ghalos)

    def chunk_rows(k):
        first, count, _ = CHUNKS[k]
        return pl.ds(first * CH, count * CH)

    def shard_rows(k):
        first, count, _ = CHUNKS[k]
        return pl.ds(first * 16, count * 16)

    def block_rows(k, member):
        first, count, _ = CHUNKS[k]
        return pl.ds(pl.multiple_of(first * CH + member * (count * 16), 16), count * 16)

    def pair_copy(k):
        rows = chunk_rows(k)
        return remote(
            local_w.at[1 - core, rows], pair_w.at[rows], pair_ssem.at[0, k], pair_rsem.at[0, k], partner
        )

    def plane_copies(k, back):
        axes = CHUNKS[k][2]
        copies = []
        for n, (j, i) in enumerate(plane_steps()):
            if back:
                source = target = full_w.at[core, block_rows(k, member_of(axes))]
            else:
                source = half_w.at[block_rows(k, member_of(axes, j, i))]
                target = plane_w.at[n, shard_rows(k)]
            copies.append(
                remote(
                    source, target, plane_ssem.at[back, k, n], plane_rsem.at[back, k, n],
                    on_plane(axes, j, i),
                )
            )
        return copies

    def line_copies(k):
        axis = CHUNKS[k][2][2]
        pos = position[axis]
        spot = line_w.at[pos, shard_rows(k)]
        return [
            remote(
                spot, spot, line_ssem.at[k, j], line_rsem.at[k, j], device_at(**{axis: j})
            )
            for j in range(1, 4)
        ]

    def last_copy(k):
        spot = full_w.at[core, chunk_rows(k)]
        return remote(spot, spot, pair_ssem.at[1, k], pair_rsem.at[1, k], partner)

    def reduce_step(k, step):
        axes = CHUNKS[k][2]
        rows, shard = chunk_rows(k), shard_rows(k)
        if step == 0:
            pair_copy(k).start()
        elif step == 1:
            pair_copy(k).wait_recv()
            both = local_w[core, rows].astype(F32) + pair_w[rows].astype(F32)
            half_w[rows] = both.astype(BF16)
            for copy in plane_copies(k, 0):
                copy.start()
        elif step == 2:
            for copy in plane_copies(k, 0):
                copy.wait_recv()
            total = half_w[block_rows(k, member_of(axes))].astype(F32)
            for j in range(15):
                total = total + plane_w[j, shard].astype(F32)
            line_w[position[axes[2]], shard] = total.astype(BF16)
            for copy in line_copies(k):
                copy.start()
        elif step == 3:
            for copy in line_copies(k):
                copy.wait_recv()
            total = line_w[0, shard].astype(F32)
            for j in range(1, 4):
                total = total + line_w[j, shard].astype(F32)
            full_w[core, block_rows(k, member_of(axes))] = total.astype(BF16)
            for copy in plane_copies(k, 1):
                copy.start()
        elif step == 4:
            for copy in plane_copies(k, 1):
                copy.wait_recv()
            last_copy(k).start()
        else:
            last_copy(k).wait_recv()

    def tap_of(tap, carry):
        a, b = tap // 3, tap % 3
        lhs = trans[b, :, pl.ds(pl.multiple_of(a * COLS, COLS), ROWS * COLS)]
        rhs = grad3[pl.ds(1, ROWS), :, CH : 2 * CH].reshape(ROWS * COLS, CH)
        part = jnp.dot(lhs, rhs, preferred_element_type=F32)
        rows = pl.ds(pl.multiple_of(tap * CH, CH), CH)
        for c in range(2):
            local_w[c, rows, :] = part[:, c * 128 : c * 128 + 128].astype(BF16)
        return carry

    after_taps = [[(0, 0)], [(1, 0), (0, 1)], [(2, 0), (1, 1)]]
    for k, (first, count, _) in enumerate(CHUNKS):
        lax.fori_loop(first, first + count, tap_of, 0)
        for chunk, step in after_taps[k]:
            reduce_step(chunk, step)
        if k < 2:
            emb_start(k + 1, emb_finish(k))

    receive_halos(ghalos)

    def grad_shift(row, carry):
        wide = grad3[row, :, CH : 2 * CH].astype(F32)
        near = jnp.where(has_left, ghalo_l[pl.ds(7 + row, 1), :], 0.0)
        far = jnp.where(has_right, ghalo_r[pl.ds(7 + row, 1), :], 0.0)
        low, high = columns_of(wide, near, far)
        grad3[row, :, 0:CH] = high.astype(BF16)
        grad3[row, :, 2 * CH : 3 * CH] = low.astype(BF16)
        return carry

    for a in range(3):
        for b in range(3):
            taps_t[a, b * CH : (b + 1) * CH, :] = taps[a, b * CH : (b + 1) * CH, :].T
    lax.fori_loop(0, PAD // 2, grad_shift, 0)
    reduce_step(2, 1)
    lax.fori_loop(PAD // 2, PAD, grad_shift, 0)
    for row, present in ((0, has_up), (PAD - 1, has_down)):
        edge = grad3[row].astype(F32)
        grad3[row] = jnp.where(present, edge, 0.0).astype(BF16)

    def back_block(step, carry):
        first = step * CONV_ROWS
        tr = step // (16 // CONV_ROWS)
        total = conv_block(grad3, taps_t, first, True)
        for k in range(CONV_ROWS):
            out_buf[first + k] = (total[k] + spread[tr, k % 2]).astype(BF16)
        return carry

    order = [[(0, 2)], [(1, 2)], [(0, 3), (2, 2)], [(1, 3)]]
    for part in range(4):
        for chunk, step in order[part]:
            reduce_step(chunk, step)
        lax.fori_loop(2 * part, 2 * part + 2, back_block, 0)
    emb_start(3, emb_finish(2))
    for chunk, step in [(2, 3), (0, 4), (1, 4), (2, 4), (0, 5), (1, 5), (2, 5)]:
        reduce_step(chunk, step)
    emb_out[...] = emb_finish(3)[0:1, :] * (1.0 / math.sqrt(GY * GX * TILES))

    drain_halos(halos)
    drain_halos(ghalos)
    for copy in code_copies + tok_copies:
        copy.wait_send()
    for k in range(len(CHUNKS)):
        for copy in [pair_copy(k), last_copy(k)] + line_copies(k):
            copy.wait_send()
        for back in range(2):
            for copy in plane_copies(k, back):
                copy.wait_send()
    for step in range(4):
        for copy in emb_copies(step):
            copy.wait_send()


def finish(emb, grad, conv, emb_out, grad_out, conv_out, wide, sem):
    copies = [
        pltpu.make_async_copy(emb, emb_out, sem.at[0]),
        pltpu.make_async_copy(grad.at[pl.ds(0, 16)], grad_out.at[pl.ds(0, 16)], sem.at[1]),
        pltpu.make_async_copy(grad.at[pl.ds(16, 16)], grad_out.at[pl.ds(16, 16)], sem.at[2]),
    ]
    for copy in copies:
        copy.start()
    for k in range(3):
        rows = pl.ds(k * 3 * CH, 3 * CH)
        for c in range(2):
            wide[rows, c * 128 : c * 128 + 128] = conv[c, rows].astype(F32) * (1.0 / loss_scale)
        copy = pltpu.make_async_copy(wide.at[rows], conv_out.at[rows], sem.at[3 + k])
        copy.start()
        copies.append(copy)
    for copy in copies:
        copy.wait()


def per_device(features, tissue, owner_map, w_conv, w_stride, w_query, w_key, w_value, cotangent):
    whole = pl.BlockSpec(memory_space=pl.ANY)
    vector = pl.BlockSpec(memory_space=pltpu.VMEM)
    dma = pltpu.SemaphoreType.DMA
    columns = pltpu.VMEM((ROWS, CH), F32)
    column_halo = pltpu.VMEM((ROWS + 16, CH), F32)
    embedding, input_grad, conv_grad = pl.pallas_call(
        kernel,
        out_shape=(
            pltpu.VMEM((1, CH), F32),
            pltpu.VMEM((ROWS, COLS, CH), BF16),
            pltpu.VMEM((2, 9 * CH, 128), BF16),
        ),
        in_specs=[whole] * 9,
        out_specs=(vector, vector, vector),
        scratch_shapes=[
            pltpu.VMEM((PAD, COLS, CH), BF16),
            pltpu.VMEM((PAD, COLS, 3 * CH), BF16),
            pltpu.VMEM((3, CH, PAD * COLS), BF16),
            pltpu.VMEM((ROWS, COLS, CH), F32),
            pltpu.VMEM((PAD, COLS, 3 * CH), BF16),
            pltpu.VMEM((3, 3 * CH, CH), BF16),
            pltpu.VMEM((3, 3 * CH, CH), BF16),
            pltpu.VMEM((4 * CH, CH), BF16),
            pltpu.VMEM((CH, 3 * CH), F32),
            pltpu.VMEM((3, CH, 3 * CH), BF16),
            pltpu.VMEM((2, COLS, CH), F32),
            pltpu.VMEM((2, 2, COLS, CH), F32),
            pltpu.VMEM((2, 2, COLS, CH), F32),
            columns, columns, column_halo, column_halo,
            columns, columns, column_halo, column_halo,
            columns, columns,
            pltpu.VMEM((GX, TILES, CH), BF16),
            pltpu.VMEM((GX, TILES, 128), BF16),
            pltpu.VMEM((TILES, 128), F32),
            pltpu.SMEM((2, 8), jnp.int32),
            pltpu.SMEM((1, TILES), jnp.int32),
            pltpu.VMEM((1, CH), F32),
            pltpu.VMEM((TILES, 4 * CH), F32),
            pltpu.VMEM((2, 9 * CH, 128), BF16),
            pltpu.VMEM((9 * CH, 128), BF16),
            pltpu.VMEM((9 * CH, 128), BF16),
            pltpu.VMEM((15, 144, 128), BF16),
            pltpu.VMEM((4, 144, 128), BF16),
            pltpu.VMEM((4, 4, 8, CH), F32),
            dma((9,)), dma((8,)), dma((8,)), dma((8,)), dma((8,)),
            dma((2, GX)), dma((2, GX)),
            dma((2, 3, 16)), dma((2, 3, 16)), dma((3, 4)), dma((3, 4)), dma((2, 3)), dma((2, 3)),
            dma((4, 4)), dma((4, 4)),
        ],
        compiler_params=pltpu.CompilerParams(
            collective_id=0, has_side_effects=True, vmem_limit_bytes=56 * 1024 * 1024
        ),
    )(
        features, tissue, owner_map.reshape(1, TILES), w_conv.reshape(3, 3 * CH, CH),
        w_stride.reshape(4 * CH, CH), w_query, w_key, w_value, cotangent.reshape(1, CH),
    )
    embedding, input_grad, conv_grad = pl.pallas_call(
        finish,
        out_shape=(
            jax.ShapeDtypeStruct((1, CH), F32),
            jax.ShapeDtypeStruct((ROWS, COLS, CH), BF16),
            jax.ShapeDtypeStruct((9 * CH, CH), F32),
        ),
        in_specs=[vector, vector, vector],
        out_specs=(whole, whole, whole),
        scratch_shapes=[pltpu.VMEM((9 * CH, CH), F32), dma((6,))],
    )(*(pltpu.with_memory_space_constraint(x, pltpu.VMEM) for x in (embedding, input_grad, conv_grad)))
    return embedding.reshape(CH), input_grad, conv_grad.reshape(9, CH, CH)


def solution(mesh):
    in_specs = (
        P("gy", "gx", None), P("gy", "gx"), P("gy", "gx", None, None),
        P(), P(), P(), P(), P(), P(),
    )
    out_specs = (P(), P("gy", "gx", None), P())
    return jax.shard_map(
        per_device, mesh=mesh, in_specs=in_specs, out_specs=out_specs, check_vma=False
    )
```
